32 devices in a mesh: grp: 2 (over x), dp: 4 (over z), tp: 4 (over y, core).
Axes of the slice: x: 2, y: 2, z: 4, core: 2. Of those that a mesh axis runs over, the one named last changes fastest.
Arguments:
- image_rows: bfloat16 [8192, 1024], P(('grp', 'dp', 'tp')), may hold values from -6 to 6
- text_states: bfloat16 [8, 128, 1024], P(('grp', 'dp')), may hold values from -6 to 6
- caption_lengths: int32 [8], P(('grp', 'dp')), may hold values from 1 to 128, as said below
- out_grad: bfloat16 [8192, 1024], P(('grp', 'dp')), may hold values from -6 to 6
- self_query: bfloat16 [1024, 1024], P(None, 'tp'), may hold values from -0.1875 to 0.1875
- self_key: bfloat16 [1024, 1024], P(None, 'tp'), may hold values from -0.1875 to 0.1875
- self_value: bfloat16 [1024, 1024], P(None, 'tp'), may hold values from -0.1875 to 0.1875
- self_output: bfloat16 [1024, 1024], P('tp'), may hold values from -1 to 1
- cross_query: bfloat16 [1024, 1024], P(None, 'tp'), may hold values from -0.1875 to 0.1875
- cross_key: bfloat16 [1024, 1024], P(None, 'tp'), may hold values from -0.1875 to 0.1875
- cross_value: bfloat16 [1024, 1024], P(None, 'tp'), may hold values from -0.1875 to 0.1875
- cross_output: bfloat16 [1024, 1024], P('tp'), may hold values from -0.375 to 0.375
- mlp_up: bfloat16 [1024, 4096], P(None, 'tp'), may hold values from -0.1875 to 0.1875
- mlp_down: bfloat16 [4096, 1024], P('tp'), may hold values from -0.09375 to 0.09375
- attn_gain: float32 [1024], replicated, may hold values from 0.5 to 1.5
- attn_shift: float32 [1024], replicated, may hold values from -1.75 to 1.75
- cross_gain: float32 [1024], replicated, may hold values from 0.5 to 1.5
- cross_shift: float32 [1024], replicated, may hold values from -1.75 to 1.75
- mlp_gain: float32 [1024], replicated, may hold values from 0.5 to 1.5
- mlp_shift: float32 [1024], replicated, may hold values from -1.75 to 1.75
Outputs:
- layer_out: bfloat16 [8192, 1024], P(('grp', 'dp', 'tp'))
- image_grad: float32 [8192, 1024], P(('grp', 'dp', 'tp'))
- text_grad: float32 [8, 128, 1024], P(('grp', 'dp'))
- self_query_grad: float32 [1024, 1024], P('dp', 'tp')
- self_key_grad: float32 [1024, 1024], P('dp', 'tp')
- self_value_grad: float32 [1024, 1024], P('dp', 'tp')
- self_output_grad: float32 [1024, 1024], P('tp', 'dp')
- cross_query_grad: float32 [1024, 1024], P('dp', 'tp')
- cross_key_grad: float32 [1024, 1024], P('dp', 'tp')
- cross_value_grad: float32 [1024, 1024], P('dp', 'tp')
- cross_output_grad: float32 [1024, 1024], P('tp', 'dp')
- mlp_up_grad: float32 [1024, 4096], P('dp', 'tp')
- mlp_down_grad: float32 [4096, 1024], P('tp', 'dp')
- attn_gain_grad: float32 [1024], P('dp')
- attn_shift_grad: float32 [1024], P('dp')
- cross_gain_grad: float32 [1024], P('dp')
- cross_shift_grad: float32 [1024], P('dp')
- mlp_gain_grad: float32 [1024], P('dp')
- mlp_shift_grad: float32 [1024], P('dp')
The draws below stay inside these ranges and needn't reach their ends.
Inputs may be any that keep to these rules, and one draw needn't show every extreme that they name: Image i's caption holds its first caption_lengths[i] slots; in every draw at least one image has all 128.
All inputs are finite; a program needn't handle non-finite values.
Results may differ from the reference program's by a relative error of at most 0.022.
Values may be sent and summed in bfloat16 or wider, within the bound.
A program may use at most 128 MiB of HBM per device.

```python
import math
import jax
import jax.numpy as jnp
from jax import lax

D = 1024
HEADS = 16
HEAD = 64
FF = 4096
TEXT = 128
SEQ = 1024
IMAGES = 8
TOKENS = 8192


def draw_caption_lengths(key, part):
    power_key = jax.random.fold_in(key, 101)
    value_key = jax.random.fold_in(key, 202)
    place_key = jax.random.fold_in(key, 303)
    powers = jax.random.randint(power_key, (IMAGES,), 0, 8)
    ceiling = jnp.left_shift(jnp.ones((IMAGES,), jnp.int32), powers)
    drawn = jax.random.randint(value_key, (IMAGES,), 0, 1048576) % ceiling + 1
    longest = jax.random.randint(place_key, (), 0, IMAGES)
    drawn = jnp.where(jnp.arange(IMAGES) == longest, TEXT, drawn)
    return jnp.minimum(drawn, TEXT).astype(jnp.int32)


def levels(key, shape, pieces, smallest, high):
    def one(axis_at, shards_of):
        draws = jax.random.uniform(jax.random.fold_in(jax.random.fold_in(key, 6), axis_at), (shards_of,), jnp.float32, smallest / len(pieces), high / len(pieces))
        return jnp.repeat(jnp.exp(draws), shape[axis_at] // shards_of).reshape((-1,) + (1,) * (len(shape) - axis_at - 1))

    level = one(*pieces[0])
    for cut in pieces[1:]:
        level = level * one(*cut)
    return level


def scatter_about(rng, extent, width, bound, shards=(), held_as=jnp.bfloat16):
    level = levels(rng, extent, shards, -0.22, 0.18) if shards else 1.0
    result = jax.random.normal(rng, extent, jnp.float32) * width * level
    return jnp.minimum(jnp.maximum(result, -bound), bound).astype(held_as)


def setup_inputs(seed: int = 0) -> dict:
    arg_keys = jax.random.split(jax.random.key(seed), 21)
    return {
        "image_rows": scatter_about(arg_keys[0], (TOKENS, D), 1.0, 6.0, ((0, 32),)),
        "text_states": scatter_about(arg_keys[1], (IMAGES, TEXT, D), 1.0, 6.0, ((0, 8),)),
        "caption_lengths": draw_caption_lengths(jax.random.fold_in(arg_keys[20], 71), 0),
        "out_grad": scatter_about(arg_keys[3], (TOKENS, D), 1.0, 6.0, ((0, 8),)),
        "self_query": scatter_about(arg_keys[4], (D, HEADS * HEAD), D ** -0.5, 0.1875, ((1, 4),)),
        "self_key": scatter_about(arg_keys[5], (D, HEADS * HEAD), D ** -0.5, 0.1875, ((1, 4),)),
        "self_value": scatter_about(arg_keys[6], (D, HEADS * HEAD), D ** -0.5, 0.1875, ((1, 4),)),
        "self_output": scatter_about(arg_keys[7], (HEADS * HEAD, D), (HEADS * HEAD // 32) ** -0.5, 1.0, ((0, 4),)),
        "cross_query": scatter_about(arg_keys[8], (D, HEADS * HEAD), D ** -0.5, 0.1875, ((1, 4),)),
        "cross_key": scatter_about(arg_keys[9], (D, HEADS * HEAD), D ** -0.5, 0.1875, ((1, 4),)),
        "cross_value": scatter_about(arg_keys[10], (D, HEADS * HEAD), D ** -0.5, 0.1875, ((1, 4),)),
        "cross_output": scatter_about(arg_keys[11], (HEADS * HEAD, D), (HEADS * HEAD // 4) ** -0.5, 0.375, ((0, 4),)),
        "mlp_up": scatter_about(arg_keys[12], (D, FF), D ** -0.5, 0.1875, ((1, 4),)),
        "mlp_down": scatter_about(arg_keys[13], (FF, D), FF ** -0.5, 0.09375, ((0, 4),)),
        "attn_gain": jnp.clip(1.0 + 0.1 * jax.random.normal(arg_keys[14], (D,), jnp.float32), 0.5, 1.5),
        "attn_shift": scatter_about(arg_keys[15], (D,), 0.3, 1.75, (), jnp.float32),
        "cross_gain": jnp.clip(1.0 + 0.1 * jax.random.normal(arg_keys[16], (D,), jnp.float32), 0.5, 1.5),
        "cross_shift": scatter_about(arg_keys[17], (D,), 0.3, 1.75, (), jnp.float32),
        "mlp_gain": jnp.clip(1.0 + 0.1 * jax.random.normal(arg_keys[18], (D,), jnp.float32), 0.5, 1.5),
        "mlp_shift": scatter_about(arg_keys[19], (D,), 0.3, 1.75, (), jnp.float32),
    }


EPSILON = 1e-05
MASKED = -1e+30
PRECISE = lax.Precision.HIGHEST

@jax.custom_vjp
def low(v):
    return lax.optimization_barrier(v.astype(jnp.bfloat16)).astype(jnp.float32)

@jax.custom_vjp
def low_back(v):
    return v

def low_keep(v):
    return (low(v), None)

def low_pass(kept, grad):
    return (grad,)

def back_keep(v):
    return (v, None)

def back_low(kept, grad):
    return (low(grad),)
low.defvjp(low_keep, low_pass)
low_back.defvjp(back_keep, back_low)

def matmul(left, right):
    return jnp.dot(left, right, precision=PRECISE)

def layer_norm(hidden, norm_gain, norm_shift):
    middle = lax.optimization_barrier(jnp.mean(hidden, axis=-1, keepdims=True))
    centred = hidden - middle
    spread = lax.optimization_barrier(jnp.mean(centred * centred, axis=-1, keepdims=True))
    return centred * lax.rsqrt(spread + EPSILON) * norm_gain + norm_shift

def softmax_rows(scores):
    row_peak = lax.optimization_barrier(jnp.max(scores, axis=-1, keepdims=True))
    shifted = jnp.exp(scores - row_peak)
    return shifted / lax.optimization_barrier(jnp.sum(shifted, axis=-1, keepdims=True))

def attend_image(queries, keys, values, keep_mask):
    scores = low_back(jnp.einsum('qhd,khd->hqk', queries, keys, precision=PRECISE) * HEAD ** (-0.5))
    scores = jnp.where(keep_mask[None], scores, MASKED)
    probs = low(softmax_rows(scores))
    mixed = jnp.einsum('hqk,khd->qhd', probs, values, precision=PRECISE)
    return mixed.reshape(mixed.shape[0], -1)

def self_image(items):
    queries, keys, values = items
    keep_mask = jnp.arange(SEQ)[:, None] >= jnp.arange(SEQ)[None, :]
    return attend_image(queries, keys, values, keep_mask)

def cross_image(items):
    queries, keys, values, length_one = items
    keep_mask = jnp.broadcast_to(jnp.arange(TEXT)[None, :] < length_one, (SEQ, TEXT))
    return attend_image(queries, keys, values, keep_mask)

def layer_group(row_block, text_block, length_block, params):
    self_query, self_key, self_value, self_output, cross_query, cross_key, cross_value, cross_output, mlp_up, mlp_down, attn_gain, attn_shift, cross_gain, cross_shift, mlp_gain, mlp_shift = params
    image_count = text_block.shape[0]
    norm_one = low(layer_norm(row_block, attn_gain, attn_shift))
    queries = low_back(low(matmul(norm_one, self_query))).reshape(image_count, SEQ, HEADS, HEAD)
    keys = low_back(low(matmul(norm_one, self_key))).reshape(image_count, SEQ, HEADS, HEAD)
    values = low_back(low(matmul(norm_one, self_value))).reshape(image_count, SEQ, HEADS, HEAD)
    self_mix = lax.map(jax.checkpoint(self_image), (queries, keys, values))
    self_mix = low_back(low(self_mix.reshape(image_count * SEQ, HEADS * HEAD)))
    after_self = row_block + low_back(matmul(self_mix, self_output))
    norm_two = low(layer_norm(after_self, cross_gain, cross_shift))
    cross_q = low_back(low(matmul(norm_two, cross_query))).reshape(image_count, SEQ, HEADS, HEAD)
    text_flat = text_block.reshape(image_count * TEXT, -1)
    cross_k = low_back(low(matmul(text_flat, cross_key))).reshape(image_count, TEXT, HEADS, HEAD)
    cross_v = low_back(low(matmul(text_flat, cross_value))).reshape(image_count, TEXT, HEADS, HEAD)
    cross_mix = lax.map(jax.checkpoint(cross_image), (cross_q, cross_k, cross_v, length_block))
    cross_mix = low_back(low(cross_mix.reshape(image_count * SEQ, HEADS * HEAD)))
    after_cross = after_self + low_back(matmul(cross_mix, cross_output))
    norm_three = low(layer_norm(after_cross, mlp_gain, mlp_shift))
    pre_act = low_back(matmul(norm_three, mlp_up))
    activated = low(jax.nn.gelu(pre_act, approximate=True))
    return after_cross + low_back(matmul(activated, mlp_down))

def reference(image_rows, text_states, caption_lengths, out_grad, self_query, self_key, self_value, self_output, cross_query, cross_key, cross_value, cross_output, mlp_up, mlp_down, attn_gain, attn_shift, cross_gain, cross_shift, mlp_gain, mlp_shift):
    weights = tuple((item.astype(jnp.float32) for item in (self_query, self_key, self_value, self_output, cross_query, cross_key, cross_value, cross_output, mlp_up, mlp_down, attn_gain, attn_shift, cross_gain, cross_shift, mlp_gain, mlp_shift)))
    group_images = math.gcd(IMAGES, max(1, 4096 // SEQ))
    steps_count = IMAGES // group_images
    lengths_grouped = caption_lengths.reshape(steps_count, group_images)

    def forward(all_rows, all_texts, *params):

        def one_step(carry, items):
            row_block, text_block, length_block = items
            return (carry, jax.checkpoint(layer_group)(row_block, text_block, length_block, params))
        _, outputs = lax.scan(one_step, jnp.zeros((), jnp.float32), (all_rows.reshape(steps_count, group_images * SEQ, -1), all_texts.reshape(steps_count, group_images, TEXT, -1), lengths_grouped))
        return outputs.reshape(all_rows.shape)
    layer_out, pullback = jax.vjp(forward, image_rows.astype(jnp.float32), text_states.astype(jnp.float32), *weights)
    grads = pullback(out_grad.astype(jnp.float32))
    return (layer_out.astype(jnp.bfloat16), grads[0], grads[1], grads[2], grads[3], grads[4], grads[5], grads[6], grads[7], grads[8], grads[9], grads[10], grads[11], grads[12], grads[13], grads[14], grads[15], grads[16], grads[17])
```

```python
import functools

import jax
import jax.numpy as jnp
from jax import lax
from jax.experimental import pallas as pl
from jax.experimental.pallas import tpu as pltpu
from jax.sharding import PartitionSpec as P

HEAD = 64
TEXT = 128
SEQ = 1024
BLOCK_LIMIT = 512
EPSILON = 1e-05
MASKED = -1e30
MESH = pl.DeviceIdType.MESH
F32 = jnp.float32
BF16 = jnp.bfloat16
ANY = pl.BlockSpec(memory_space=pl.ANY)
VM = pl.BlockSpec(memory_space=pltpu.VMEM)
GRANT = 60 * 1024 * 1024


def nn(left, right):
    return lax.dot_general(left, right, (((1,), (0,)), ((), ())), preferred_element_type=F32)


def nt(left, right):
    return lax.dot_general(left, right, (((1,), (1,)), ((), ())), preferred_element_type=F32)


def tn(left, right):
    return lax.dot_general(left, right, (((0,), (0,)), ((), ())), preferred_element_type=F32)


def norm_stats(hidden):
    middle = jnp.mean(hidden, axis=-1, keepdims=True)
    centred = hidden - middle
    spread = jnp.mean(centred * centred, axis=-1, keepdims=True)
    rstd = lax.rsqrt(spread + EPSILON)
    return centred * rstd, rstd


def norm_input_grad(xhat, rstd, gain, cotangent):
    scaled = cotangent * gain
    first = jnp.mean(scaled, axis=-1, keepdims=True)
    second = jnp.mean(scaled * xhat, axis=-1, keepdims=True)
    return (scaled - first - xhat * second) * rstd


def fold_rows(value):
    rows = value.shape[0]
    total = value[0:8]
    for start in range(8, rows, 8):
        total = total + value[start : start + 8]
    return total


def lane_keep(shape, part):
    lanes = lax.broadcasted_iota(jnp.int32, shape, 1)
    return (lanes // HEAD) == part


def pick(value, part):
    return jnp.where(lane_keep(value.shape, part), value, jnp.zeros_like(value))


def merge(first, second):
    return jnp.where(lane_keep(first.shape, 0), first, second)


CHUNK = 128
STEPS = 4
SUB = 32


def natural(core, step):
    return 256 * (core + 2 * (step // 2)) + 128 * (step % 2)


def middle_kernel(
    x_full, self_mix, out_grad, wo_h, wcq_h, wco_h, wup_h, wdn_h,
    ck_ref, cv_ref, bias_ref, cg_ref, cs_ref, mg_ref, ms_ref,
    smg_out, sb_out, act_out, dup_out, ddn_out, dcq_out, dco_out, dck_out, dcv_out, parts_out, resid_out, ac_out,
    wo, wcq, wco, wup, wdn, smix, og, xr, h1, h2, acc, g2, nf, act, pg, cq, cmix, cqg,
    rr, yr, sst, yst, pbuf, dkv, smg, upst, dnst, dco, dcq, parts,
    load_sem, cs_sem, cr_sem, ns_sem, nr_sem, ys_sem, yr_sem, out_sem,
):
    rank = lax.axis_index("tp")
    core = lax.rem(rank, 2)
    chip = rank // 2
    pal = rank + 1 - 2 * core
    far = lax.rem(rank + 2, 4)
    barrier = pltpu.get_barrier_semaphore()
    for peer in (pal, far):
        pl.semaphore_signal(barrier, inc=1, device_id={"tp": peer}, device_id_type=MESH)

    loads = []

    def load(src, dst):
        copy = pltpu.make_async_copy(src, dst, load_sem.at[len(loads)])
        copy.start()
        loads.append(copy)

    for k in range(STEPS):
        for c in range(2):
            load(self_mix.at[pl.ds(natural(c, k), CHUNK)], smix.at[pl.ds(k * 256 + c * 128, CHUNK)])
    load(wo_h, wo)
    n_first = len(loads)
    for k in range(STEPS):
        start = pl.multiple_of(256 * (core + 2 * (k // 2)) + 128 * (k % 2), 128)
        load(x_full.at[pl.ds(start, CHUNK)], xr.at[pl.ds(k * CHUNK, CHUNK)])
    load(wcq_h, wcq)
    load(wco_h, wco)
    n_second = len(loads)
    for k in range(STEPS):
        for c in range(2):
            load(out_grad.at[pl.ds(natural(c, k), CHUNK)], og.at[pl.ds(k * 256 + c * 128, CHUNK)])
    load(wup_h, wup)
    load(wdn_h, wdn)
    n_third = len(loads)

    dkv[...] = jnp.zeros_like(dkv)
    parts[...] = jnp.zeros_like(parts)

    def own(k):
        return pl.ds(pl.multiple_of(k * CHUNK, CHUNK), CHUNK)

    def pair(k):
        return pl.ds(pl.multiple_of(k * 256, 256), 256)

    def mine(k):
        return pl.ds(pl.multiple_of(k * 256 + core * CHUNK, CHUNK), CHUNK)

    def red_copy(s, k):
        return pltpu.make_async_remote_copy(
            sst.at[own(k)], rr.at[s, own(k)], cs_sem.at[s, k], cr_sem.at[s, k],
            device_id={"tp": pal}, device_id_type=MESH)

    def far_copy(s, k):
        return pltpu.make_async_remote_copy(
            yst.at[own(k)], yr.at[s, own(k)], ys_sem.at[s, k], yr_sem.at[s, k],
            device_id={"tp": far}, device_id_type=MESH)

    def norm_copy(s, k):
        return pltpu.make_async_remote_copy(
            nf.at[s, mine(k)], nf.at[s, mine(k)], ns_sem.at[s, k], nr_sem.at[s, k],
            device_id={"tp": pal}, device_id_type=MESH)

    def produce(s, k, columns):
        for j, value in columns:
            pbuf[:, j : j + value.shape[1]] = value
        if s > 0:
            red_copy(s - 1, k).wait_send()
        sst[own(k)] = pbuf[pl.ds(pl.multiple_of((1 - core) * CHUNK, CHUNK), CHUNK), :].astype(BF16)
        red_copy(s, k).start()
        acc[own(k)] = pbuf[pl.ds(pl.multiple_of(core * CHUNK, CHUNK), CHUNK), :]

    def finish(s, k):
        if s > 0:
            far_copy(s - 1, k).wait_send()
        red_copy(s, k).wait_recv()
        total = acc[own(k)] + rr[s, own(k)].astype(F32)
        acc[own(k)] = total
        yst[own(k)] = total.astype(BF16)
        far_copy(s, k).start()

    def sub(k, r):
        return pl.ds(pl.multiple_of(k * CHUNK + r * SUB, SUB), SUB)

    def msub(k, r):
        return pl.ds(pl.multiple_of(k * 256 + core * CHUNK + r * SUB, SUB), SUB)

    for copy in loads[:n_first]:
        copy.wait()
    pl.semaphore_wait(barrier, 2)

    @pl.loop(0, STEPS)
    def _(k):
        rows = smix[pair(k), :]
        produce(0, k, [(j, nn(rows, wo[:, j : j + 512])) for j in (0, 512)])

        @pl.when(k > 0)
        def _():
            finish(0, k - 1)

    finish(0, STEPS - 1)
    for copy in loads[n_first:n_second]:
        copy.wait()

    scale = HEAD ** (-0.5)

    def place(src, dst, k, c, slot):
        start = pl.multiple_of(256 * (c + 2 * (k // 2)) + 128 * (k % 2), 128)
        return pltpu.make_async_copy(
            src.at[pl.ds(pl.multiple_of(k * 256 + c * CHUNK, CHUNK), CHUNK)],
            dst.at[pl.ds(start, CHUNK)], out_sem.at[slot + 2 * k + c])

    @pl.loop(0, STEPS)
    def _(k):
        far_copy(0, k).wait_recv()
        for r in range(CHUNK // SUB):
            hidden = xr[sub(k, r)].astype(F32) + acc[sub(k, r)] + yr[0, sub(k, r)].astype(F32)
            h1[sub(k, r)] = hidden
            xhat, _ = norm_stats(hidden)
            nf[0, msub(k, r)] = (xhat * cg_ref[...] + cs_ref[...]).astype(BF16)
        norm_copy(0, k).start()

        @pl.when(k > 0)
        def _():
            finish(1, k - 1)

        norm_copy(0, k).wait_recv()
        cq[pair(k)] = nn(nf[0, pair(k)], wcq[...]).astype(BF16)
        for slab in range(2):
            lanes = slice(slab * 128, slab * 128 + 128)
            query = cq[pair(k), lanes]
            key, value = ck_ref[:, lanes], cv_ref[:, lanes]
            mixed = []
            for part in range(2):
                scores = nt(pick(query, part), key) * scale + bias_ref[...]
                shifted = jnp.exp(scores - jnp.max(scores, axis=-1, keepdims=True))
                probs = shifted / jnp.sum(shifted, axis=-1, keepdims=True)
                mixed.append(nn(probs.astype(BF16), value))
            cmix[pair(k), lanes] = merge(*mixed).astype(BF16)
        rows = cmix[pair(k), :]
        produce(1, k, [(j, nn(rows, wco[:, j : j + 512])) for j in (0, 512)])

    finish(1, STEPS - 1)
    for copy in loads[n_second:n_third]:
        copy.wait()

    @pl.loop(0, STEPS)
    def _(k):
        far_copy(1, k).wait_recv()
        for r in range(CHUNK // SUB):
            hidden = h1[sub(k, r)] + acc[sub(k, r)] + yr[1, sub(k, r)].astype(F32)
            h2[sub(k, r)] = hidden
            xhat, _ = norm_stats(hidden)
            nf[1, msub(k, r)] = (xhat * mg_ref[...] + ms_ref[...]).astype(BF16)
        norm_copy(1, k).start()

        @pl.when(k > 0)
        def _():
            finish(2, k - 1)

        norm_copy(1, k).wait_recv()
        rows = nf[1, pair(k)]
        grads = og[pair(k), :]
        for j in range(0, 1024, 256):
            cols = slice(j, j + 256)
            pre = nn(rows, wup[:, cols])
            back = nt(grads, wdn[cols, :])
            square = pre * pre
            bend = jnp.tanh(0.7978845608028654 * pre * (1.0 + 0.044715 * square))
            half = 0.5 * (1.0 + bend)
            act[pair(k), cols] = (pre * half).astype(BF16)
            slope = half + 0.5 * pre * (1.0 - bend * bend) * (
                0.7978845608028654 * (1.0 + 3 * 0.044715 * square))
            pg[pair(k), cols] = (back * slope).astype(BF16)
        rows = pg[pair(k), :]
        produce(2, k, [(j, nt(rows, wup[j : j + 256, :])) for j in range(0, 1024, 256)])
        for c in range(2):
            place(act, act_out, k, c, 2).start()

    finish(2, STEPS - 1)

    def dup_copy(k):
        at = pl.multiple_of(k * 256, 256)
        return pltpu.make_async_copy(upst, dup_out.at[pl.ds(at, 256)], out_sem.at[0])

    def ddn_copy(k):
        at = pl.multiple_of(k * 256, 256)
        return pltpu.make_async_copy(dnst, ddn_out.at[:, pl.ds(at, 256)], out_sem.at[1])

    def own_rows(k):
        return jnp.where(k // 2 == chip, 1.0, 0.0)

    @pl.loop(0, STEPS)
    def _(k):
        @pl.when(k > 0)
        def _():
            dup_copy(k - 1).wait()
            ddn_copy(k - 1).wait()

        at = pl.multiple_of(k * 256, 256)
        upst[...] = tn(nf[1, :, pl.ds(at, 256)], pg[...]).astype(BF16)
        dup_copy(k).start()
        for j in range(0, 1024, 256):
            dnst[j : j + 256, :] = tn(act[:, j : j + 256], og[:, pl.ds(at, 256)]).astype(BF16)
        ddn_copy(k).start()
        far_copy(2, k).wait_recv()
        keep = own_rows(k)
        for r in range(CHUNK // SUB):
            third = acc[sub(k, r)] + yr[2, sub(k, r)].astype(F32)
            xhat, rstd = norm_stats(h2[sub(k, r)])
            parts[2] += fold_rows(third * xhat) * keep
            parts[3] += fold_rows(third) * keep
            resid = og[msub(k, r)].astype(F32) + norm_input_grad(xhat, rstd, mg_ref[...], third)
            g2[sub(k, r)] = resid
            nf[2, msub(k, r)] = resid.astype(BF16)
        norm_copy(2, k).start()

        @pl.when(k > 0)
        def _():
            finish(3, k - 1)

        norm_copy(2, k).wait_recv()
        mix_grad = nt(nf[2, pair(k)], wco[...]).astype(BF16)
        for slab in range(2):
            lanes = slice(slab * 128, slab * 128 + 128)
            query = cq[pair(k), lanes]
            grad = mix_grad[:, lanes]
            key, value = ck_ref[:, lanes], cv_ref[:, lanes]
            moved = []
            for part in range(2):
                one_q, one_g = pick(query, part), pick(grad, part)
                scores = nt(one_q, key) * scale + bias_ref[...]
                shifted = jnp.exp(scores - jnp.max(scores, axis=-1, keepdims=True))
                probs = shifted / jnp.sum(shifted, axis=-1, keepdims=True)
                prob_grad = nt(one_g, value)
                inner = jnp.sum(probs * prob_grad, axis=-1, keepdims=True)
                score_grad = (probs * (prob_grad - inner)).astype(BF16)
                moved.append(nn(score_grad, key) * scale)
                dkv[0, :, lanes] += tn(score_grad, one_q)
                dkv[1, :, lanes] += tn(probs.astype(BF16), one_g)
            cqg[pair(k), lanes] = merge(*moved).astype(BF16)
        rows = cqg[pair(k), :]
        produce(3, k, [(j, nt(rows, wcq[j : j + 512, :])) for j in (0, 512)])

    finish(3, STEPS - 1)
    for copy in (dup_copy(STEPS - 1), ddn_copy(STEPS - 1)):
        copy.wait()

    @pl.loop(0, STEPS)
    def _(k):
        at = pl.multiple_of(k * 256, 256)
        dcq[pl.ds(at, 256), :] = tn(nf[0, :, pl.ds(at, 256)], cqg[...]).astype(BF16)
        dco[:, pl.ds(at, 256)] = tn(cmix[...], nf[2, :, pl.ds(at, 256)]).astype(BF16)
        far_copy(3, k).wait_recv()
        keep = own_rows(k)
        for r in range(CHUNK // SUB):
            second = acc[sub(k, r)] + yr[3, sub(k, r)].astype(F32)
            xhat, rstd = norm_stats(h1[sub(k, r)])
            parts[0] += fold_rows(second * xhat) * keep
            parts[1] += fold_rows(second) * keep
            resid = g2[sub(k, r)] + norm_input_grad(xhat, rstd, cg_ref[...], second)
            g2[sub(k, r)] = resid
            nf[3, msub(k, r)] = resid.astype(BF16)
        norm_copy(3, k).start()
        norm_copy(3, k).wait_recv()
        smg[pair(k)] = nt(nf[3, pair(k)], wo[...]).astype(BF16)
        for c in range(2):
            place(smg, smg_out, k, c, 10).start()
            place(nf.at[3], sb_out, k, c, 18).start()

    mine_rows = pl.ds(pl.multiple_of(chip * 256, 256), 256)
    final = [
        pltpu.make_async_copy(g2.at[mine_rows], resid_out, out_sem.at[26]),
        pltpu.make_async_copy(h2.at[mine_rows], ac_out, out_sem.at[27]),
        pltpu.make_async_copy(dcq, dcq_out, out_sem.at[28]),
        pltpu.make_async_copy(dco, dco_out, out_sem.at[29]),
    ]
    for copy in final:
        copy.start()
    dck_out[...] = (dkv[0] * scale).astype(BF16)
    dcv_out[...] = dkv[1].astype(BF16)
    parts_out[...] = parts[...]
    for k in range(STEPS):
        red_copy(3, k).wait_send()
        far_copy(3, k).wait_send()
        for s in range(4):
            norm_copy(s, k).wait_send()
        for c in range(2):
            place(act, act_out, k, c, 2).wait()
            place(smg, smg_out, k, c, 10).wait()
            place(nf.at[3], sb_out, k, c, 18).wait()
    for copy in final:
        copy.wait()


def middle(x_full, self_mix, out_grad, wo, wcq, wco, wup, wdn, ck, cv, bias, gains):
    full = jax.ShapeDtypeStruct((1024, 1024), BF16)
    narrow = jax.ShapeDtypeStruct((1024, 256), BF16)
    short = jax.ShapeDtypeStruct((128, 256), BF16)
    block = jax.ShapeDtypeStruct((256, 1024), F32)
    outs = [
        narrow, full, full, full, full, narrow, jax.ShapeDtypeStruct((256, 1024), BF16), short, short,
        jax.ShapeDtypeStruct((4, 8, 1024), F32), block, block,
    ]
    out_specs = [ANY] * 7 + [VM] * 3 + [ANY] * 2
    vm = pltpu.VMEM
    dma = pltpu.SemaphoreType.DMA
    scratch = [
        vm((256, 1024), BF16), vm((1024, 256), BF16), vm((256, 1024), BF16), vm((1024, 1024), BF16),
        vm((1024, 1024), BF16), vm((1024, 256), BF16), vm((1024, 1024), BF16), vm((512, 1024), BF16),
        vm((512, 1024), F32), vm((512, 1024), F32), vm((512, 1024), F32), vm((512, 1024), F32),
        vm((4, 1024, 1024), BF16), vm((1024, 1024), BF16), vm((1024, 1024), BF16),
        vm((1024, 256), BF16), vm((1024, 256), BF16), vm((1024, 256), BF16),
        vm((4, 512, 1024), BF16), vm((4, 512, 1024), BF16), vm((512, 1024), BF16), vm((512, 1024), BF16),
        vm((256, 1024), F32), vm((2, 128, 256), F32), vm((1024, 256), BF16),
        vm((256, 1024), BF16), vm((1024, 256), BF16), vm((256, 1024), BF16), vm((1024, 256), BF16),
        vm((4, 8, 1024), F32),
        dma((32,)), dma((4, 4)), dma((4, 4)), dma((4, 4)), dma((4, 4)), dma((4, 4)), dma((4, 4)), dma((32,)),
    ]
    return pl.pallas_call(
        middle_kernel,
        out_shape=outs,
        in_specs=[ANY] * 8 + [VM] * 7,
        out_specs=out_specs,
        scratch_shapes=scratch,
        name="middle",
        compiler_params=pltpu.CompilerParams(
            collective_id=1, has_side_effects=True, vmem_limit_bytes=GRANT),
    )(x_full, self_mix, out_grad, wo, wcq, wco, wup, wdn, ck, cv, bias, *gains)


def matmul(left, right):
    return jnp.dot(left, right, preferred_element_type=jnp.float32)


def matmul_tn(left, right):
    return lax.dot_general(
        left, right, (((0,), (0,)), ((), ())), preferred_element_type=jnp.float32
    )


def matmul_nt(left, right):
    return lax.dot_general(
        left, right, (((1,), (1,)), ((), ())), preferred_element_type=jnp.float32
    )


def layer_norm(hidden, norm_gain, norm_shift):
    middle = jnp.mean(hidden, axis=-1, keepdims=True)
    centred = hidden - middle
    spread = jnp.mean(centred * centred, axis=-1, keepdims=True)
    return centred * lax.rsqrt(spread + EPSILON) * norm_gain + norm_shift


def norm_back(hidden, norm_gain, norm_shift, cotangent):
    _, pullback = jax.vjp(layer_norm, hidden, norm_gain, norm_shift)
    return pullback(cotangent)


def gelu_tanh(inputs):
    return jax.nn.gelu(inputs, approximate=True)


def gelu_back(pre_act, cotangent):
    _, pullback = jax.vjp(gelu_tanh, pre_act)
    return pullback(cotangent)[0]


def take_rows(array, start, count):
    return lax.dynamic_slice_in_dim(array, start, count, 0)


def block_scores(query_block, key_block, keep_mask):
    scores = jnp.einsum(
        "qhd,khd->hqk", query_block, key_block, preferred_element_type=jnp.float32
    ) * HEAD ** (-0.5)
    return jnp.where(keep_mask[None], scores, MASKED)


def attend_forward(queries, keys, values, key_len, block_rows, keep_fn):
    total_rows, columns = queries.shape
    heads_here = columns // HEAD
    per_image = SEQ // block_rows

    def one_block(number):
        image_pos = number // per_image
        query_block = take_rows(queries, number * block_rows, block_rows).reshape(
            block_rows, heads_here, HEAD
        )
        key_block = take_rows(keys, image_pos * key_len, key_len).reshape(key_len, heads_here, HEAD)
        value_block = take_rows(values, image_pos * key_len, key_len).reshape(
            key_len, heads_here, HEAD
        )
        scores = block_scores(query_block, key_block, keep_fn(image_pos, number % per_image))
        row_peak = jnp.max(scores, axis=-1, keepdims=True)
        shifted = jnp.exp(scores - row_peak)
        totals = jnp.sum(shifted, axis=-1, keepdims=True)
        probs = (shifted / totals).astype(jnp.bfloat16)
        mixed = jnp.einsum("hqk,khd->qhd", probs, value_block, preferred_element_type=jnp.float32)
        return (
            mixed.reshape(block_rows, columns).astype(jnp.bfloat16),
            (row_peak + jnp.log(totals))[..., 0],
        )

    mixed, log_sums = lax.map(one_block, jnp.arange(total_rows // block_rows))
    return (mixed.reshape(total_rows, columns), log_sums)


def attend_backward(queries, keys, values, log_sums, out_grads, key_len, block_rows, keep_fn):
    total_rows, columns = queries.shape
    heads_here = columns // HEAD
    per_image = SEQ // block_rows

    def one_block(carry, items):
        key_acc, value_acc = carry
        number, log_sum = items
        image_pos = number // per_image
        key_start = image_pos * key_len
        query_block = take_rows(queries, number * block_rows, block_rows).reshape(
            block_rows, heads_here, HEAD
        )
        key_block = take_rows(keys, key_start, key_len).reshape(key_len, heads_here, HEAD)
        value_block = take_rows(values, key_start, key_len).reshape(key_len, heads_here, HEAD)
        scores = block_scores(query_block, key_block, keep_fn(image_pos, number % per_image))
        probs = jnp.exp(scores - log_sum[..., None])
        grad_block = take_rows(out_grads, number * block_rows, block_rows).reshape(
            block_rows, heads_here, HEAD
        )
        prob_grad = jnp.einsum(
            "qhd,khd->hqk", grad_block, value_block, preferred_element_type=jnp.float32
        )
        inner = jnp.sum(probs * prob_grad, axis=-1, keepdims=True)
        score_grad = (probs * (prob_grad - inner)).astype(jnp.bfloat16)
        query_grad = jnp.einsum(
            "hqk,khd->qhd", score_grad, key_block, preferred_element_type=jnp.float32
        ) * HEAD ** (-0.5)
        key_part = jnp.einsum(
            "hqk,qhd->khd", score_grad, query_block, preferred_element_type=jnp.float32
        ) * HEAD ** (-0.5)
        value_part = jnp.einsum(
            "hqk,qhd->khd",
            probs.astype(jnp.bfloat16),
            grad_block,
            preferred_element_type=jnp.float32,
        )
        key_acc = take_rows(key_acc, key_start, key_len) + key_part.reshape(key_len, columns)
        value_acc = take_rows(value_acc, key_start, key_len) + value_part.reshape(key_len, columns)
        return ((key_acc, value_acc), query_grad.reshape(block_rows, columns).astype(jnp.bfloat16))

    empty = jnp.zeros(keys.shape, jnp.float32)
    (key_acc, value_acc), query_grads = lax.scan(
        one_block, (empty, empty), (jnp.arange(total_rows // block_rows), log_sums)
    )
    return (
        query_grads.reshape(total_rows, columns),
        key_acc.astype(jnp.bfloat16),
        value_acc.astype(jnp.bfloat16),
    )


def local(
    image_rows,
    text_states,
    caption_lengths,
    out_grad,
    self_query,
    self_key,
    self_value,
    self_output,
    cross_query,
    cross_key,
    cross_value,
    cross_output,
    mlp_up,
    mlp_down,
    attn_gain,
    attn_shift,
    cross_gain,
    cross_shift,
    mlp_gain,
    mlp_shift,
):
    tp_rank = lax.axis_index("tp")
    own_rows = image_rows.shape[0]
    block_rows = min(BLOCK_LIMIT, SEQ)
    x_here = image_rows.astype(jnp.float32)

    def self_causal(image_pos, block_pos):
        query_pos = block_pos * block_rows + jnp.arange(block_rows)
        return query_pos[:, None] >= jnp.arange(SEQ)[None, :]

    def text_keep(image_pos, block_pos):
        return jnp.broadcast_to(
            jnp.arange(TEXT)[None, :] < caption_lengths[image_pos], (block_rows, TEXT)
        )

    x_full = lax.all_gather(image_rows, "tp", axis=0, tiled=True)
    first_in = layer_norm(x_full.astype(jnp.float32), attn_gain, attn_shift).astype(jnp.bfloat16)
    queries = matmul(first_in, self_query).astype(jnp.bfloat16)
    keys = matmul(first_in, self_key).astype(jnp.bfloat16)
    values = matmul(first_in, self_value).astype(jnp.bfloat16)
    self_mix, self_sums = attend_forward(queries, keys, values, SEQ, block_rows, self_causal)
    text_flat = text_states.reshape(-1, text_states.shape[-1])
    cross_k = matmul(text_flat, cross_key).astype(jnp.bfloat16)
    cross_v = matmul(text_flat, cross_value).astype(jnp.bfloat16)
    bias = jnp.where(jnp.arange(TEXT)[None, :] < caption_lengths[0], 0.0, MASKED)
    gains = [item[None, :] for item in (cross_gain, cross_shift, mlp_gain, mlp_shift)]
    (
        self_mix_grad, self_back, activated, up_grad, down_grad, cross_query_grad, cross_output_grad,
        cross_k_grad, cross_v_grad, norm_parts, self_resid, after_cross,
    ) = middle(
        x_full, self_mix, out_grad, self_output, cross_query, cross_output, mlp_up, mlp_down,
        cross_k, cross_v, bias, gains)
    cross_gain_part, cross_shift_part, mlp_gain_part, mlp_shift_part = jnp.sum(norm_parts, axis=1)
    layer_out = (
        after_cross
        + lax.psum_scatter(
            matmul(activated, mlp_down).astype(jnp.bfloat16), "tp", scatter_dimension=0, tiled=True
        ).astype(jnp.float32)
    ).astype(jnp.bfloat16)
    cross_key_grad = matmul_tn(text_flat, cross_k_grad)
    cross_value_grad = matmul_tn(text_flat, cross_v_grad)
    text_part = (matmul_nt(cross_k_grad, cross_key) + matmul_nt(cross_v_grad, cross_value)).reshape(
        text_states.shape
    )
    self_output_grad = matmul_tn(self_mix, self_back)
    query_grad, key_grad, value_grad = attend_backward(
        queries, keys, values, self_sums, self_mix_grad, SEQ, block_rows, self_causal
    )
    self_query_grad = matmul_tn(first_in, query_grad)
    self_key_grad = matmul_tn(first_in, key_grad)
    self_value_grad = matmul_tn(first_in, value_grad)
    start = jnp.int32(0)
    first_grad = lax.psum_scatter(
        (
            matmul_nt(take_rows(query_grad, start, own_rows * lax.axis_size("tp")), self_query)
            + matmul_nt(take_rows(key_grad, start, own_rows * lax.axis_size("tp")), self_key)
            + matmul_nt(take_rows(value_grad, start, own_rows * lax.axis_size("tp")), self_value)
        ).astype(jnp.bfloat16),
        "tp",
        scatter_dimension=0,
        tiled=True,
    ).astype(jnp.float32)
    input_dh, attn_gain_part, attn_shift_part = norm_back(x_here, attn_gain, attn_shift, first_grad)
    image_grad = self_resid + input_dh
    norm_parts = jnp.stack(
        [
            attn_gain_part,
            attn_shift_part,
            cross_gain_part,
            cross_shift_part,
            mlp_gain_part,
            mlp_shift_part,
        ]
    )
    text_grad, norm_sums = (
        lax.psum(text_part.astype(jnp.bfloat16), "tp").astype(jnp.float32),
        lax.psum(norm_parts.astype(jnp.bfloat16), "tp").astype(jnp.float32),
    )
    shards = (
        lax.psum_scatter(
            self_query_grad.astype(jnp.bfloat16), "dp", scatter_dimension=0, tiled=True
        ).astype(jnp.float32),
        lax.psum_scatter(
            self_key_grad.astype(jnp.bfloat16), "dp", scatter_dimension=0, tiled=True
        ).astype(jnp.float32),
        lax.psum_scatter(
            self_value_grad.astype(jnp.bfloat16), "dp", scatter_dimension=0, tiled=True
        ).astype(jnp.float32),
        lax.psum_scatter(
            self_output_grad.astype(jnp.bfloat16), "dp", scatter_dimension=1, tiled=True
        ).astype(jnp.float32),
        lax.psum_scatter(
            cross_query_grad.astype(jnp.bfloat16), "dp", scatter_dimension=0, tiled=True
        ).astype(jnp.float32),
        lax.psum_scatter(
            cross_key_grad.astype(jnp.bfloat16), "dp", scatter_dimension=0, tiled=True
        ).astype(jnp.float32),
        lax.psum_scatter(
            cross_value_grad.astype(jnp.bfloat16), "dp", scatter_dimension=0, tiled=True
        ).astype(jnp.float32),
        lax.psum_scatter(
            cross_output_grad.astype(jnp.bfloat16), "dp", scatter_dimension=1, tiled=True
        ).astype(jnp.float32),
        lax.psum_scatter(
            up_grad.astype(jnp.bfloat16), "dp", scatter_dimension=0, tiled=True
        ).astype(jnp.float32),
        lax.psum_scatter(
            down_grad.astype(jnp.bfloat16), "dp", scatter_dimension=1, tiled=True
        ).astype(jnp.float32),
        lax.psum_scatter(
            norm_sums.astype(jnp.bfloat16), "dp", scatter_dimension=1, tiled=True
        ).astype(jnp.float32),
    )
    shards = (
        lax.psum(shards[0].astype(jnp.bfloat16), "grp").astype(jnp.float32),
        lax.psum(shards[1].astype(jnp.bfloat16), "grp").astype(jnp.float32),
        lax.psum(shards[2].astype(jnp.bfloat16), "grp").astype(jnp.float32),
        lax.psum(shards[3].astype(jnp.bfloat16), "grp").astype(jnp.float32),
        lax.psum(shards[4].astype(jnp.bfloat16), "grp").astype(jnp.float32),
        lax.psum(shards[5].astype(jnp.bfloat16), "grp").astype(jnp.float32),
        lax.psum(shards[6].astype(jnp.bfloat16), "grp").astype(jnp.float32),
        lax.psum(shards[7].astype(jnp.bfloat16), "grp").astype(jnp.float32),
        lax.psum(shards[8].astype(jnp.bfloat16), "grp").astype(jnp.float32),
        lax.psum(shards[9].astype(jnp.bfloat16), "grp").astype(jnp.float32),
        lax.psum(shards[10].astype(jnp.bfloat16), "grp").astype(jnp.float32),
    )
    norm_shards = shards[10]
    return (
        layer_out,
        image_grad,
        text_grad,
        shards[0],
        shards[1],
        shards[2],
        shards[3],
        shards[4],
        shards[5],
        shards[6],
        shards[7],
        shards[8],
        shards[9],
        norm_shards[0],
        norm_shards[1],
        norm_shards[2],
        norm_shards[3],
        norm_shards[4],
        norm_shards[5],
    )


def solution(mesh):
    placed = (
        P(("grp", "dp", "tp"), None),
        P(("grp", "dp"), None, None),
        P(("grp", "dp")),
        P(("grp", "dp"), None),
        P(None, "tp"),
        P(None, "tp"),
        P(None, "tp"),
        P("tp", None),
        P(None, "tp"),
        P(None, "tp"),
        P(None, "tp"),
        P("tp", None),
        P(None, "tp"),
        P("tp", None),
        P(),
        P(),
        P(),
        P(),
        P(),
        P(),
    )
    return jax.shard_map(
        local,
        mesh=mesh,
        in_specs=placed,
        out_specs=(
            P(("grp", "dp", "tp"), None),
            P(("grp", "dp", "tp"), None),
            P(("grp", "dp"), None, None),
            P("dp", "tp"),
            P("dp", "tp"),
            P("dp", "tp"),
            P("tp", "dp"),
            P("dp", "tp"),
            P("dp", "tp"),
            P("dp", "tp"),
            P("tp", "dp"),
            P("dp", "tp"),
            P("tp", "dp"),
            P("dp"),
            P("dp"),
            P("dp"),
            P("dp"),
            P("dp"),
            P("dp"),
        ),
        check_vma=False,
    )
```

```python
import functools

import jax
import jax.numpy as jnp
from jax import lax
from jax.experimental import pallas as pl
from jax.experimental.pallas import tpu as pltpu
from jax.sharding import PartitionSpec as P

HEAD = 64
TEXT = 128
EPSILON = 1e-05
MASKED = -1e30
MESH = pl.DeviceIdType.MESH
F32 = jnp.float32
BF16 = jnp.bfloat16
ANY = pl.BlockSpec(memory_space=pl.ANY)
VM = pl.BlockSpec(memory_space=pltpu.VMEM)
GRANT = 60 * 1024 * 1024


def nn(left, right):
    return lax.dot_general(left, right, (((1,), (0,)), ((), ())), preferred_element_type=F32)


def nt(left, right):
    return lax.dot_general(left, right, (((1,), (1,)), ((), ())), preferred_element_type=F32)


def tn(left, right):
    return lax.dot_general(left, right, (((0,), (0,)), ((), ())), preferred_element_type=F32)


def norm_stats(hidden):
    middle = jnp.mean(hidden, axis=-1, keepdims=True)
    centred = hidden - middle
    spread = jnp.mean(centred * centred, axis=-1, keepdims=True)
    rstd = lax.rsqrt(spread + EPSILON)
    return centred * rstd, rstd


def norm_input_grad(xhat, rstd, gain, cotangent):
    scaled = cotangent * gain
    first = jnp.mean(scaled, axis=-1, keepdims=True)
    second = jnp.mean(scaled * xhat, axis=-1, keepdims=True)
    return (scaled - first - xhat * second) * rstd


def fold_rows(value):
    rows = value.shape[0]
    total = value[0:8]
    for start in range(8, rows, 8):
        total = total + value[start : start + 8]
    return total


def lane_keep(shape, part):
    lanes = lax.broadcasted_iota(jnp.int32, shape, 1)
    return (lanes // HEAD) == part


def pick(value, part):
    return jnp.where(lane_keep(value.shape, part), value, jnp.zeros_like(value))


def merge(first, second):
    return jnp.where(lane_keep(first.shape, 0), first, second)


CHUNK = 128
STEPS = 4
SUB = 32


def natural(core, step):
    return 256 * (core + 2 * (step // 2)) + 128 * (step % 2)


def middle_kernel(
    dp, x_full, self_mix, out_grad, wo_h, wcq_h, wco_h, wup_h, wdn_h,
    ck_ref, cv_ref, bias_ref, cg_ref, cs_ref, mg_ref, ms_ref,
    smg_out, sb_out, act_out, dup_out, ddn_out, dcq_out, dco_out, dck_out, dcv_out, parts_out, resid_out, ac_out,
    wo, wcq, wco, wup, wdn, smix, og, xr, h1, h2, acc, g2, nf, act, pg, cq, cmix, cqg,
    rr, yr, sst, yst, pbuf, dkv, smg, upst, dnst, dco, dcq, parts,
    load_sem, cs_sem, cr_sem, ns_sem, nr_sem, ys_sem, yr_sem, out_sem,
):
    span = 1024 // dp
    per = 256 // span
    rank = lax.axis_index("tp")
    core = lax.rem(rank, 2)
    chip = rank // 2
    pal = rank + 1 - 2 * core
    far = lax.rem(rank + 2, 4)
    barrier = pltpu.get_barrier_semaphore()
    for peer in (pal, far):
        pl.semaphore_signal(barrier, inc=1, device_id={"tp": peer}, device_id_type=MESH)

    loads = []

    def load(src, dst):
        copy = pltpu.make_async_copy(src, dst, load_sem.at[len(loads)])
        copy.start()
        loads.append(copy)

    for k in range(STEPS):
        for c in range(2):
            load(self_mix.at[pl.ds(natural(c, k), CHUNK)], smix.at[pl.ds(k * 256 + c * 128, CHUNK)])
    load(wo_h, wo)
    n_first = len(loads)
    for k in range(STEPS):
        start = pl.multiple_of(256 * (core + 2 * (k // 2)) + 128 * (k % 2), 128)
        load(x_full.at[pl.ds(start, CHUNK)], xr.at[pl.ds(k * CHUNK, CHUNK)])
    load(wcq_h, wcq)
    load(wco_h, wco)
    n_second = len(loads)
    for k in range(STEPS):
        for c in range(2):
            load(out_grad.at[pl.ds(natural(c, k), CHUNK)], og.at[pl.ds(k * 256 + c * 128, CHUNK)])
    load(wup_h, wup)
    load(wdn_h, wdn)
    n_third = len(loads)

    dkv[...] = jnp.zeros_like(dkv)
    parts[...] = jnp.zeros_like(parts)

    def own(k):
        return pl.ds(pl.multiple_of(k * CHUNK, CHUNK), CHUNK)

    def pair(k):
        return pl.ds(pl.multiple_of(k * 256, 256), 256)

    def mine(k):
        return pl.ds(pl.multiple_of(k * 256 + core * CHUNK, CHUNK), CHUNK)

    def red_copy(s, k):
        return pltpu.make_async_remote_copy(
            sst.at[own(k)], rr.at[s, own(k)], cs_sem.at[s, k], cr_sem.at[s, k],
            device_id={"tp": pal}, device_id_type=MESH)

    def far_copy(s, k):
        return pltpu.make_async_remote_copy(
            yst.at[own(k)], yr.at[s, own(k)], ys_sem.at[s, k], yr_sem.at[s, k],
            device_id={"tp": far}, device_id_type=MESH)

    def norm_copy(s, k):
        return pltpu.make_async_remote_copy(
            nf.at[s, mine(k)], nf.at[s, mine(k)], ns_sem.at[s, k], nr_sem.at[s, k],
            device_id={"tp": pal}, device_id_type=MESH)

    def produce(s, k, columns):
        for j, value in columns:
            pbuf[:, j : j + value.shape[1]] = value
        if s > 0:
            red_copy(s - 1, k).wait_send()
        sst[own(k)] = pbuf[pl.ds(pl.multiple_of((1 - core) * CHUNK, CHUNK), CHUNK), :].astype(BF16)
        red_copy(s, k).start()
        acc[own(k)] = pbuf[pl.ds(pl.multiple_of(core * CHUNK, CHUNK), CHUNK), :]

    def finish(s, k):
        if s > 0:
            far_copy(s - 1, k).wait_send()
        red_copy(s, k).wait_recv()
        total = acc[own(k)] + rr[s, own(k)].astype(F32)
        acc[own(k)] = total
        yst[own(k)] = total.astype(BF16)
        far_copy(s, k).start()

    def sub(k, r):
        return pl.ds(pl.multiple_of(k * CHUNK + r * SUB, SUB), SUB)

    def msub(k, r):
        return pl.ds(pl.multiple_of(k * 256 + core * CHUNK + r * SUB, SUB), SUB)

    for copy in loads[:n_first]:
        copy.wait()
    pl.semaphore_wait(barrier, 2)

    @pl.loop(0, STEPS)
    def _(k):
        rows = smix[pair(k), :]
        produce(0, k, [(j, nn(rows, wo[:, j : j + 512])) for j in (0, 512)])

        @pl.when(k > 0)
        def _():
            finish(0, k - 1)

    finish(0, STEPS - 1)
    for copy in loads[n_first:n_second]:
        copy.wait()

    scale = HEAD ** (-0.5)

    def act_copy(k):
        return pltpu.make_async_copy(act.at[pair(k)], act_out.at[pair(k)], out_sem.at[2 + k])

    def place(src, dst, k, c, slot):
        start = pl.multiple_of(256 * (c + 2 * (k // 2)) + 128 * (k % 2), 128)
        return pltpu.make_async_copy(
            src.at[pl.ds(pl.multiple_of(k * 256 + c * CHUNK, CHUNK), CHUNK)],
            dst.at[pl.ds(start, CHUNK)], out_sem.at[slot + 2 * k + c])

    @pl.loop(0, STEPS)
    def _(k):
        far_copy(0, k).wait_recv()
        for r in range(CHUNK // SUB):
            hidden = xr[sub(k, r)].astype(F32) + acc[sub(k, r)] + yr[0, sub(k, r)].astype(F32)
            h1[sub(k, r)] = hidden
            xhat, _ = norm_stats(hidden)
            nf[0, msub(k, r)] = (xhat * cg_ref[...] + cs_ref[...]).astype(BF16)
        norm_copy(0, k).start()

        @pl.when(k > 0)
        def _():
            finish(1, k - 1)

        norm_copy(0, k).wait_recv()
        cq[pair(k)] = nn(nf[0, pair(k)], wcq[...]).astype(BF16)
        for slab in range(2):
            lanes = slice(slab * 128, slab * 128 + 128)
            query = cq[pair(k), lanes]
            key, value = ck_ref[:, lanes], cv_ref[:, lanes]
            mixed = []
            for part in range(2):
                scores = nt(pick(query, part), key) * scale + bias_ref[...]
                shifted = jnp.exp(scores - jnp.max(scores, axis=-1, keepdims=True))
                probs = shifted / jnp.sum(shifted, axis=-1, keepdims=True)
                mixed.append(nn(probs.astype(BF16), value))
            cmix[pair(k), lanes] = merge(*mixed).astype(BF16)
        rows = cmix[pair(k), :]
        produce(1, k, [(j, nn(rows, wco[:, j : j + 512])) for j in (0, 512)])

    finish(1, STEPS - 1)
    for copy in loads[n_second:n_third]:
        copy.wait()

    @pl.loop(0, STEPS)
    def _(k):
        far_copy(1, k).wait_recv()
        for r in range(CHUNK // SUB):
            hidden = h1[sub(k, r)] + acc[sub(k, r)] + yr[1, sub(k, r)].astype(F32)
            h2[sub(k, r)] = hidden
            xhat, _ = norm_stats(hidden)
            nf[1, msub(k, r)] = (xhat * mg_ref[...] + ms_ref[...]).astype(BF16)
        norm_copy(1, k).start()

        @pl.when(k > 0)
        def _():
            finish(2, k - 1)

        norm_copy(1, k).wait_recv()
        rows = nf[1, pair(k)]
        grads = og[pair(k), :]
        for j in range(0, 1024, 256):
            cols = slice(j, j + 256)
            pre = nn(rows, wup[:, cols])
            back = nt(grads, wdn[cols, :])
            square = pre * pre
            bend = jnp.tanh(0.7978845608028654 * pre * (1.0 + 0.044715 * square))
            half = 0.5 * (1.0 + bend)
            act[pair(k), cols] = (pre * half).astype(BF16)
            slope = half + 0.5 * pre * (1.0 - bend * bend) * (
                0.7978845608028654 * (1.0 + 3 * 0.044715 * square))
            pg[pair(k), cols] = (back * slope).astype(BF16)
        rows = pg[pair(k), :]
        produce(2, k, [(j, nt(rows, wup[j : j + 256, :])) for j in range(0, 1024, 256)])
        act_copy(k).start()

    finish(2, STEPS - 1)

    def dup_copy(k):
        return pltpu.make_async_copy(upst, dup_out.at[pl.ds(k * per, per)], out_sem.at[0])

    def ddn_copy(k):
        return pltpu.make_async_copy(dnst, ddn_out.at[pl.ds(k * per, per)], out_sem.at[1])

    def own_rows(k):
        return jnp.where(k // 2 == chip, 1.0, 0.0)

    @pl.loop(0, STEPS)
    def _(k):
        @pl.when(k > 0)
        def _():
            dup_copy(k - 1).wait()
            ddn_copy(k - 1).wait()

        at = pl.multiple_of(k * 256, 256)
        value = tn(nf[1, :, pl.ds(at, 256)], pg[...]).astype(BF16)
        for u in range(per):
            upst[u, 0] = value[u * span : u * span + span // 2]
            upst[u, 1] = value[u * span + span // 2 : (u + 1) * span]
        dup_copy(k).start()
        grads = og[:, pl.ds(at, 256)]
        for j in range(0, 1024, 256):
            value = tn(act[:, j : j + 256], grads).astype(BF16)
            for u in range(per):
                dnst[u, j // 512, j % 512 : j % 512 + 256] = value[:, u * span : (u + 1) * span]
        ddn_copy(k).start()
        far_copy(2, k).wait_recv()
        keep = own_rows(k)
        for r in range(CHUNK // SUB):
            third = acc[sub(k, r)] + yr[2, sub(k, r)].astype(F32)
            xhat, rstd = norm_stats(h2[sub(k, r)])
            parts[2] += fold_rows(third * xhat) * keep
            parts[3] += fold_rows(third) * keep
            resid = og[msub(k, r)].astype(F32) + norm_input_grad(xhat, rstd, mg_ref[...], third)
            g2[sub(k, r)] = resid
            nf[2, msub(k, r)] = resid.astype(BF16)
        norm_copy(2, k).start()

        @pl.when(k > 0)
        def _():
            finish(3, k - 1)

        norm_copy(2, k).wait_recv()
        mix_grad = nt(nf[2, pair(k)], wco[...]).astype(BF16)
        for slab in range(2):
            lanes = slice(slab * 128, slab * 128 + 128)
            query = cq[pair(k), lanes]
            grad = mix_grad[:, lanes]
            key, value = ck_ref[:, lanes], cv_ref[:, lanes]
            moved = []
            for part in range(2):
                one_q, one_g = pick(query, part), pick(grad, part)
                scores = nt(one_q, key) * scale + bias_ref[...]
                shifted = jnp.exp(scores - jnp.max(scores, axis=-1, keepdims=True))
                probs = shifted / jnp.sum(shifted, axis=-1, keepdims=True)
                prob_grad = nt(one_g, value)
                inner = jnp.sum(probs * prob_grad, axis=-1, keepdims=True)
                score_grad = (probs * (prob_grad - inner)).astype(BF16)
                moved.append(nn(score_grad, key) * scale)
                dkv[0, :, lanes] += tn(score_grad, one_q)
                dkv[1, :, lanes] += tn(probs.astype(BF16), one_g)
            cqg[pair(k), lanes] = merge(*moved).astype(BF16)
        rows = cqg[pair(k), :]
        produce(3, k, [(j, nt(rows, wcq[j : j + 512, :])) for j in (0, 512)])

    finish(3, STEPS - 1)
    for copy in (dup_copy(STEPS - 1), ddn_copy(STEPS - 1)):
        copy.wait()

    @pl.loop(0, STEPS)
    def _(k):
        at = pl.multiple_of(k * 256, 256)
        value = tn(nf[0, :, pl.ds(at, 256)], cqg[...]).astype(BF16)
        for u in range(per):
            dcq[k * per + u, 0] = value[u * span : u * span + span // 2]
            dcq[k * per + u, 1] = value[u * span + span // 2 : (u + 1) * span]
        value = tn(cmix[...], nf[2, :, pl.ds(at, 256)]).astype(BF16)
        for u in range(per):
            dco[k * per + u, 0] = value[:128, u * span : (u + 1) * span]
            dco[k * per + u, 1] = value[128:, u * span : (u + 1) * span]
        far_copy(3, k).wait_recv()
        keep = own_rows(k)
        for r in range(CHUNK // SUB):
            second = acc[sub(k, r)] + yr[3, sub(k, r)].astype(F32)
            xhat, rstd = norm_stats(h1[sub(k, r)])
            parts[0] += fold_rows(second * xhat) * keep
            parts[1] += fold_rows(second) * keep
            resid = g2[sub(k, r)] + norm_input_grad(xhat, rstd, cg_ref[...], second)
            g2[sub(k, r)] = resid
            nf[3, msub(k, r)] = resid.astype(BF16)
        norm_copy(3, k).start()
        norm_copy(3, k).wait_recv()
        smg[pair(k)] = nt(nf[3, pair(k)], wo[...]).astype(BF16)
        for c in range(2):
            place(smg, smg_out, k, c, 10).start()
            place(nf.at[3], sb_out, k, c, 18).start()

    mine_rows = pl.ds(pl.multiple_of(chip * 256, 256), 256)
    final = [
        pltpu.make_async_copy(g2.at[mine_rows], resid_out, out_sem.at[26]),
        pltpu.make_async_copy(h2.at[mine_rows], ac_out, out_sem.at[27]),
        pltpu.make_async_copy(dcq, dcq_out, out_sem.at[28]),
        pltpu.make_async_copy(dco, dco_out, out_sem.at[29]),
    ]
    for copy in final:
        copy.start()
    dck_out[...] = (dkv[0] * scale).astype(BF16)
    dcv_out[...] = dkv[1].astype(BF16)
    parts_out[...] = parts[...]
    for k in range(STEPS):
        red_copy(3, k).wait_send()
        far_copy(3, k).wait_send()
        for s in range(4):
            norm_copy(s, k).wait_send()
        act_copy(k).wait()
        for c in range(2):
            place(smg, smg_out, k, c, 10).wait()
            place(nf.at[3], sb_out, k, c, 18).wait()
    for copy in final:
        copy.wait()


def middle(dp, x_full, self_mix, out_grad, wo, wcq, wco, wup, wdn, ck, cv, bias, gains):
    full = jax.ShapeDtypeStruct((1024, 1024), BF16)
    narrow = jax.ShapeDtypeStruct((1024, 256), BF16)
    short = jax.ShapeDtypeStruct((128, 256), BF16)
    block = jax.ShapeDtypeStruct((256, 1024), F32)
    part = 1024 // dp
    per = 256 // part
    pieces = [(part // 2, 1024), (512, part), (part // 2, 256), (128, part)]
    outs = [
        narrow, full, full] + [jax.ShapeDtypeStruct((dp, 2) + s, BF16) for s in pieces] + [short, short,
        jax.ShapeDtypeStruct((4, 8, 1024), F32), block, block,
    ]
    out_specs = [ANY] * 7 + [VM] * 3 + [ANY] * 2
    vm = pltpu.VMEM
    dma = pltpu.SemaphoreType.DMA
    scratch = [
        vm((256, 1024), BF16), vm((1024, 256), BF16), vm((256, 1024), BF16), vm((1024, 1024), BF16),
        vm((1024, 1024), BF16), vm((1024, 256), BF16), vm((1024, 1024), BF16), vm((512, 1024), BF16),
        vm((512, 1024), F32), vm((512, 1024), F32), vm((512, 1024), F32), vm((512, 1024), F32),
        vm((4, 1024, 1024), BF16), vm((1024, 1024), BF16), vm((1024, 1024), BF16),
        vm((1024, 256), BF16), vm((1024, 256), BF16), vm((1024, 256), BF16),
        vm((4, 512, 1024), BF16), vm((4, 512, 1024), BF16), vm((512, 1024), BF16), vm((512, 1024), BF16),
        vm((256, 1024), F32), vm((2, 128, 256), F32), vm((1024, 256), BF16),
        *[vm((per, 2) + s, BF16) for s in pieces[:2]], vm((dp, 2) + pieces[3], BF16), vm((dp, 2) + pieces[2], BF16),
        vm((4, 8, 1024), F32),
        dma((32,)), dma((4, 4)), dma((4, 4)), dma((4, 4)), dma((4, 4)), dma((4, 4)), dma((4, 4)), dma((32,)),
    ]
    return pl.pallas_call(
        functools.partial(middle_kernel, dp),
        out_shape=outs,
        in_specs=[ANY] * 8 + [VM] * 7,
        out_specs=out_specs,
        scratch_shapes=scratch,
        name="middle",
        compiler_params=pltpu.CompilerParams(
            collective_id=1, has_side_effects=True, vmem_limit_bytes=GRANT),
    )(x_full, self_mix, out_grad, wo, wcq, wco, wup, wdn, ck, cv, bias, *gains)


def front_kernel(
    x_own, wq_h, wk_h, wv_h, text_h, wck_h, wcv_h, ag_ref, as_ref,
    x_out, n1_out, q_out, k_out, v_out, mix_out, p0_out, p1_out, p2_out, p3_out, ck_out, cv_out,
    xf, n1, q, k, v, mix, p0, p1, p2, p3, wq, wk, wv, text, wck, wcv,
    load_sem, y_s, y_r, c_s, c_r, f_s, f_r, out_sem,
):
    rank = lax.axis_index("tp")
    core = lax.rem(rank, 2)
    pal = rank + 1 - 2 * core
    far = lax.rem(rank + 2, 4)
    beyond = lax.rem(pal + 2, 4)
    barrier = pltpu.get_barrier_semaphore()
    for peer in (pal, far):
        pl.semaphore_signal(barrier, inc=1, device_id={"tp": peer}, device_id_type=MESH)
    loads = [
        pltpu.make_async_copy(src, dst, load_sem.at[i])
        for i, (src, dst) in enumerate([
            (x_own, xf.at[pl.ds(pl.multiple_of(rank * 256, 256), 256)]),
            (text_h, text), (wck_h, wck), (wcv_h, wcv), (wq_h, wq), (wk_h, wk), (wv_h, wv)])
    ]
    for copy in loads:
        copy.start()

    def part(block, i, size):
        return pl.ds(pl.multiple_of(block * 256 + i * size, size), size)

    across = [
        pltpu.make_async_remote_copy(
            x_own.at[pl.ds(i * 64, 64)], xf.at[part(rank, i, 64)], y_s.at[i], y_r.at[i],
            device_id={"tp": far}, device_id_type=MESH)
        for i in range(4)
    ]
    beside = pltpu.make_async_remote_copy(
        x_own, xf.at[part(rank, 0, 256)], c_s.at[0], c_r.at[0], device_id={"tp": pal}, device_id_type=MESH)
    onward = [
        pltpu.make_async_remote_copy(
            xf.at[part(far, i, 64)], xf.at[part(far, i, 64)], f_s.at[i], f_r.at[i],
            device_id={"tp": pal}, device_id_type=MESH)
        for i in range(4)
    ]
    pl.semaphore_wait(barrier, 2)
    for copy in across:
        copy.start()
    beside.start()

    for copy in loads[1:4]:
        copy.wait()
    ck_out[...] = nn(text[...], wck[...]).astype(BF16)
    cv_out[...] = nn(text[...], wcv[...]).astype(BF16)
    for copy in loads[4:] + loads[:1]:
        copy.wait()

    def project(block, i):
        for r in range(4):
            rows = pl.ds(pl.multiple_of(block * 256 + i * 128 + r * 32, 32), 32)
            xhat, _ = norm_stats(xf[rows].astype(F32))
            n1[rows] = (xhat * ag_ref[...] + as_ref[...]).astype(BF16)
        rows = part(block, i, 128)
        value = n1[rows]
        q[rows] = (nn(value, wq[...]).astype(BF16) * 0.125).astype(BF16)
        k[rows] = nn(value, wk[...]).astype(BF16)
        v[rows] = nn(value, wv[...]).astype(BF16)

    def both(block):
        @pl.loop(0, 2)
        def _(i):
            project(block, i)

    both(rank)
    beside.wait_recv()
    both(pal)
    for half in range(2):
        for i in (2 * half, 2 * half + 1):
            across[i].wait_recv()
            onward[i].start()
        project(far, half)
        for i in (2 * half, 2 * half + 1):
            onward[i].wait_recv()
        project(beyond, half)
    outs = [
        pltpu.make_async_copy(src, dst, out_sem.at[i])
        for i, (src, dst) in enumerate([(xf, x_out), (n1, n1_out), (q, q_out), (k, k_out), (v, v_out)])
    ]
    for copy in outs:
        copy.start()

    kept = (p0, p1, p2, p3)
    below = lax.broadcasted_iota(jnp.int32, (256, 256), 0) >= lax.broadcasted_iota(jnp.int32, (256, 256), 1)

    @pl.loop(0, 2)
    def _(slab):
        lanes = pl.ds(pl.multiple_of(slab * 128, 128), 128)
        for i in range(4):
            done, end = i * 256, i * 256 + 256
            query = q[done:end, lanes]
            mixed = []
            for half in range(2):
                one = pick(query, half)
                diag = jnp.where(below, nt(one, k[done:end, lanes]), MASKED)
                peak = jnp.max(diag, axis=-1, keepdims=True)
                if i:
                    past = nt(one, k[0:done, lanes])
                    peak = jnp.maximum(peak, jnp.max(past, axis=-1, keepdims=True))
                    past = jnp.exp(past - peak)
                diag = jnp.exp(diag - peak)
                total = jnp.sum(diag, axis=-1, keepdims=True)
                if i:
                    total = total + jnp.sum(past, axis=-1, keepdims=True)
                inverse = 1.0 / total
                probs = (diag * inverse).astype(BF16)
                kept[i][slab * 2 + half, :, done:end] = probs
                out = nn(probs, v[done:end, lanes])
                if i:
                    probs = (past * inverse).astype(BF16)
                    kept[i][slab * 2 + half, :, 0:done] = probs
                    out = out + nn(probs, v[0:done, lanes])
                mixed.append(out)
            mix[done:end, lanes] = merge(*mixed).astype(BF16)

    tail = [
        pltpu.make_async_copy(src, dst, out_sem.at[5 + i])
        for i, (src, dst) in enumerate(
            [(mix, mix_out), (p0, p0_out), (p1, p1_out), (p2, p2_out), (p3, p3_out)])
    ]
    for copy in tail:
        copy.start()
    for copy in across + [beside] + onward:
        copy.wait_send()
    for copy in outs + tail:
        copy.wait()


def front(x_own, wq, wk, wv, text, wck, wcv, gains):
    full = ((1024, 1024), BF16)
    narrow = ((1024, 256), BF16)
    short = ((128, 256), BF16)
    probs = [((4, 256, 256 * (i + 1)), BF16) for i in range(4)]
    vm = pltpu.VMEM
    dma = pltpu.SemaphoreType.DMA
    return pl.pallas_call(
        front_kernel,
        out_shape=[jax.ShapeDtypeStruct(*item) for item in [full, full, narrow, narrow, narrow, narrow] + probs + [short, short]],
        in_specs=[ANY] * 7 + [VM] * 2,
        out_specs=[ANY] * 10 + [VM] * 2,
        scratch_shapes=[vm(*item) for item in [full, full, narrow, narrow, narrow, narrow] + probs
                        + [narrow] * 3 + [((128, 1024), BF16), narrow, narrow]]
        + [dma((8,)), dma((4,)), dma((4,)), dma((1,)), dma((1,)), dma((4,)), dma((4,)), dma((12,))],
        name="front",
        compiler_params=pltpu.CompilerParams(
            collective_id=2, has_side_effects=True, vmem_limit_bytes=GRANT),
    )(x_own, wq, wk, wv, text, wck, wcv, *gains)


class Reduce:
    def __init__(self, number, source, own, x_buf, z_buf, out, sems, place):
        self.source, self.own, self.x_buf, self.z_buf, self.out = source, own, x_buf, z_buf, out
        self.group, self.depth, self.size = place
        xs, xr, zs, zr, gs, gr = sems
        other = 1 - self.group
        self.x_copy = pltpu.make_async_remote_copy(
            source.at[:, other], x_buf, xs.at[number], xr.at[number],
            device_id={"grp": other}, device_id_type=MESH)
        self.z_copies = [
            pltpu.make_async_remote_copy(
                x_buf.at[lax.rem(self.depth + r, self.size)], z_buf.at[r - 1],
                zs.at[number, r - 1], zr.at[number, r - 1],
                device_id={"dp": lax.rem(self.depth + r, self.size)}, device_id_type=MESH)
            for r in range(1, self.size)
        ]
        self.g_copy = pltpu.make_async_remote_copy(
            out.at[self.group], out.at[self.group], gs.at[number], gr.at[number],
            device_id={"grp": other}, device_id_type=MESH)

    def start(self):
        self.x_copy.start()

    def add(self):
        self.x_copy.wait_recv()

        @pl.loop(0, self.size)
        def _(d):
            mine = self.own[d] if self.own is not None else self.source[d, self.group]
            self.x_buf[d] = (self.x_buf[d].astype(F32) + mine.astype(F32)).astype(BF16)

        for copy in self.z_copies:
            copy.start()

    def total(self):
        for copy in self.z_copies:
            copy.wait_recv()
        total = self.x_buf[self.depth].astype(F32)
        for r in range(self.size - 1):
            total = total + self.z_buf[r].astype(F32)
        self.out[self.group] = total.astype(BF16)
        self.g_copy.start()

    def end(self):
        self.x_copy.wait_send()
        for copy in self.z_copies:
            copy.wait_send()
        self.g_copy.wait()


def back_kernel(dp, *refs):
    (smix_h, sb_h, act_h, wdn_h, smg_h, q_h, k_h, v_h, p0_h, p1_h, p2_h, p3_h, n1_h, wq_h, wk_h, wv_h,
     x_own, resid_h, ac_h, dup_h, ddn_h, dcq_h, dco_h, text, wck, wcv, dck, dcv, parts_in, ag_ref) = refs[:30]
    (layer_out, image_grad, text_out, norm_out, up_o, dn_o, cq_o, co_o, ck_o, cv_o, so_o, sq_o, sk_o, sv_o) = refs[30:44]
    (smix, sb, act, wdn, smg, q, k, v, p0, p1, p2, p3, n1, wq, wk, wv, xo, resid, ac,
     up_y, dn_y, cq_y, co_y, ck_g, cv_g, so_g, sq_g, sk_g, sv_g) = refs[44:73]
    x_bufs, z_bufs = refs[73:83], refs[83:93]
    (dq, dk, dv, dkv, acc, sst, rr, yst, yr, tpart, t_st, t_rr, t_yst, t_yr, t_fin, npart, n_tp, nsum, n_all) = refs[93:112]
    (load_sem, xs, xr, zs, zr, gs, gr, cs_sem, cr_sem, ys_sem, yr_sem, t_s, t_r, n_s, n_r, m_s, m_r) = refs[112:]

    rank = lax.axis_index("tp")
    group = lax.axis_index("grp")
    depth = lax.axis_index("dp")
    core = lax.rem(rank, 2)
    chip = rank // 2
    pal = rank + 1 - 2 * core
    far = lax.rem(rank + 2, 4)
    others = [(g, r) for g in range(2) for r in range(dp) if g or r]
    barrier = pltpu.get_barrier_semaphore()
    for r in range(1, 4):
        pl.semaphore_signal(barrier, inc=1, device_id={"tp": lax.rem(rank + r, 4)}, device_id_type=MESH)

    def at_other(g, r):
        return {"grp": lax.rem(group + g, 2), "dp": lax.rem(depth + r, dp)}

    for g, r in others:
        pl.semaphore_signal(barrier, inc=1, device_id=at_other(g, r), device_id_type=MESH)

    pairs = [
        (smix_h, smix), (sb_h, sb), (act_h, act), (wdn_h, wdn), (smg_h, smg), (q_h, q), (k_h, k), (v_h, v),
        (p0_h, p0), (p1_h, p1), (p2_h, p2), (p3_h, p3), (n1_h, n1), (wq_h, wq), (wk_h, wk), (wv_h, wv),
        (x_own, xo), (resid_h, resid), (ac_h, ac),
        (dup_h.at[:, group], up_y), (ddn_h.at[:, group], dn_y), (dcq_h.at[:, group], cq_y), (dco_h.at[:, group], co_y),
    ]
    loads = [pltpu.make_async_copy(src, dst, load_sem.at[i]) for i, (src, dst) in enumerate(pairs)]
    for copy in loads:
        copy.start()

    place = (group, depth, dp)
    sems = (xs, xr, zs, zr, gs, gr)
    sources = (dup_h, ddn_h, dcq_h, dco_h, ck_g, cv_g, so_g, sq_g, sk_g, sv_g)
    owns = (up_y, dn_y, cq_y, co_y) + (None,) * 6
    outs = (up_o, dn_o, cq_o, co_o, ck_o, cv_o, so_o, sq_o, sk_o, sv_o)
    pieces = [
        Reduce(i, sources[i], owns[i], x_bufs[i], z_bufs[i], outs[i], sems, place) for i in range(10)
    ]
    pl.semaphore_wait(barrier, 3 + len(others))
    for piece in pieces[:4]:
        piece.start()

    scale = HEAD ** (-0.5)
    depth_rows = 1024 // dp
    per = 256 // depth_rows

    def rows_grad(ref, left, right):
        for m in range(4):
            value = tn(left[:, m * 256 : m * 256 + 256], right[...]).astype(BF16)
            for u in range(per):
                piece = value[u * depth_rows : (u + 1) * depth_rows]
                ref[m * per + u, 0] = piece[: depth_rows // 2]
                ref[m * per + u, 1] = piece[depth_rows // 2 :]

    rows_grad(ck_g, text, dck)
    rows_grad(cv_g, text, dcv)
    pieces[4].start()
    pieces[5].start()
    tpart[...] = nt(dck[...], wck[...]) + nt(dcv[...], wcv[...])

    def t_rows(c):
        return pl.ds(pl.multiple_of(c * 64, 64), 64)

    t_st[...] = tpart[t_rows(1 - core)].astype(BF16)
    t_red = pltpu.make_async_remote_copy(
        t_st, t_rr, t_s.at[0], t_r.at[0], device_id={"tp": pal}, device_id_type=MESH)
    t_red.start()

    for copy in loads[:2]:
        copy.wait()
    for d in range(dp):
        value = tn(smix[...], sb[:, d * depth_rows : (d + 1) * depth_rows]).astype(BF16)
        so_g[d, 0] = value[:128]
        so_g[d, 1] = value[128:]
    pieces[6].start()
    t_red.wait_recv()
    t_yst[...] = (tpart[t_rows(core)] + t_rr[...].astype(F32)).astype(BF16)
    t_far = pltpu.make_async_remote_copy(
        t_yst, t_yr, t_s.at[1], t_r.at[1], device_id={"tp": far}, device_id_type=MESH)
    t_far.start()

    def own(i):
        return pl.ds(pl.multiple_of(i * CHUNK, CHUNK), CHUNK)

    class Scatter:
        def __init__(self, n):
            self.n = n

        def red(self, i):
            n = self.n
            return pltpu.make_async_remote_copy(
                sst.at[n, own(i)], rr.at[n, own(i)], cs_sem.at[n, i], cr_sem.at[n, i],
                device_id={"tp": pal}, device_id_type=MESH)

        def far(self, j):
            n = self.n
            return pltpu.make_async_remote_copy(
                yst.at[n, own(j)], yr.at[n, own(j)], ys_sem.at[n, j], yr_sem.at[n, j],
                device_id={"tp": far}, device_id_type=MESH)

        def put(self, i, theirs, ours):
            sst[self.n, own(i)] = theirs.astype(BF16)
            self.red(i).start()
            acc[self.n, own(i)] = ours

        def send(self, j):
            i = 2 * (1 - chip) + j
            self.red(i).wait_recv()
            yst[self.n, own(j)] = (acc[self.n, own(i)] + rr[self.n, own(i)].astype(F32)).astype(BF16)
            self.far(j).start()

        def keep(self, j):
            self.red(2 * chip + j).wait_recv()
            self.far(j).wait_recv()

        def value(self, j, r):
            i = 2 * chip + j
            rows = pl.ds(pl.multiple_of(i * CHUNK + r * SUB, SUB), SUB)
            near = pl.ds(j * CHUNK + r * SUB, SUB)
            return acc[self.n, rows] + rr[self.n, rows].astype(F32) + yr[self.n, near].astype(F32)

        def end(self):
            for i in range(4):
                self.red(i).wait_send()
            for j in range(2):
                self.far(j).wait_send()

    layer, first = Scatter(0), Scatter(1)
    for copy in loads[2:4]:
        copy.wait()

    def sequence(step):
        return lax.rem(2 * (1 - chip) + step, 4)

    @pl.loop(0, 4)
    def _(step):
        i = sequence(step)
        theirs = act[pl.ds(pl.multiple_of(i * 256 + (1 - core) * CHUNK, CHUNK), CHUNK), :]
        ours = act[pl.ds(pl.multiple_of(i * 256 + core * CHUNK, CHUNK), CHUNK), :]
        layer.put(i, nn(theirs, wdn[...]), nn(ours, wdn[...]))

        @pl.when((step > 0) & (step < 3))
        def _():
            layer.send(step - 1)

    for copy in loads[4:12]:
        copy.wait()
    dkv[...] = jnp.zeros_like(dkv)
    kept = (p0, p1, p2, p3)

    @pl.loop(0, 2)
    def _(slab):
        lanes = pl.ds(pl.multiple_of(slab * 128, 128), 128)
        for i in range(4):
            begin, end = i * 256, i * 256 + 256
            query, grad = q[begin:end, lanes], smg[begin:end, lanes]
            product = grad.astype(F32) * smix[begin:end, lanes].astype(F32)
            moved = []
            for half in range(2):
                one_q, one_g = pick(query, half), pick(grad, half)
                inner = jnp.sum(pick(product, half), axis=-1, keepdims=True)
                probs = kept[i][slab * 2 + half]
                prob_grad = nt(one_g, v[0:end, lanes])
                score_grad = (probs.astype(F32) * (prob_grad - inner)).astype(BF16)
                moved.append(nn(score_grad, k[0:end, lanes]))
                dkv[0, 0:end, lanes] += tn(score_grad, one_q)
                dkv[1, 0:end, lanes] += tn(probs, one_g)
            dq[begin:end, lanes] = (merge(*moved) * scale).astype(BF16)

    dk[...] = dkv[0].astype(BF16)
    dv[...] = dkv[1].astype(BF16)

    for copy in loads[12:]:
        copy.wait()
    pieces[0].add()

    @pl.loop(0, 4)
    def _(step):
        i = sequence(step)

        def partial(c):
            start = pl.multiple_of(256 * (c + 2 * (i // 2)) + 128 * lax.rem(i, 2), 128)
            rows = pl.ds(start, CHUNK)
            return nt(dq[rows], wq[...]) + nt(dk[rows], wk[...]) + nt(dv[rows], wv[...])

        first.put(i, partial(1 - core), partial(core))

        @pl.when((step > 0) & (step < 3))
        def _():
            first.send(step - 1)

    rows_grad(sq_g, n1, dq)
    pieces[7].start()
    rows_grad(sk_g, n1, dk)
    pieces[8].start()
    rows_grad(sv_g, n1, dv)
    pieces[9].start()

    for j in range(2):
        layer.keep(j)
        for r in range(CHUNK // SUB):
            rows = slice(j * CHUNK + r * SUB, j * CHUNK + r * SUB + SUB)
            layer_out[rows] = (ac[rows] + layer.value(j, r)).astype(BF16)

    t_far.wait_recv()
    t_fin[t_rows(core)] = (t_yst[...].astype(F32) + t_yr[...].astype(F32)).astype(BF16)
    t_share = pltpu.make_async_remote_copy(
        t_fin.at[t_rows(core)], t_fin.at[t_rows(core)], t_s.at[2], t_r.at[2],
        device_id={"tp": pal}, device_id_type=MESH)
    t_share.start()

    npart[...] = jnp.zeros_like(npart)
    for j in range(2):
        first.keep(j)
        for r in range(CHUNK // SUB):
            rows = slice(j * CHUNK + r * SUB, j * CHUNK + r * SUB + SUB)
            given = first.value(j, r)
            xhat, rstd = norm_stats(xo[rows].astype(F32))
            npart[0] += fold_rows(given * xhat)
            npart[1] += fold_rows(given)
            image_grad[rows] = resid[rows] + norm_input_grad(xhat, rstd, ag_ref[...], given)

    def line(ref, i):
        return jnp.sum(ref[i], axis=0, keepdims=True)

    n_tp[rank] = jnp.concatenate(
        [line(npart, 0), line(npart, 1)] + [line(parts_in, i) for i in range(4)]
        + [jnp.zeros((2, 1024), F32)], axis=0)
    n_copies = [
        pltpu.make_async_remote_copy(
            n_tp.at[rank], n_tp.at[rank], n_s.at[r - 1], n_r.at[r - 1],
            device_id={"tp": lax.rem(rank + r, 4)}, device_id_type=MESH)
        for r in range(1, 4)
    ]
    for copy in n_copies:
        copy.start()
    pieces[1].add()
    pieces[0].total()
    for copy in n_copies:
        copy.wait_recv()
    summed = n_tp[0] + n_tp[1] + n_tp[2] + n_tp[3]
    for d in range(dp):
        nsum[d] = summed[:, d * depth_rows : (d + 1) * depth_rows]
    slot = group * dp + depth
    m_copies = [
        pltpu.make_async_remote_copy(
            nsum.at[lax.rem(depth + r, dp)], n_all.at[slot], m_s.at[i], m_r.at[i],
            device_id=at_other(g, r), device_id_type=MESH)
        for i, (g, r) in enumerate(others)
    ]
    for copy in m_copies:
        copy.start()
    n_all[slot] = nsum[depth]

    pieces[2].add()
    pieces[3].add()
    pieces[4].add()
    pieces[1].total()
    pieces[5].add()
    pieces[6].add()
    for i in range(2, 5):
        pieces[i].total()
    pieces[7].add()
    pieces[5].total()
    pieces[8].add()
    pieces[6].total()
    pieces[9].add()
    for i in range(7, 10):
        pieces[i].total()
    for copy in m_copies:
        copy.wait_recv()
    total = n_all[0]
    for i in range(1, 2 * dp):
        total = total + n_all[i]
    norm_out[...] = total
    t_share.wait_recv()
    text_out[...] = t_fin[...]
    for copy in m_copies + n_copies + [t_red, t_far, t_share]:
        copy.wait_send()
    layer.end()
    first.end()
    for piece in pieces:
        piece.end()


def piece_shapes(dp):
    part = 1024 // dp
    rows = (part // 2, 256)
    columns = (128, part)
    return [(part // 2, 1024), (512, part), rows, columns, rows, rows, columns, rows, rows, rows]


def back(dp, *operands):
    part = 1024 // dp
    full = ((1024, 1024), BF16)
    narrow = ((1024, 256), BF16)
    probs = [((4, 256, 256 * (i + 1)), BF16) for i in range(4)]
    shapes = piece_shapes(dp)
    block = ((256, 1024), F32)
    outs = [((256, 1024), BF16), block, ((128, 1024), BF16), ((8, part), F32)] + [((2,) + s, BF16) for s in shapes]
    scratch = (
        [narrow, full, full, full] + [narrow] * 4 + probs + [full] + [narrow] * 3
        + [((256, 1024), BF16), block, block]
        + [((dp,) + s, BF16) for s in shapes[:4]]
        + [((dp, 2) + s, BF16) for s in shapes[4:]]
        + [((dp,) + s, BF16) for s in shapes]
        + [((dp - 1,) + s, BF16) for s in shapes]
        + [narrow] * 3
        + [((2, 1024, 256), F32), ((2, 512, 1024), F32), ((2, 512, 1024), BF16), ((2, 512, 1024), BF16),
           ((2, 256, 1024), BF16), ((2, 256, 1024), BF16), ((128, 1024), F32),
           ((64, 1024), BF16), ((64, 1024), BF16), ((64, 1024), BF16), ((64, 1024), BF16), ((128, 1024), BF16),
           ((2, 8, 1024), F32), ((4, 8, 1024), F32), ((dp, 8, part), F32), ((2 * dp, 8, part), F32)]
    )
    dma = pltpu.SemaphoreType.DMA
    many = 2 * dp - 1
    sems = [dma((24,)), dma((10,)), dma((10,)), dma((10, dp - 1)), dma((10, dp - 1)), dma((10,)), dma((10,)),
            dma((2, 4)), dma((2, 4)), dma((2, 2)), dma((2, 2)), dma((3,)), dma((3,)), dma((3,)), dma((3,)),
            dma((many,)), dma((many,))]
    return pl.pallas_call(
        functools.partial(back_kernel, dp),
        out_shape=[jax.ShapeDtypeStruct(*item) for item in outs],
        in_specs=[ANY] * 23 + [VM] * 7,
        out_specs=[VM] * len(outs),
        scratch_shapes=[pltpu.VMEM(*item) for item in scratch] + sems,
        name="back",
        compiler_params=pltpu.CompilerParams(
            collective_id=3, has_side_effects=True, vmem_limit_bytes=GRANT),
    )(*operands)


def emit_kernel(n, *refs):
    for given, out in zip(refs[:n], refs[n:]):
        if len(given.shape) == 3:
            rows = given.shape[1]
            out[0:rows] = given[0].astype(F32)
            out[rows : 2 * rows] = given[1].astype(F32)
        else:
            out[...] = given[...].astype(out.dtype)


def emit(arrays):
    outs = []
    for i, item in enumerate(arrays):
        if len(item.shape) == 3:
            outs.append(jax.ShapeDtypeStruct((2 * item.shape[1], item.shape[2]), F32))
        else:
            outs.append(jax.ShapeDtypeStruct(item.shape, BF16 if i == 0 else F32))
    return pl.pallas_call(
        functools.partial(emit_kernel, len(arrays)),
        out_shape=outs,
        in_specs=[VM] * len(arrays),
        out_specs=[VM] * len(arrays),
        name="emit",
        compiler_params=pltpu.CompilerParams(vmem_limit_bytes=GRANT),
    )(*arrays)


def local(
    dp,
    image_rows,
    text_states,
    caption_lengths,
    out_grad,
    self_query,
    self_key,
    self_value,
    self_output,
    cross_query,
    cross_key,
    cross_value,
    cross_output,
    mlp_up,
    mlp_down,
    attn_gain,
    attn_shift,
    cross_gain,
    cross_shift,
    mlp_gain,
    mlp_shift,
):
    text = text_states[0]
    bias = jnp.where(jnp.arange(TEXT)[None, :] < caption_lengths[0], 0.0, MASKED)
    x_full, norm_one, q, k, v, self_mix, p0, p1, p2, p3, cross_k, cross_v = front(
        image_rows, self_query, self_key, self_value, text, cross_key, cross_value,
        [attn_gain[None, :], attn_shift[None, :]])
    gains = [item[None, :] for item in (cross_gain, cross_shift, mlp_gain, mlp_shift)]
    mix_grad, self_back, activated, up, down, c_query, c_output, k_grad, v_grad, parts, resid, after_cross = middle(
        dp, x_full, self_mix, out_grad, self_output, cross_query, cross_output, mlp_up, mlp_down,
        cross_k, cross_v, bias, gains)
    layer_out, image_grad, text_grad, norms, *grads = back(
        dp, self_mix, self_back, activated, mlp_down, mix_grad, q, k, v, p0, p1, p2, p3, norm_one,
        self_query, self_key, self_value, image_rows, resid, after_cross, up, down, c_query, c_output,
        text, cross_key, cross_value, k_grad, v_grad, parts, attn_gain[None, :])
    layer_out, image_grad, text_grad, norms, up, down, cq, co, ck, cv, so, sq, sk, sv = emit(
        [layer_out, image_grad, text_grad, norms, *grads])
    return (
        layer_out, image_grad, text_grad[None], sq, sk, sv, so, cq, ck, cv, co, up, down,
        norms[0], norms[1], norms[2], norms[3], norms[4], norms[5])


def solution(mesh):
    placed = (
        P(("grp", "dp", "tp"), None),
        P(("grp", "dp"), None, None),
        P(("grp", "dp")),
        P(("grp", "dp"), None),
        P(None, "tp"),
        P(None, "tp"),
        P(None, "tp"),
        P("tp", None),
        P(None, "tp"),
        P(None, "tp"),
        P(None, "tp"),
        P("tp", None),
        P(None, "tp"),
        P("tp", None),
        P(),
        P(),
        P(),
        P(),
        P(),
        P(),
    )
    return jax.shard_map(
        functools.partial(local, mesh.shape["dp"]),
        mesh=mesh,
        in_specs=placed,
        out_specs=(
            P(("grp", "dp", "tp"), None),
            P(("grp", "dp", "tp"), None),
            P(("grp", "dp"), None, None),
            P("dp", "tp"),
            P("dp", "tp"),
            P("dp", "tp"),
            P("tp", "dp"),
            P("dp", "tp"),
            P("dp", "tp"),
            P("dp", "tp"),
            P("tp", "dp"),
            P("dp", "tp"),
            P("tp", "dp"),
            P("dp"),
            P("dp"),
            P("dp"),
            P("dp"),
            P("dp"),
            P("dp"),
        ),
        check_vma=False,
    )
```

```python
import functools

import jax
import jax.numpy as jnp
from jax import lax
from jax.experimental import pallas as pl
from jax.experimental.pallas import tpu as pltpu
from jax.sharding import PartitionSpec as P

HEAD = 64
TEXT = 128
EPSILON = 1e-05
MASKED = -1e30
MESH = pl.DeviceIdType.MESH
F32 = jnp.float32
BF16 = jnp.bfloat16
ANY = pl.BlockSpec(memory_space=pl.ANY)
VM = pl.BlockSpec(memory_space=pltpu.VMEM)
GRANT = 60 * 1024 * 1024


def nn(left, right):
    return lax.dot_general(left, right, (((1,), (0,)), ((), ())), preferred_element_type=F32)


def nt(left, right):
    return lax.dot_general(left, right, (((1,), (1,)), ((), ())), preferred_element_type=F32)


def tn(left, right):
    return lax.dot_general(left, right, (((0,), (0,)), ((), ())), preferred_element_type=F32)


def norm_stats(hidden):
    middle = jnp.mean(hidden, axis=-1, keepdims=True)
    centred = hidden - middle
    spread = jnp.mean(centred * centred, axis=-1, keepdims=True)
    rstd = lax.rsqrt(spread + EPSILON)
    return centred * rstd, rstd


def norm_input_grad(xhat, rstd, gain, cotangent):
    scaled = cotangent * gain
    first = jnp.mean(scaled, axis=-1, keepdims=True)
    second = jnp.mean(scaled * xhat, axis=-1, keepdims=True)
    return (scaled - first - xhat * second) * rstd


def fold_rows(value):
    rows = value.shape[0]
    total = value[0:8]
    for start in range(8, rows, 8):
        total = total + value[start : start + 8]
    return total


def lane_keep(shape, part):
    lanes = lax.broadcasted_iota(jnp.int32, shape, 1)
    return (lanes // HEAD) == part


def pick(value, part):
    return jnp.where(lane_keep(value.shape, part), value, jnp.zeros_like(value))


def merge(first, second):
    return jnp.where(lane_keep(first.shape, 0), first, second)


class Piece:
    def __init__(self, place, source, x_buf, z_buf, x_sems, z_sems):
        self.place, self.source, self.x_buf, self.z_buf = place, source, x_buf, z_buf
        self.x_sems, self.z_sems = x_sems, z_sems

    def x_copy(self):
        other = 1 - self.place[0]
        return pltpu.make_async_remote_copy(
            self.source.at[:, other], self.x_buf, *self.x_sems,
            device_id={"grp": other}, device_id_type=MESH)

    def z_copies(self):
        _, depth, size = self.place
        return [
            pltpu.make_async_remote_copy(
                self.x_buf.at[lax.rem(depth + r, size)], self.z_buf.at[r - 1],
                self.z_sems[0].at[r - 1], self.z_sems[1].at[r - 1],
                device_id={"dp": lax.rem(depth + r, size)}, device_id_type=MESH)
            for r in range(1, size)
        ]

    def start(self):
        self.x_copy().start()

    def add(self, own=None):
        self.x_copy().wait_recv()

        @pl.loop(0, self.place[2])
        def _(d):
            mine = own[d] if own is not None else self.source[d, self.place[0]]
            self.x_buf[d] = (self.x_buf[d].astype(F32) + mine.astype(F32)).astype(BF16)

    def spread(self):
        for copy in self.z_copies():
            copy.start()

    def total(self):
        for copy in self.z_copies():
            copy.wait_recv()
        total = self.x_buf[self.place[1]].astype(F32)
        for r in range(self.place[2] - 1):
            total = total + self.z_buf[r].astype(F32)
        return total.astype(BF16)

    def x_end(self):
        self.x_copy().wait_send()

    def z_end(self):
        for copy in self.z_copies():
            copy.wait_send()


class Across:
    def __init__(self, place, source, z_buf, sums, theirs, out, z_sems, g_sems):
        group, depth, size = place
        self.place, self.source, self.z_buf, self.sums, self.theirs, self.out = place, source, z_buf, sums, theirs, out
        self.z_copies = [
            pltpu.make_async_remote_copy(
                source.at[lax.rem(depth + r, size)], z_buf.at[r - 1], z_sems[0].at[r - 1], z_sems[1].at[r - 1],
                device_id={"dp": lax.rem(depth + r, size)}, device_id_type=MESH)
            for r in range(1, size)
        ]
        self.g_copy = pltpu.make_async_remote_copy(
            sums, theirs, *g_sems, device_id={"grp": 1 - group}, device_id_type=MESH)

    def start(self):
        for copy in self.z_copies:
            copy.start()

    def total(self):
        for copy in self.z_copies:
            copy.wait_recv()
        total = self.source[self.place[1]].astype(F32)
        for r in range(self.place[2] - 1):
            total = total + self.z_buf[r].astype(F32)
        self.sums[...] = total.astype(BF16)
        self.g_copy.start()

    def end(self):
        self.g_copy.wait_recv()
        self.out[...] = (self.sums[...].astype(F32) + self.theirs[...].astype(F32)).astype(BF16)
        self.g_copy.wait_send()
        for copy in self.z_copies:
            copy.wait_send()


CHUNK = 128
STEPS = 4
SUB = 32


def natural(core, step):
    return 256 * (core + 2 * (step // 2)) + 128 * (step % 2)


def middle_kernel(
    dp, x_full, self_mix, out_grad, wo_h, wcq_h, wco_h, wup_h, wdn_h,
    ck_ref, cv_ref, bias_ref, cg_ref, cs_ref, mg_ref, ms_ref,
    smg_out, sb_out, act_out, uf_out, df_out, ul_out, dl_out, dcq_out, dco_out, dck_out, dcv_out, parts_out, resid_out, ac_out,
    wo, wcq, wco, wup, wdn, smix, og, xr, h1, h2, acc, g2, nf, act, pg, cq, cmix, cqg,
    rr, yr, sst, yst, pbuf, dkv, smg, ug, dg, ux, dx, uz, dz, uf, df, dco, dcq, parts,
    load_sem, cs_sem, cr_sem, ns_sem, nr_sem, ys_sem, yr_sem, xs_sem, xr_sem, zs_sem, zr_sem, out_sem,
):
    span = 1024 // dp
    per = 256 // span
    rank = lax.axis_index("tp")
    core = lax.rem(rank, 2)
    chip = rank // 2
    pal = rank + 1 - 2 * core
    far = lax.rem(rank + 2, 4)
    group = lax.axis_index("grp")
    depth = lax.axis_index("dp")
    place = (group, depth, dp)
    barrier = pltpu.get_barrier_semaphore()
    for peer in (pal, far):
        pl.semaphore_signal(barrier, inc=1, device_id={"tp": peer}, device_id_type=MESH)
    pl.semaphore_signal(barrier, inc=1, device_id={"grp": 1 - group}, device_id_type=MESH)
    for r in range(1, dp):
        pl.semaphore_signal(barrier, inc=1, device_id={"dp": lax.rem(depth + r, dp)}, device_id_type=MESH)

    loads = []

    def load(src, dst):
        copy = pltpu.make_async_copy(src, dst, load_sem.at[len(loads)])
        copy.start()
        loads.append(copy)

    for k in range(STEPS):
        for c in range(2):
            load(self_mix.at[pl.ds(natural(c, k), CHUNK)], smix.at[pl.ds(k * 256 + c * 128, CHUNK)])
    load(wo_h, wo)
    n_first = len(loads)
    for k in range(STEPS):
        start = pl.multiple_of(256 * (core + 2 * (k // 2)) + 128 * (k % 2), 128)
        load(x_full.at[pl.ds(start, CHUNK)], xr.at[pl.ds(k * CHUNK, CHUNK)])
    load(wcq_h, wcq)
    load(wco_h, wco)
    n_second = len(loads)
    for k in range(STEPS):
        for c in range(2):
            load(out_grad.at[pl.ds(natural(c, k), CHUNK)], og.at[pl.ds(k * 256 + c * 128, CHUNK)])
    load(wup_h, wup)
    load(wdn_h, wdn)
    n_third = len(loads)

    dkv[...] = jnp.zeros_like(dkv)
    parts[...] = jnp.zeros_like(parts)

    def own(k):
        return pl.ds(pl.multiple_of(k * CHUNK, CHUNK), CHUNK)

    def pair(k):
        return pl.ds(pl.multiple_of(k * 256, 256), 256)

    def mine(k):
        return pl.ds(pl.multiple_of(k * 256 + core * CHUNK, CHUNK), CHUNK)

    def red_copy(s, k):
        return pltpu.make_async_remote_copy(
            sst.at[own(k)], rr.at[s, own(k)], cs_sem.at[s, k], cr_sem.at[s, k],
            device_id={"tp": pal}, device_id_type=MESH)

    def far_copy(s, k):
        return pltpu.make_async_remote_copy(
            yst.at[own(k)], yr.at[s, own(k)], ys_sem.at[s, k], yr_sem.at[s, k],
            device_id={"tp": far}, device_id_type=MESH)

    def norm_copy(s, k):
        return pltpu.make_async_remote_copy(
            nf.at[s, mine(k)], nf.at[s, mine(k)], ns_sem.at[s, k], nr_sem.at[s, k],
            device_id={"tp": pal}, device_id_type=MESH)

    def produce(s, k, columns):
        for j, value in columns:
            pbuf[:, j : j + value.shape[1]] = value
        if s > 0:
            red_copy(s - 1, k).wait_send()
        sst[own(k)] = pbuf[pl.ds(pl.multiple_of((1 - core) * CHUNK, CHUNK), CHUNK), :].astype(BF16)
        red_copy(s, k).start()
        acc[own(k)] = pbuf[pl.ds(pl.multiple_of(core * CHUNK, CHUNK), CHUNK), :]

    def finish(s, k):
        if s > 0:
            far_copy(s - 1, k).wait_send()
        red_copy(s, k).wait_recv()
        total = acc[own(k)] + rr[s, own(k)].astype(F32)
        acc[own(k)] = total
        yst[own(k)] = total.astype(BF16)
        far_copy(s, k).start()

    def sub(k, r):
        return pl.ds(pl.multiple_of(k * CHUNK + r * SUB, SUB), SUB)

    def msub(k, r):
        return pl.ds(pl.multiple_of(k * 256 + core * CHUNK + r * SUB, SUB), SUB)

    for copy in loads[:n_first]:
        copy.wait()
    pl.semaphore_wait(barrier, 2 + dp)

    @pl.loop(0, STEPS)
    def _(k):
        rows = smix[pair(k), :]
        produce(0, k, [(j, nn(rows, wo[:, j : j + 512])) for j in (0, 512)])

        @pl.when(k > 0)
        def _():
            finish(0, k - 1)

    finish(0, STEPS - 1)
    for copy in loads[n_first:n_second]:
        copy.wait()

    scale = HEAD ** (-0.5)

    def act_copy(k):
        return pltpu.make_async_copy(act.at[pair(k)], act_out.at[pair(k)], out_sem.at[2 + k])

    def settle(src, dst, k, c, slot):
        start = pl.multiple_of(256 * (c + 2 * (k // 2)) + 128 * (k % 2), 128)
        return pltpu.make_async_copy(
            src.at[pl.ds(pl.multiple_of(k * 256 + c * CHUNK, CHUNK), CHUNK)],
            dst.at[pl.ds(start, CHUNK)], out_sem.at[slot + 2 * k + c])

    @pl.loop(0, STEPS)
    def _(k):
        far_copy(0, k).wait_recv()
        for r in range(CHUNK // SUB):
            hidden = xr[sub(k, r)].astype(F32) + acc[sub(k, r)] + yr[0, sub(k, r)].astype(F32)
            h1[sub(k, r)] = hidden
            xhat, _ = norm_stats(hidden)
            nf[0, msub(k, r)] = (xhat * cg_ref[...] + cs_ref[...]).astype(BF16)
        norm_copy(0, k).start()

        @pl.when(k > 0)
        def _():
            finish(1, k - 1)

        norm_copy(0, k).wait_recv()
        cq[pair(k)] = nn(nf[0, pair(k)], wcq[...]).astype(BF16)
        for slab in range(2):
            lanes = slice(slab * 128, slab * 128 + 128)
            query = cq[pair(k), lanes]
            key, value = ck_ref[:, lanes], cv_ref[:, lanes]
            mixed = []
            for part in range(2):
                scores = nt(pick(query, part), key) * scale + bias_ref[...]
                shifted = jnp.exp(scores - jnp.max(scores, axis=-1, keepdims=True))
                probs = shifted / jnp.sum(shifted, axis=-1, keepdims=True)
                mixed.append(nn(probs.astype(BF16), value))
            cmix[pair(k), lanes] = merge(*mixed).astype(BF16)
        rows = cmix[pair(k), :]
        produce(1, k, [(j, nn(rows, wco[:, j : j + 512])) for j in (0, 512)])

    finish(1, STEPS - 1)
    for copy in loads[n_second:n_third]:
        copy.wait()

    @pl.loop(0, STEPS)
    def _(k):
        far_copy(1, k).wait_recv()
        for r in range(CHUNK // SUB):
            hidden = h1[sub(k, r)] + acc[sub(k, r)] + yr[1, sub(k, r)].astype(F32)
            h2[sub(k, r)] = hidden
            xhat, _ = norm_stats(hidden)
            nf[1, msub(k, r)] = (xhat * mg_ref[...] + ms_ref[...]).astype(BF16)
        norm_copy(1, k).start()

        @pl.when(k > 0)
        def _():
            finish(2, k - 1)

        norm_copy(1, k).wait_recv()
        rows = nf[1, pair(k)]
        grads = og[pair(k), :]
        for j in range(0, 1024, 256):
            cols = slice(j, j + 256)
            pre = nn(rows, wup[:, cols])
            back = nt(grads, wdn[cols, :])
            square = pre * pre
            bend = jnp.tanh(0.7978845608028654 * pre * (1.0 + 0.044715 * square))
            half = 0.5 * (1.0 + bend)
            act[pair(k), cols] = (pre * half).astype(BF16)
            slope = half + 0.5 * pre * (1.0 - bend * bend) * (
                0.7978845608028654 * (1.0 + 3 * 0.044715 * square))
            pg[pair(k), cols] = (back * slope).astype(BF16)
        rows = pg[pair(k), :]
        produce(2, k, [(j, nt(rows, wup[j : j + 256, :])) for j in range(0, 1024, 256)])
        act_copy(k).start()

    finish(2, STEPS - 1)

    def up_piece(c):
        z = jnp.minimum(c, 2)
        return Piece(place, ug.at[c], ux.at[c], uz.at[z], (xs_sem.at[0, c], xr_sem.at[0, c]),
                     (zs_sem.at[0, z], zr_sem.at[0, z]))

    def down_piece(c):
        z = jnp.minimum(c, 2)
        return Piece(place, dg.at[c], dx.at[c], dz.at[z], (xs_sem.at[1, c], xr_sem.at[1, c]),
                     (zs_sem.at[1, z], zr_sem.at[1, z]))

    def own_rows(k):
        return jnp.where(k // 2 == chip, 1.0, 0.0)

    @pl.loop(0, STEPS)
    def _(k):
        at = pl.multiple_of(k * 256, 256)
        right = pg[:, pl.ds(at, 256)]
        for m in range(4):
            value = tn(nf[1, :, m * 256 : m * 256 + 256], right).astype(BF16)
            for u in range(per):
                ug[k, m * per + u, 0] = value[u * span : u * span + span // 2]
                ug[k, m * per + u, 1] = value[u * span + span // 2 : (u + 1) * span]
        up_piece(k).start()
        left = act[:, pl.ds(at, 256)]
        for m in range(4):
            value = tn(left, og[:, m * 256 : m * 256 + 256]).astype(BF16)
            for u in range(per):
                dg[k, m * per + u, 0] = value[:128, u * span : (u + 1) * span]
                dg[k, m * per + u, 1] = value[128:, u * span : (u + 1) * span]
        down_piece(k).start()

        @pl.when(k == 2)
        def _():
            up_piece(0).add()
            up_piece(0).spread()

        @pl.when(k == 3)
        def _():
            down_piece(0).add()
            down_piece(0).spread()

        far_copy(2, k).wait_recv()
        keep = own_rows(k)
        for r in range(CHUNK // SUB):
            third = acc[sub(k, r)] + yr[2, sub(k, r)].astype(F32)
            xhat, rstd = norm_stats(h2[sub(k, r)])
            parts[2] += fold_rows(third * xhat) * keep
            parts[3] += fold_rows(third) * keep
            resid = og[msub(k, r)].astype(F32) + norm_input_grad(xhat, rstd, mg_ref[...], third)
            g2[sub(k, r)] = resid
            nf[2, msub(k, r)] = resid.astype(BF16)
        norm_copy(2, k).start()

        @pl.when(k > 0)
        def _():
            finish(3, k - 1)

        norm_copy(2, k).wait_recv()
        mix_grad = nt(nf[2, pair(k)], wco[...]).astype(BF16)
        for slab in range(2):
            lanes = slice(slab * 128, slab * 128 + 128)
            query = cq[pair(k), lanes]
            grad = mix_grad[:, lanes]
            key, value = ck_ref[:, lanes], cv_ref[:, lanes]
            moved = []
            for part in range(2):
                one_q, one_g = pick(query, part), pick(grad, part)
                scores = nt(one_q, key) * scale + bias_ref[...]
                shifted = jnp.exp(scores - jnp.max(scores, axis=-1, keepdims=True))
                probs = shifted / jnp.sum(shifted, axis=-1, keepdims=True)
                prob_grad = nt(one_g, value)
                inner = jnp.sum(probs * prob_grad, axis=-1, keepdims=True)
                score_grad = (probs * (prob_grad - inner)).astype(BF16)
                moved.append(nn(score_grad, key) * scale)
                dkv[0, :, lanes] += tn(score_grad, one_q)
                dkv[1, :, lanes] += tn(probs.astype(BF16), one_g)
            cqg[pair(k), lanes] = merge(*moved).astype(BF16)
        rows = cqg[pair(k), :]
        produce(3, k, [(j, nt(rows, wcq[j : j + 512, :])) for j in (0, 512)])

    finish(3, STEPS - 1)
    @pl.loop(0, STEPS)
    def _(k):
        at = pl.multiple_of(k * 256, 256)
        value = tn(nf[0, :, pl.ds(at, 256)], cqg[...]).astype(BF16)
        for u in range(per):
            dcq[k * per + u, 0] = value[u * span : u * span + span // 2]
            dcq[k * per + u, 1] = value[u * span + span // 2 : (u + 1) * span]
        value = tn(cmix[...], nf[2, :, pl.ds(at, 256)]).astype(BF16)
        for u in range(per):
            dco[k * per + u, 0] = value[:128, u * span : (u + 1) * span]
            dco[k * per + u, 1] = value[128:, u * span : (u + 1) * span]

        @pl.when(k % 2 == 0)
        def _():
            up_piece(1 + k // 2).add()
            up_piece(1 + k // 2).spread()

        @pl.when(k % 2 == 1)
        def _():
            down_piece(1 + k // 2).add()
            down_piece(1 + k // 2).spread()

        far_copy(3, k).wait_recv()
        keep = own_rows(k)
        for r in range(CHUNK // SUB):
            second = acc[sub(k, r)] + yr[3, sub(k, r)].astype(F32)
            xhat, rstd = norm_stats(h1[sub(k, r)])
            parts[0] += fold_rows(second * xhat) * keep
            parts[1] += fold_rows(second) * keep
            resid = g2[sub(k, r)] + norm_input_grad(xhat, rstd, cg_ref[...], second)
            g2[sub(k, r)] = resid
            nf[3, msub(k, r)] = resid.astype(BF16)
        norm_copy(3, k).start()
        norm_copy(3, k).wait_recv()
        smg[pair(k)] = nt(nf[3, pair(k)], wo[...]).astype(BF16)
        for c in range(2):
            settle(smg, smg_out, k, c, 10).start()
            settle(nf.at[3], sb_out, k, c, 18).start()

    mine_rows = pl.ds(pl.multiple_of(chip * 256, 256), 256)
    final = [
        pltpu.make_async_copy(g2.at[mine_rows], resid_out, out_sem.at[26]),
        pltpu.make_async_copy(h2.at[mine_rows], ac_out, out_sem.at[27]),
        pltpu.make_async_copy(dcq, dcq_out, out_sem.at[28]),
        pltpu.make_async_copy(dco, dco_out, out_sem.at[29]),
    ]
    for copy in final:
        copy.start()
    for c in range(3):
        uf[c] = up_piece(c).total()
        df[c] = down_piece(c).total()
    up_piece(3).add()
    down_piece(3).add()
    late = [
        pltpu.make_async_copy(uf, uf_out, out_sem.at[30]),
        pltpu.make_async_copy(df, df_out, out_sem.at[31]),
        pltpu.make_async_copy(ux.at[3], ul_out, out_sem.at[0]),
        pltpu.make_async_copy(dx.at[3], dl_out, out_sem.at[1]),
    ]
    for copy in late:
        copy.start()
    dck_out[...] = (dkv[0] * scale).astype(BF16)
    dcv_out[...] = dkv[1].astype(BF16)
    parts_out[...] = parts[...]
    for k in range(STEPS):
        red_copy(3, k).wait_send()
        far_copy(3, k).wait_send()
        for s in range(4):
            norm_copy(s, k).wait_send()
        act_copy(k).wait()
        for c in range(2):
            settle(smg, smg_out, k, c, 10).wait()
            settle(nf.at[3], sb_out, k, c, 18).wait()
    for c in range(4):
        up_piece(c).x_end()
        down_piece(c).x_end()
    for c in range(3):
        up_piece(c).z_end()
        down_piece(c).z_end()
    for copy in final + late:
        copy.wait()


def middle(dp, x_full, self_mix, out_grad, wo, wcq, wco, wup, wdn, ck, cv, bias, gains):
    full = jax.ShapeDtypeStruct((1024, 1024), BF16)
    narrow = jax.ShapeDtypeStruct((1024, 256), BF16)
    short = jax.ShapeDtypeStruct((128, 256), BF16)
    block = jax.ShapeDtypeStruct((256, 1024), F32)
    part = 1024 // dp
    rows, columns = (part // 2, 256), (128, part)
    outs = [
        narrow, full, full] + [
        jax.ShapeDtypeStruct(item, BF16)
        for item in ((3,) + rows, (3,) + columns, (dp,) + rows, (dp,) + columns, (dp, 2) + rows, (dp, 2) + columns)
    ] + [short, short,
        jax.ShapeDtypeStruct((4, 8, 1024), F32), block, block,
    ]
    out_specs = [ANY] * 9 + [VM] * 3 + [ANY] * 2
    vm = pltpu.VMEM
    dma = pltpu.SemaphoreType.DMA
    scratch = [
        vm((256, 1024), BF16), vm((1024, 256), BF16), vm((256, 1024), BF16), vm((1024, 1024), BF16),
        vm((1024, 1024), BF16), vm((1024, 256), BF16), vm((1024, 1024), BF16), vm((512, 1024), BF16),
        vm((512, 1024), F32), vm((512, 1024), F32), vm((512, 1024), F32), vm((512, 1024), F32),
        vm((4, 1024, 1024), BF16), vm((1024, 1024), BF16), vm((1024, 1024), BF16),
        vm((1024, 256), BF16), vm((1024, 256), BF16), vm((1024, 256), BF16),
        vm((4, 512, 1024), BF16), vm((4, 512, 1024), BF16), vm((512, 1024), BF16), vm((512, 1024), BF16),
        vm((256, 1024), F32), vm((2, 128, 256), F32), vm((1024, 256), BF16),
        vm((4, dp, 2) + rows, BF16), vm((4, dp, 2) + columns, BF16), vm((4, dp) + rows, BF16), vm((4, dp) + columns, BF16),
        vm((3, dp - 1) + rows, BF16), vm((3, dp - 1) + columns, BF16), vm((3,) + rows, BF16), vm((3,) + columns, BF16),
        vm((dp, 2) + columns, BF16), vm((dp, 2) + rows, BF16),
        vm((4, 8, 1024), F32),
        dma((32,)), dma((4, 4)), dma((4, 4)), dma((4, 4)), dma((4, 4)), dma((4, 4)), dma((4, 4)),
        dma((2, 4)), dma((2, 4)), dma((2, 3, dp - 1)), dma((2, 3, dp - 1)), dma((32,)),
    ]
    return pl.pallas_call(
        functools.partial(middle_kernel, dp),
        out_shape=outs,
        in_specs=[ANY] * 8 + [VM] * 7,
        out_specs=out_specs,
        scratch_shapes=scratch,
        name="middle",
        compiler_params=pltpu.CompilerParams(
            collective_id=1, has_side_effects=True, vmem_limit_bytes=GRANT),
    )(x_full, self_mix, out_grad, wo, wcq, wco, wup, wdn, ck, cv, bias, *gains)


def front_kernel(
    x_own, wq_h, wk_h, wv_h, text_h, wck_h, wcv_h, ag_ref, as_ref,
    x_out, n1_out, q_out, k_out, v_out, mix_out, p0_out, p1_out, p2_out, p3_out, ck_out, cv_out,
    xf, n1, q, k, v, mix, p0, p1, p2, p3, wq, wk, wv, text, wck, wcv,
    load_sem, y_s, y_r, c_s, c_r, f_s, f_r, out_sem,
):
    rank = lax.axis_index("tp")
    core = lax.rem(rank, 2)
    pal = rank + 1 - 2 * core
    far = lax.rem(rank + 2, 4)
    beyond = lax.rem(pal + 2, 4)
    barrier = pltpu.get_barrier_semaphore()
    for peer in (pal, far):
        pl.semaphore_signal(barrier, inc=1, device_id={"tp": peer}, device_id_type=MESH)
    loads = [
        pltpu.make_async_copy(src, dst, load_sem.at[i])
        for i, (src, dst) in enumerate([
            (x_own, xf.at[pl.ds(pl.multiple_of(rank * 256, 256), 256)]),
            (text_h, text), (wck_h, wck), (wcv_h, wcv), (wq_h, wq), (wk_h, wk), (wv_h, wv)])
    ]
    for copy in loads:
        copy.start()

    def part(block, i, size):
        return pl.ds(pl.multiple_of(block * 256 + i * size, size), size)

    across = [
        pltpu.make_async_remote_copy(
            x_own.at[pl.ds(i * 64, 64)], xf.at[part(rank, i, 64)], y_s.at[i], y_r.at[i],
            device_id={"tp": far}, device_id_type=MESH)
        for i in range(4)
    ]
    beside = pltpu.make_async_remote_copy(
        x_own, xf.at[part(rank, 0, 256)], c_s.at[0], c_r.at[0], device_id={"tp": pal}, device_id_type=MESH)
    onward = [
        pltpu.make_async_remote_copy(
            xf.at[part(far, i, 64)], xf.at[part(far, i, 64)], f_s.at[i], f_r.at[i],
            device_id={"tp": pal}, device_id_type=MESH)
        for i in range(4)
    ]
    pl.semaphore_wait(barrier, 2)
    for copy in across:
        copy.start()
    beside.start()

    for copy in loads[1:4]:
        copy.wait()
    ck_out[...] = nn(text[...], wck[...]).astype(BF16)
    cv_out[...] = nn(text[...], wcv[...]).astype(BF16)
    for copy in loads[4:] + loads[:1]:
        copy.wait()

    def project(block, i):
        for r in range(4):
            rows = pl.ds(pl.multiple_of(block * 256 + i * 128 + r * 32, 32), 32)
            xhat, _ = norm_stats(xf[rows].astype(F32))
            n1[rows] = (xhat * ag_ref[...] + as_ref[...]).astype(BF16)
        rows = part(block, i, 128)
        value = n1[rows]
        q[rows] = (nn(value, wq[...]).astype(BF16) * 0.125).astype(BF16)
        k[rows] = nn(value, wk[...]).astype(BF16)
        v[rows] = nn(value, wv[...]).astype(BF16)

    def both(block):
        @pl.loop(0, 2)
        def _(i):
            project(block, i)

    both(rank)
    beside.wait_recv()
    both(pal)
    for half in range(2):
        for i in (2 * half, 2 * half + 1):
            across[i].wait_recv()
            onward[i].start()
        project(far, half)
        for i in (2 * half, 2 * half + 1):
            onward[i].wait_recv()
        project(beyond, half)
    outs = [
        pltpu.make_async_copy(src, dst, out_sem.at[i])
        for i, (src, dst) in enumerate([(xf, x_out), (n1, n1_out), (q, q_out), (k, k_out), (v, v_out)])
    ]
    for copy in outs:
        copy.start()

    kept = (p0, p1, p2, p3)
    below = lax.broadcasted_iota(jnp.int32, (256, 256), 0) >= lax.broadcasted_iota(jnp.int32, (256, 256), 1)

    @pl.loop(0, 2)
    def _(slab):
        lanes = pl.ds(pl.multiple_of(slab * 128, 128), 128)
        for i in range(4):
            done, end = i * 256, i * 256 + 256
            query = q[done:end, lanes]
            mixed = []
            for half in range(2):
                one = pick(query, half)
                diag = jnp.where(below, nt(one, k[done:end, lanes]), MASKED)
                peak = jnp.max(diag, axis=-1, keepdims=True)
                if i:
                    past = nt(one, k[0:done, lanes])
                    peak = jnp.maximum(peak, jnp.max(past, axis=-1, keepdims=True))
                    past = jnp.exp(past - peak)
                diag = jnp.exp(diag - peak)
                total = jnp.sum(diag, axis=-1, keepdims=True)
                if i:
                    total = total + jnp.sum(past, axis=-1, keepdims=True)
                inverse = 1.0 / total
                probs = (diag * inverse).astype(BF16)
                kept[i][slab * 2 + half, :, done:end] = probs
                out = nn(probs, v[done:end, lanes])
                if i:
                    probs = (past * inverse).astype(BF16)
                    kept[i][slab * 2 + half, :, 0:done] = probs
                    out = out + nn(probs, v[0:done, lanes])
                mixed.append(out)
            mix[done:end, lanes] = merge(*mixed).astype(BF16)

    tail = [
        pltpu.make_async_copy(src, dst, out_sem.at[5 + i])
        for i, (src, dst) in enumerate(
            [(mix, mix_out), (p0, p0_out), (p1, p1_out), (p2, p2_out), (p3, p3_out)])
    ]
    for copy in tail:
        copy.start()
    for copy in across + [beside] + onward:
        copy.wait_send()
    for copy in outs + tail:
        copy.wait()


def front(x_own, wq, wk, wv, text, wck, wcv, gains):
    full = ((1024, 1024), BF16)
    narrow = ((1024, 256), BF16)
    short = ((128, 256), BF16)
    probs = [((4, 256, 256 * (i + 1)), BF16) for i in range(4)]
    vm = pltpu.VMEM
    dma = pltpu.SemaphoreType.DMA
    return pl.pallas_call(
        front_kernel,
        out_shape=[jax.ShapeDtypeStruct(*item) for item in [full, full, narrow, narrow, narrow, narrow] + probs + [short, short]],
        in_specs=[ANY] * 7 + [VM] * 2,
        out_specs=[ANY] * 10 + [VM] * 2,
        scratch_shapes=[vm(*item) for item in [full, full, narrow, narrow, narrow, narrow] + probs
                        + [narrow] * 3 + [((128, 1024), BF16), narrow, narrow]]
        + [dma((8,)), dma((4,)), dma((4,)), dma((1,)), dma((1,)), dma((4,)), dma((4,)), dma((12,))],
        name="front",
        compiler_params=pltpu.CompilerParams(
            collective_id=2, has_side_effects=True, vmem_limit_bytes=GRANT),
    )(x_own, wq, wk, wv, text, wck, wcv, *gains)


def back_kernel(dp, *refs):
    refs = list(refs)

    def take(n):
        taken, refs[:n] = refs[:n], []
        return taken

    (smix_h, sb_h, act_h, wdn_h, smg_h, q_h, k_h, v_h, p0_h, p1_h, p2_h, p3_h, n1_h, wq_h, wk_h, wv_h,
     x_own, resid_h, ac_h, dcq_h, dco_h, ul_h, dl_h, uf_h, df_h) = take(25)
    text, wck, wcv, dck, dcv, parts_in, ag_ref = take(7)
    layer_out, image_grad, text_out, norm_out, up_o, dn_o, cq_o, co_o, ck_o, cv_o, so_o, sq_o, sk_o, sv_o = take(14)
    (smix, sb, act, wdn, smg, q, k, v, p0, p1, p2, p3, n1, wq, wk, wv, xo, resid, ac,
     cq_y, co_y, ul_x, dl_x) = take(23)
    ck_g, cv_g, so_g, sq_g, sk_g, sv_g = take(6)
    x_bufs, z_bufs = take(6), take(8)
    ck_z, cv_z, ck_t, cv_t, ck_p, cv_p = take(6)
    (dq, dk, dv, dkv, acc, sst, rr, yst, yr, tpart, t_st, t_rr, t_yst, t_yr, t_fin, npart, n_tp, nsum, n_all) = take(19)
    (load_sem, xs, xr, zs, zr, gs, gr, cs_sem, cr_sem, ys_sem, yr_sem, t_s, t_r, n_s, n_r, m_s, m_r) = take(17)

    rank = lax.axis_index("tp")
    group = lax.axis_index("grp")
    depth = lax.axis_index("dp")
    core = lax.rem(rank, 2)
    chip = rank // 2
    pal = rank + 1 - 2 * core
    far = lax.rem(rank + 2, 4)
    others = [(g, r) for g in range(2) for r in range(dp) if g or r]
    barrier = pltpu.get_barrier_semaphore()
    for r in range(1, 4):
        pl.semaphore_signal(barrier, inc=1, device_id={"tp": lax.rem(rank + r, 4)}, device_id_type=MESH)

    def at_other(g, r):
        return {"grp": lax.rem(group + g, 2), "dp": lax.rem(depth + r, dp)}

    for g, r in others:
        pl.semaphore_signal(barrier, inc=1, device_id=at_other(g, r), device_id_type=MESH)

    pairs = [
        (smix_h, smix), (sb_h, sb), (act_h, act), (wdn_h, wdn), (smg_h, smg), (q_h, q), (k_h, k), (v_h, v),
        (p0_h, p0), (p1_h, p1), (p2_h, p2), (p3_h, p3), (n1_h, n1), (wq_h, wq), (wk_h, wk), (wv_h, wv),
        (x_own, xo), (resid_h, resid), (ac_h, ac),
        (dcq_h.at[:, group], cq_y), (dco_h.at[:, group], co_y), (ul_h, ul_x), (dl_h, dl_x),
    ]
    pairs += [(uf_h.at[c], up_o.at[c, group]) for c in range(3)] + [(df_h.at[c], dn_o.at[c, group]) for c in range(3)]
    loads = [pltpu.make_async_copy(src, dst, load_sem.at[i]) for i, (src, dst) in enumerate(pairs)]
    for copy in loads:
        copy.start()

    place = (group, depth, dp)

    def piece(n, source, x_buf):
        return Piece(place, source, x_buf, z_bufs[n], (xs.at[n], xr.at[n]), (zs.at[n], zr.at[n]))

    def give(n, src, out):
        return pltpu.make_async_remote_copy(
            src, out, gs.at[n], gr.at[n], device_id={"grp": 1 - group}, device_id_type=MESH)

    cq_p, co_p = piece(0, dcq_h, x_bufs[0]), piece(1, dco_h, x_bufs[1])
    so_p, sq_p, sk_p, sv_p = [
        piece(2 + i, g, x_bufs[2 + i]) for i, g in enumerate((so_g, sq_g, sk_g, sv_g))]
    ul_p, dl_p = piece(6, None, ul_x), piece(7, None, dl_x)
    halves = [
        (cq_p, cq_o), (co_p, co_o), (so_p, so_o), (sq_p, sq_o), (sk_p, sk_o), (sv_p, sv_o), (ul_p, up_o.at[3]),
        (dl_p, dn_o.at[3])]
    gives = [give(n, out.at[group], out.at[group]) for n, (_, out) in enumerate(halves)]
    early = [give(8 + c, uf_h.at[c], up_o.at[c, group]) for c in range(3)]
    early += [give(11 + c, df_h.at[c], dn_o.at[c, group]) for c in range(3)]
    ck_a = Across(place, ck_g, ck_z, ck_t, ck_p, ck_o, (zs.at[8], zr.at[8]), (gs.at[14], gr.at[14]))
    cv_a = Across(place, cv_g, cv_z, cv_t, cv_p, cv_o, (zs.at[9], zr.at[9]), (gs.at[15], gr.at[15]))

    def finish(n):
        one, out = halves[n]
        out[group] = one.total()
        gives[n].start()

    pl.semaphore_wait(barrier, 3 + len(others))
    cq_p.start()
    co_p.start()
    for copy in early:
        copy.start()
    for copy in loads[21:23]:
        copy.wait()
    ul_p.spread()
    dl_p.spread()

    scale = HEAD ** (-0.5)
    depth_rows = 1024 // dp
    per = 256 // depth_rows

    def rows_grad(ref, left, right):
        for m in range(4):
            value = tn(left[:, m * 256 : m * 256 + 256], right[...]).astype(BF16)
            for u in range(per):
                part = value[u * depth_rows : (u + 1) * depth_rows]
                ref[m * per + u, 0] = part[: depth_rows // 2]
                ref[m * per + u, 1] = part[depth_rows // 2 :]

    rows_grad(ck_g, text, dck)
    rows_grad(cv_g, text, dcv)
    ck_a.start()
    cv_a.start()
    tpart[...] = nt(dck[...], wck[...]) + nt(dcv[...], wcv[...])

    def t_rows(c):
        return pl.ds(pl.multiple_of(c * 64, 64), 64)

    t_st[...] = tpart[t_rows(1 - core)].astype(BF16)
    t_red = pltpu.make_async_remote_copy(
        t_st, t_rr, t_s.at[0], t_r.at[0], device_id={"tp": pal}, device_id_type=MESH)
    t_red.start()

    for copy in loads[:2]:
        copy.wait()
    for d in range(dp):
        value = tn(smix[...], sb[:, d * depth_rows : (d + 1) * depth_rows]).astype(BF16)
        so_g[d, 0] = value[:128]
        so_g[d, 1] = value[128:]
    so_p.start()
    t_red.wait_recv()
    t_yst[...] = (tpart[t_rows(core)] + t_rr[...].astype(F32)).astype(BF16)
    t_far = pltpu.make_async_remote_copy(
        t_yst, t_yr, t_s.at[1], t_r.at[1], device_id={"tp": far}, device_id_type=MESH)
    t_far.start()

    def own(i):
        return pl.ds(pl.multiple_of(i * CHUNK, CHUNK), CHUNK)

    class Scatter:
        def __init__(self, n):
            self.n = n

        def red(self, i):
            n = self.n
            return pltpu.make_async_remote_copy(
                sst.at[n, own(i)], rr.at[n, own(i)], cs_sem.at[n, i], cr_sem.at[n, i],
                device_id={"tp": pal}, device_id_type=MESH)

        def far(self, j):
            n = self.n
            return pltpu.make_async_remote_copy(
                yst.at[n, own(j)], yr.at[n, own(j)], ys_sem.at[n, j], yr_sem.at[n, j],
                device_id={"tp": far}, device_id_type=MESH)

        def put(self, i, theirs, ours):
            sst[self.n, own(i)] = theirs.astype(BF16)
            self.red(i).start()
            acc[self.n, own(i)] = ours

        def send(self, j):
            i = 2 * (1 - chip) + j
            self.red(i).wait_recv()
            yst[self.n, own(j)] = (acc[self.n, own(i)] + rr[self.n, own(i)].astype(F32)).astype(BF16)
            self.far(j).start()

        def keep(self, j):
            self.red(2 * chip + j).wait_recv()
            self.far(j).wait_recv()

        def value(self, j, r):
            i = 2 * chip + j
            rows = pl.ds(pl.multiple_of(i * CHUNK + r * SUB, SUB), SUB)
            near = pl.ds(j * CHUNK + r * SUB, SUB)
            return acc[self.n, rows] + rr[self.n, rows].astype(F32) + yr[self.n, near].astype(F32)

        def end(self):
            for i in range(4):
                self.red(i).wait_send()
            for j in range(2):
                self.far(j).wait_send()

    layer, first = Scatter(0), Scatter(1)
    for copy in loads[2:4]:
        copy.wait()

    def sequence(step):
        return lax.rem(2 * (1 - chip) + step, 4)

    @pl.loop(0, 4)
    def _(step):
        i = sequence(step)
        theirs = act[pl.ds(pl.multiple_of(i * 256 + (1 - core) * CHUNK, CHUNK), CHUNK), :]
        ours = act[pl.ds(pl.multiple_of(i * 256 + core * CHUNK, CHUNK), CHUNK), :]
        layer.put(i, nn(theirs, wdn[...]), nn(ours, wdn[...]))

        @pl.when((step > 0) & (step < 3))
        def _():
            layer.send(step - 1)

    for copy in loads[4:12]:
        copy.wait()
    dkv[...] = jnp.zeros_like(dkv)
    kept = (p0, p1, p2, p3)

    @pl.loop(0, 2)
    def _(slab):
        lanes = pl.ds(pl.multiple_of(slab * 128, 128), 128)
        for i in range(4):
            begin, end = i * 256, i * 256 + 256
            query, grad = q[begin:end, lanes], smg[begin:end, lanes]
            product = grad.astype(F32) * smix[begin:end, lanes].astype(F32)
            moved = []
            for half in range(2):
                one_q, one_g = pick(query, half), pick(grad, half)
                inner = jnp.sum(pick(product, half), axis=-1, keepdims=True)
                probs = kept[i][slab * 2 + half]
                prob_grad = nt(one_g, v[0:end, lanes])
                score_grad = (probs.astype(F32) * (prob_grad - inner)).astype(BF16)
                moved.append(nn(score_grad, k[0:end, lanes]))
                dkv[0, 0:end, lanes] += tn(score_grad, one_q)
                dkv[1, 0:end, lanes] += tn(probs, one_g)
            dq[begin:end, lanes] = (merge(*moved) * scale).astype(BF16)

    dk[...] = dkv[0].astype(BF16)
    dv[...] = dkv[1].astype(BF16)

    for copy in loads[12:21] + loads[23:]:
        copy.wait()
    rows_grad(sq_g, n1, dq)
    sq_p.start()
    rows_grad(sk_g, n1, dk)
    sk_p.start()
    rows_grad(sv_g, n1, dv)
    sv_p.start()
    cq_p.add(cq_y)
    cq_p.spread()
    co_p.add(co_y)
    co_p.spread()

    @pl.loop(0, 4)
    def _(step):
        i = sequence(step)

        def partial(c):
            start = pl.multiple_of(256 * (c + 2 * (i // 2)) + 128 * lax.rem(i, 2), 128)
            rows = pl.ds(start, CHUNK)
            return nt(dq[rows], wq[...]) + nt(dk[rows], wk[...]) + nt(dv[rows], wv[...])

        first.put(i, partial(1 - core), partial(core))

        @pl.when((step > 0) & (step < 3))
        def _():
            first.send(step - 1)

    finish(6)
    finish(7)
    so_p.add()
    so_p.spread()
    ck_a.total()
    cv_a.total()
    for j in range(2):
        layer.keep(j)
        for r in range(CHUNK // SUB):
            rows = slice(j * CHUNK + r * SUB, j * CHUNK + r * SUB + SUB)
            layer_out[rows] = (ac[rows] + layer.value(j, r)).astype(BF16)

    t_far.wait_recv()
    t_fin[t_rows(core)] = (t_yst[...].astype(F32) + t_yr[...].astype(F32)).astype(BF16)
    t_share = pltpu.make_async_remote_copy(
        t_fin.at[t_rows(core)], t_fin.at[t_rows(core)], t_s.at[2], t_r.at[2],
        device_id={"tp": pal}, device_id_type=MESH)
    t_share.start()

    npart[...] = jnp.zeros_like(npart)
    for j in range(2):
        first.keep(j)
        for r in range(CHUNK // SUB):
            rows = slice(j * CHUNK + r * SUB, j * CHUNK + r * SUB + SUB)
            given = first.value(j, r)
            xhat, rstd = norm_stats(xo[rows].astype(F32))
            npart[0] += fold_rows(given * xhat)
            npart[1] += fold_rows(given)
            image_grad[rows] = resid[rows] + norm_input_grad(xhat, rstd, ag_ref[...], given)

    def line(ref, i):
        return jnp.sum(ref[i], axis=0, keepdims=True)

    n_tp[rank] = jnp.concatenate(
        [line(npart, 0), line(npart, 1)] + [line(parts_in, i) for i in range(4)]
        + [jnp.zeros((2, 1024), F32)], axis=0)
    n_copies = [
        pltpu.make_async_remote_copy(
            n_tp.at[rank], n_tp.at[rank], n_s.at[r - 1], n_r.at[r - 1],
            device_id={"tp": lax.rem(rank + r, 4)}, device_id_type=MESH)
        for r in range(1, 4)
    ]
    for copy in n_copies:
        copy.start()
    sq_p.add()
    sq_p.spread()
    finish(0)
    finish(1)
    for copy in n_copies:
        copy.wait_recv()
    summed = n_tp[0] + n_tp[1] + n_tp[2] + n_tp[3]
    for d in range(dp):
        nsum[d] = summed[:, d * depth_rows : (d + 1) * depth_rows]
    slot = group * dp + depth
    m_copies = [
        pltpu.make_async_remote_copy(
            nsum.at[lax.rem(depth + r, dp)], n_all.at[slot], m_s.at[i], m_r.at[i],
            device_id=at_other(g, r), device_id_type=MESH)
        for i, (g, r) in enumerate(others)
    ]
    for copy in m_copies:
        copy.start()
    n_all[slot] = nsum[depth]

    sk_p.add()
    sk_p.spread()
    finish(2)
    finish(3)
    sv_p.add()
    sv_p.spread()
    finish(4)
    finish(5)
    ck_a.end()
    cv_a.end()
    for copy in m_copies:
        copy.wait_recv()
    total = n_all[0]
    for i in range(1, 2 * dp):
        total = total + n_all[i]
    norm_out[...] = total
    t_share.wait_recv()
    text_out[...] = t_fin[...]
    for copy in m_copies + n_copies + [t_red, t_far, t_share]:
        copy.wait_send()
    layer.end()
    first.end()
    for n, (one, _) in enumerate(halves):
        if n < 6:
            one.x_end()
        one.z_end()
        gives[n].wait()
    for copy in early:
        copy.wait()


def back(dp, *operands):
    part = 1024 // dp
    full = ((1024, 1024), BF16)
    narrow = ((1024, 256), BF16)
    probs = [((4, 256, 256 * (i + 1)), BF16) for i in range(4)]
    rows, columns = (part // 2, 256), (128, part)
    block = ((256, 1024), F32)
    kinds = [rows, columns, rows, rows, columns, rows, rows, rows]
    outs = [((256, 1024), BF16), block, ((128, 1024), BF16), ((8, part), F32), ((4, 2) + rows, BF16), ((4, 2) + columns, BF16)]
    outs += [((2,) + s, BF16) for s in kinds]
    scratch = (
        [narrow, full, full, full] + [narrow] * 4 + probs + [full] + [narrow] * 3
        + [((256, 1024), BF16), block, block]
        + [((dp,) + s, BF16) for s in (rows, columns, rows, columns)]
        + [((dp, 2) + s, BF16) for s in kinds[2:]]
        + [((dp,) + s, BF16) for s in (rows, columns, columns, rows, rows, rows)]
        + [((dp - 1,) + s, BF16) for s in (rows, columns, columns, rows, rows, rows, rows, columns)]
        + [((dp - 1, 2) + rows, BF16)] * 2 + [((2,) + rows, BF16)] * 4
        + [narrow] * 3
        + [((2, 1024, 256), F32), ((2, 512, 1024), F32), ((2, 512, 1024), BF16), ((2, 512, 1024), BF16),
           ((2, 256, 1024), BF16), ((2, 256, 1024), BF16), ((128, 1024), F32),
           ((64, 1024), BF16), ((64, 1024), BF16), ((64, 1024), BF16), ((64, 1024), BF16), ((128, 1024), BF16),
           ((2, 8, 1024), F32), ((4, 8, 1024), F32), ((dp, 8, part), F32), ((2 * dp, 8, part), F32)]
    )
    dma = pltpu.SemaphoreType.DMA
    many = 2 * dp - 1
    sems = [dma((32,)), dma((6,)), dma((6,)), dma((10, dp - 1)), dma((10, dp - 1)), dma((16,)), dma((16,)),
            dma((2, 4)), dma((2, 4)), dma((2, 2)), dma((2, 2)), dma((3,)), dma((3,)), dma((3,)), dma((3,)),
            dma((many,)), dma((many,))]
    return pl.pallas_call(
        functools.partial(back_kernel, dp),
        out_shape=[jax.ShapeDtypeStruct(*item) for item in outs],
        in_specs=[ANY] * 25 + [VM] * 7,
        out_specs=[VM] * len(outs),
        scratch_shapes=[pltpu.VMEM(*item) for item in scratch] + sems,
        name="back",
        compiler_params=pltpu.CompilerParams(
            collective_id=3, has_side_effects=True, vmem_limit_bytes=GRANT),
    )(*operands)


def emit_kernel(n, *refs):
    layer, image, text, norms, up, down = refs[:6]
    outs = refs[n:]
    outs[0][...] = layer[...]
    outs[1][...] = image[...]
    outs[2][...] = text[...].astype(F32)
    for i in range(6):
        outs[3 + i][...] = norms[i]
    rows, columns = up.shape[2], down.shape[2]
    for c in range(4):
        for h in range(2):
            outs[9][h * rows : (h + 1) * rows, c * 256 : c * 256 + 256] = up[c, h].astype(F32)
            at = c * 256 + h * columns
            outs[10][at : at + columns, :] = down[c, h].astype(F32)
    for given, out in zip(refs[6:n], outs[11:]):
        rows = given.shape[1]
        for h in range(2):
            out[h * rows : (h + 1) * rows] = given[h].astype(F32)


def emit(arrays):
    part = arrays[3].shape[1]
    shapes = [(part,)] * 6 + [(part, 1024), (1024, part)]
    outs = [jax.ShapeDtypeStruct((256, 1024), BF16), jax.ShapeDtypeStruct((256, 1024), F32), jax.ShapeDtypeStruct((128, 1024), F32)]
    outs += [jax.ShapeDtypeStruct(item, F32) for item in shapes]
    outs += [jax.ShapeDtypeStruct((2 * item.shape[1], item.shape[2]), F32) for item in arrays[6:]]
    return pl.pallas_call(
        functools.partial(emit_kernel, len(arrays)),
        out_shape=outs,
        in_specs=[VM] * len(arrays),
        out_specs=[VM] * len(outs),
        name="emit",
        compiler_params=pltpu.CompilerParams(vmem_limit_bytes=GRANT),
    )(*arrays)


def local(
    dp,
    image_rows,
    text_states,
    caption_lengths,
    out_grad,
    self_query,
    self_key,
    self_value,
    self_output,
    cross_query,
    cross_key,
    cross_value,
    cross_output,
    mlp_up,
    mlp_down,
    attn_gain,
    attn_shift,
    cross_gain,
    cross_shift,
    mlp_gain,
    mlp_shift,
):
    text = text_states[0]
    bias = jnp.where(jnp.arange(TEXT)[None, :] < caption_lengths[0], 0.0, MASKED)
    x_full, norm_one, q, k, v, self_mix, p0, p1, p2, p3, cross_k, cross_v = front(
        image_rows, self_query, self_key, self_value, text, cross_key, cross_value,
        [attn_gain[None, :], attn_shift[None, :]])
    gains = [item[None, :] for item in (cross_gain, cross_shift, mlp_gain, mlp_shift)]
    (mix_grad, self_back, activated, up_sum, down_sum, up_late, down_late, c_query, c_output, k_grad, v_grad, parts, resid,
     after_cross) = middle(
        dp, x_full, self_mix, out_grad, self_output, cross_query, cross_output, mlp_up, mlp_down,
        cross_k, cross_v, bias, gains)
    arrays = back(
        dp, self_mix, self_back, activated, mlp_down, mix_grad, q, k, v, p0, p1, p2, p3, norm_one,
        self_query, self_key, self_value, image_rows, resid, after_cross, c_query, c_output, up_late, down_late,
        up_sum, down_sum, text, cross_key, cross_value, k_grad, v_grad, parts, attn_gain[None, :])
    layer_out, image_grad, text_grad, *rest = emit(arrays)
    norms, (up, down, cq, co, ck, cv, so, sq, sk, sv) = rest[:6], rest[6:]
    return (layer_out, image_grad, text_grad[None], sq, sk, sv, so, cq, ck, cv, co, up, down, *norms)


def solution(mesh):
    placed = (
        P(("grp", "dp", "tp"), None),
        P(("grp", "dp"), None, None),
        P(("grp", "dp")),
        P(("grp", "dp"), None),
        P(None, "tp"),
        P(None, "tp"),
        P(None, "tp"),
        P("tp", None),
        P(None, "tp"),
        P(None, "tp"),
        P(None, "tp"),
        P("tp", None),
        P(None, "tp"),
        P("tp", None),
        P(),
        P(),
        P(),
        P(),
        P(),
        P(),
    )
    return jax.shard_map(
        functools.partial(local, mesh.shape["dp"]),
        mesh=mesh,
        in_specs=placed,
        out_specs=(
            P(("grp", "dp", "tp"), None),
            P(("grp", "dp", "tp"), None),
            P(("grp", "dp"), None, None),
            P("dp", "tp"),
            P("dp", "tp"),
            P("dp", "tp"),
            P("tp", "dp"),
            P("dp", "tp"),
            P("dp", "tp"),
            P("dp", "tp"),
            P("tp", "dp"),
            P("dp", "tp"),
            P("tp", "dp"),
            P("dp"),
            P("dp"),
            P("dp"),
            P("dp"),
            P("dp"),
            P("dp"),
        ),
        check_vma=False,
    )
```

```python
import functools

import jax
import jax.numpy as jnp
from jax import lax
from jax.experimental import pallas as pl
from jax.experimental.pallas import tpu as pltpu
from jax.sharding import PartitionSpec as P

HEAD = 64
TEXT = 128
EPSILON = 1e-05
MASKED = -1e30
MESH = pl.DeviceIdType.MESH
F32 = jnp.float32
BF16 = jnp.bfloat16
ANY = pl.BlockSpec(memory_space=pl.ANY)
VM = pl.BlockSpec(memory_space=pltpu.VMEM)
GRANT = 60 * 1024 * 1024


def nn(left, right):
    return lax.dot_general(left, right, (((1,), (0,)), ((), ())), preferred_element_type=F32)


def nt(left, right):
    return lax.dot_general(left, right, (((1,), (1,)), ((), ())), preferred_element_type=F32)


def tn(left, right):
    return lax.dot_general(left, right, (((0,), (0,)), ((), ())), preferred_element_type=F32)


def norm_stats(hidden):
    middle = jnp.mean(hidden, axis=-1, keepdims=True)
    centred = hidden - middle
    spread = jnp.mean(centred * centred, axis=-1, keepdims=True)
    rstd = lax.rsqrt(spread + EPSILON)
    return centred * rstd, rstd


def norm_input_grad(xhat, rstd, gain, cotangent):
    scaled = cotangent * gain
    first = jnp.mean(scaled, axis=-1, keepdims=True)
    second = jnp.mean(scaled * xhat, axis=-1, keepdims=True)
    return (scaled - first - xhat * second) * rstd


def fold_rows(value):
    rows = value.shape[0]
    total = value[0:8]
    for start in range(8, rows, 8):
        total = total + value[start : start + 8]
    return total


def lane_keep(shape, part):
    lanes = lax.broadcasted_iota(jnp.int32, shape, 1)
    return (lanes // HEAD) == part


def pick(value, part):
    return jnp.where(lane_keep(value.shape, part), value, jnp.zeros_like(value))


def merge(first, second):
    return jnp.where(lane_keep(first.shape, 0), first, second)


class Piece:
    def __init__(self, place, source, x_buf, z_buf, x_sems, z_sems):
        self.place, self.source, self.x_buf, self.z_buf = place, source, x_buf, z_buf
        self.x_sems, self.z_sems = x_sems, z_sems
        depth = place[1]
        self.line = place[2] == 4
        self.mate = depth + 1 - 2 * lax.rem(depth, 2)
        self.end = (depth == 0) | (depth == 3)
        self.inner = (depth == 1) | (depth == 2)

    def x_copy(self):
        other = 1 - self.place[0]
        return pltpu.make_async_remote_copy(
            self.source.at[:, other], self.x_buf, *self.x_sems,
            device_id={"grp": other}, device_id_type=MESH)

    def z_copies(self):
        _, depth, size = self.place
        return [
            pltpu.make_async_remote_copy(
                self.x_buf.at[lax.rem(depth + r, size)], self.z_buf.at[r - 1],
                self.z_sems[0].at[r - 1], self.z_sems[1].at[r - 1],
                device_id={"dp": lax.rem(depth + r, size)}, device_id_type=MESH)
            for r in range(1, size)
        ]

    def hop(self, parts, slots, sent, got, to):
        return pltpu.make_async_remote_copy(
            self.x_buf.at[parts], self.z_buf.at[slots], self.z_sems[0].at[sent], self.z_sems[1].at[got],
            device_id={"dp": to}, device_id_type=MESH)

    def three(self):
        return self.hop(pl.ds(jnp.where(self.place[1] == 0, 1, 0), 3), pl.ds(0, 3), 0, 0, self.mate)

    def single(self):
        return self.hop(self.mate, 0, 0, 0, self.mate)

    def late(self, i):
        to = 3 - (self.mate if i else self.place[1])
        return self.hop(to, 3, 1 + i, 1, to)

    def start(self):
        self.x_copy().start()

    def add(self):
        self.x_copy().wait_recv()

        @pl.loop(0, self.place[2])
        def _(d):
            mine = self.source[d, self.place[0]]
            self.x_buf[d] = (self.x_buf[d].astype(F32) + mine.astype(F32)).astype(BF16)

    def spread(self):
        if not self.line:
            for copy in self.z_copies():
                copy.start()
            return

        @pl.when(self.end)
        def _():
            self.three().start()

        @pl.when(self.inner)
        def _():
            self.single().start()

    def pass_on(self):
        if not self.line:
            return

        @pl.when(self.inner)
        def _():
            self.three().wait_recv()
            for i in range(2):
                to = 3 - (self.mate if i else self.place[1])
                slot = to - jnp.where(self.place[1] == 1, 1, 0)
                self.x_buf[to] = (self.x_buf[to].astype(F32) + self.z_buf[slot].astype(F32)).astype(BF16)
                self.late(i).start()

    def total(self):
        depth = self.place[1]
        total = self.x_buf[depth].astype(F32)
        if not self.line:
            for copy in self.z_copies():
                copy.wait_recv()
            for r in range(self.place[2] - 1):
                total = total + self.z_buf[r].astype(F32)
            return total.astype(BF16)

        @pl.when(self.end)
        def _():
            self.single().wait_recv()

        self.late(0).wait_recv()
        near = self.z_buf[jnp.where(depth == 2, 2, 0)].astype(F32)
        return (total + near + self.z_buf[3].astype(F32)).astype(BF16)

    def x_end(self):
        self.x_copy().wait_send()

    def z_end(self):
        if not self.line:
            for copy in self.z_copies():
                copy.wait_send()
            return

        @pl.when(self.end)
        def _():
            self.three().wait_send()

        @pl.when(self.inner)
        def _():
            self.single().wait_send()
            self.late(0).wait_send()
            self.late(1).wait_send()


def slots(dp):
    return 4 if dp == 4 else dp - 1


CHUNK = 128
STEPS = 4
SUB = 32


def natural(core, step):
    return 256 * (core + 2 * (step // 2)) + 128 * (step % 2)


def middle_kernel(
    dp, x_full, self_mix, out_grad, wo_h, wcq_h, wco_h, wup_h, wdn_h,
    ck_ref, cv_ref, bias_ref, cg_ref, cs_ref, mg_ref, ms_ref,
    smg_out, sb_out, act_out, uf_out, df_out, ul_out, dcq_out, dco_out, dck_out, dcv_out, dck_over, dcv_over, parts_out, resid_out, ac_out,
    wo, wcq, wco, wup, wdn, smix, og, xr, h1, h2, acc, g2, nf, act, pg, cq, cmix, cqg,
    rr, yr, sst, yst, pbuf, dkv, smg, og2, act2, ug, ux, dx, uz, dz, uf, df, dco, dcq, cox, cqx, parts,
    load_sem, cs_sem, cr_sem, ns_sem, nr_sem, ys_sem, yr_sem, xs_sem, xr_sem, us_sem, ur_sem, ds_sem, dr_sem, os_sem, or_sem, out_sem,
):
    span = 1024 // dp
    per = 256 // span
    rank = lax.axis_index("tp")
    core = lax.rem(rank, 2)
    chip = rank // 2
    pal = rank + 1 - 2 * core
    far = lax.rem(rank + 2, 4)
    group = lax.axis_index("grp")
    depth = lax.axis_index("dp")
    place = (group, depth, dp)
    barrier = pltpu.get_barrier_semaphore()
    for peer in (pal, far):
        pl.semaphore_signal(barrier, inc=1, device_id={"tp": peer}, device_id_type=MESH)
    pl.semaphore_signal(barrier, inc=1, device_id={"grp": 1 - group}, device_id_type=MESH)
    for r in range(1, dp):
        pl.semaphore_signal(barrier, inc=1, device_id={"dp": lax.rem(depth + r, dp)}, device_id_type=MESH)

    loads = []

    def load(src, dst):
        copy = pltpu.make_async_copy(src, dst, load_sem.at[len(loads)])
        copy.start()
        loads.append(copy)

    for k in range(STEPS):
        for c in range(2):
            load(self_mix.at[pl.ds(natural(c, k), CHUNK)], smix.at[pl.ds(k * 256 + c * 128, CHUNK)])
    load(wo_h, wo)
    n_first = len(loads)
    for k in range(STEPS):
        start = pl.multiple_of(256 * (core + 2 * (k // 2)) + 128 * (k % 2), 128)
        load(x_full.at[pl.ds(start, CHUNK)], xr.at[pl.ds(k * CHUNK, CHUNK)])
    load(wcq_h, wcq)
    load(wco_h, wco)
    n_second = len(loads)
    for k in range(STEPS):
        for c in range(2):
            load(out_grad.at[pl.ds(natural(c, k), CHUNK)], og.at[pl.ds(k * 256 + c * 128, CHUNK)])
    load(wup_h, wup)
    load(wdn_h, wdn)
    n_third = len(loads)

    dkv[...] = jnp.zeros_like(dkv)
    parts[...] = jnp.zeros_like(parts)

    def own(k):
        return pl.ds(pl.multiple_of(k * CHUNK, CHUNK), CHUNK)

    def pair(k):
        return pl.ds(pl.multiple_of(k * 256, 256), 256)

    def mine(k):
        return pl.ds(pl.multiple_of(k * 256 + core * CHUNK, CHUNK), CHUNK)

    def red_copy(s, k):
        return pltpu.make_async_remote_copy(
            sst.at[own(k)], rr.at[s, own(k)], cs_sem.at[s, k], cr_sem.at[s, k],
            device_id={"tp": pal}, device_id_type=MESH)

    def far_copy(s, k):
        return pltpu.make_async_remote_copy(
            yst.at[own(k)], yr.at[s, own(k)], ys_sem.at[s, k], yr_sem.at[s, k],
            device_id={"tp": far}, device_id_type=MESH)

    def norm_copy(s, k):
        return pltpu.make_async_remote_copy(
            nf.at[s, mine(k)], nf.at[s, mine(k)], ns_sem.at[s, k], nr_sem.at[s, k],
            device_id={"tp": pal}, device_id_type=MESH)

    def produce(s, k, columns):
        for j, value in columns:
            pbuf[:, j : j + value.shape[1]] = value
        if s > 0:
            red_copy(s - 1, k).wait_send()
        sst[own(k)] = pbuf[pl.ds(pl.multiple_of((1 - core) * CHUNK, CHUNK), CHUNK), :].astype(BF16)
        red_copy(s, k).start()
        acc[own(k)] = pbuf[pl.ds(pl.multiple_of(core * CHUNK, CHUNK), CHUNK), :]

    def finish(s, k):
        if s > 0:
            far_copy(s - 1, k).wait_send()
        red_copy(s, k).wait_recv()
        total = acc[own(k)] + rr[s, own(k)].astype(F32)
        acc[own(k)] = total
        yst[own(k)] = total.astype(BF16)
        far_copy(s, k).start()

    def grads_over(k):
        start = pl.multiple_of(256 * (core + 2 * (k // 2)) + 128 * (k % 2), 128)
        return pltpu.make_async_remote_copy(
            out_grad.at[pl.ds(start, CHUNK)], og2.at[mine(k)], xs_sem.at[0, k], xr_sem.at[0, k],
            device_id={"grp": 1 - group}, device_id_type=MESH)

    def grads_on(k):
        return pltpu.make_async_remote_copy(
            og2.at[mine(k)], og2.at[mine(k)], os_sem.at[k], or_sem.at[k],
            device_id={"tp": pal}, device_id_type=MESH)

    def act_over(k):
        columns = pl.ds(pl.multiple_of((1 - group) * 512, 512), 512)
        return pltpu.make_async_remote_copy(
            act.at[pair(k), columns], act2.at[pair(k)], xs_sem.at[1, k], xr_sem.at[1, k],
            device_id={"grp": 1 - group}, device_id_type=MESH)

    def sub(k, r):
        return pl.ds(pl.multiple_of(k * CHUNK + r * SUB, SUB), SUB)

    def msub(k, r):
        return pl.ds(pl.multiple_of(k * 256 + core * CHUNK + r * SUB, SUB), SUB)

    for copy in loads[:n_first]:
        copy.wait()
    pl.semaphore_wait(barrier, 2 + dp)
    for k in range(STEPS):
        grads_over(k).start()

    @pl.loop(0, STEPS)
    def _(k):
        rows = smix[pair(k), :]
        produce(0, k, [(j, nn(rows, wo[:, j : j + 512])) for j in (0, 512)])

        @pl.when(k > 0)
        def _():
            finish(0, k - 1)

    finish(0, STEPS - 1)
    for copy in loads[n_first:n_second]:
        copy.wait()

    scale = HEAD ** (-0.5)

    def act_copy(k):
        return pltpu.make_async_copy(act.at[pair(k)], act_out.at[pair(k)], out_sem.at[2 + k])

    def settle(src, dst, k, c, slot):
        start = pl.multiple_of(256 * (c + 2 * (k // 2)) + 128 * (k % 2), 128)
        return pltpu.make_async_copy(
            src.at[pl.ds(pl.multiple_of(k * 256 + c * CHUNK, CHUNK), CHUNK)],
            dst.at[pl.ds(start, CHUNK)], out_sem.at[slot + 2 * k + c])

    @pl.loop(0, STEPS)
    def _(k):
        far_copy(0, k).wait_recv()
        for r in range(CHUNK // SUB):
            hidden = xr[sub(k, r)].astype(F32) + acc[sub(k, r)] + yr[0, sub(k, r)].astype(F32)
            h1[sub(k, r)] = hidden
            xhat, _ = norm_stats(hidden)
            nf[0, msub(k, r)] = (xhat * cg_ref[...] + cs_ref[...]).astype(BF16)
        norm_copy(0, k).start()
        grads_over(k).wait_recv()
        grads_on(k).start()

        @pl.when(k > 0)
        def _():
            finish(1, k - 1)

        norm_copy(0, k).wait_recv()
        cq[pair(k)] = nn(nf[0, pair(k)], wcq[...]).astype(BF16)
        for slab in range(2):
            lanes = slice(slab * 128, slab * 128 + 128)
            query = cq[pair(k), lanes]
            key, value = ck_ref[:, lanes], cv_ref[:, lanes]
            mixed = []
            for part in range(2):
                scores = nt(pick(query, part), key) * scale + bias_ref[...]
                shifted = jnp.exp(scores - jnp.max(scores, axis=-1, keepdims=True))
                probs = shifted / jnp.sum(shifted, axis=-1, keepdims=True)
                mixed.append(nn(probs.astype(BF16), value))
            cmix[pair(k), lanes] = merge(*mixed).astype(BF16)
        rows = cmix[pair(k), :]
        produce(1, k, [(j, nn(rows, wco[:, j : j + 512])) for j in (0, 512)])

    finish(1, STEPS - 1)
    for copy in loads[n_second:n_third]:
        copy.wait()

    @pl.loop(0, STEPS)
    def _(k):
        far_copy(1, k).wait_recv()
        for r in range(CHUNK // SUB):
            hidden = h1[sub(k, r)] + acc[sub(k, r)] + yr[1, sub(k, r)].astype(F32)
            h2[sub(k, r)] = hidden
            xhat, _ = norm_stats(hidden)
            nf[1, msub(k, r)] = (xhat * mg_ref[...] + ms_ref[...]).astype(BF16)
        norm_copy(1, k).start()

        @pl.when(k > 0)
        def _():
            finish(2, k - 1)

        norm_copy(1, k).wait_recv()
        rows = nf[1, pair(k)]
        grads = og[pair(k), :]
        for j in range(0, 1024, 256):
            cols = slice(j, j + 256)
            pre = nn(rows, wup[:, cols])
            back = nt(grads, wdn[cols, :])
            square = pre * pre
            bend = jnp.tanh(0.7978845608028654 * pre * (1.0 + 0.044715 * square))
            half = 0.5 * (1.0 + bend)
            act[pair(k), cols] = (pre * half).astype(BF16)
            slope = half + 0.5 * pre * (1.0 - bend * bend) * (
                0.7978845608028654 * (1.0 + 3 * 0.044715 * square))
            pg[pair(k), cols] = (back * slope).astype(BF16)
        act_over(k).start()
        rows = pg[pair(k), :]
        produce(2, k, [(j, nt(rows, wup[j : j + 256, :])) for j in range(0, 1024, 256)])
        act_copy(k).start()

    finish(2, STEPS - 1)

    def up_piece(c):
        z = jnp.minimum(c, 2)
        return Piece(place, ug.at[c], ux.at[c], uz.at[z], (us_sem.at[0, c], ur_sem.at[0, c]),
                     (ds_sem.at[0, z], dr_sem.at[0, z]))

    def down_piece(c):
        return Piece(place, None, dx.at[c], dz.at[c], None, (ds_sem.at[1, c], dr_sem.at[1, c]))

    def down_grad(c):
        mine_left = act[:, pl.ds(pl.multiple_of(group * 512 + c * 128, 128), 128)]
        other_left = act2[:, pl.ds(pl.multiple_of(c * 128, 128), 128)]
        for m in range(4):
            lanes = slice(m * 256, m * 256 + 256)
            value = (tn(mine_left, og[:, lanes]) + tn(other_left, og2[:, lanes])).astype(BF16)
            for u in range(per):
                dx[c, m * per + u] = value[:, u * span : (u + 1) * span]
        down_piece(c).spread()

    def own_rows(k):
        return jnp.where(k // 2 == chip, 1.0, 0.0)

    @pl.loop(0, STEPS)
    def _(k):
        at = pl.multiple_of(k * 256, 256)
        right = pg[:, pl.ds(at, 256)]
        for m in range(4):
            value = tn(nf[1, :, m * 256 : m * 256 + 256], right).astype(BF16)
            for u in range(per):
                ug[k, m * per + u, 0] = value[u * span : u * span + span // 2]
                ug[k, m * per + u, 1] = value[u * span + span // 2 : (u + 1) * span]
        up_piece(k).start()

        @pl.when(k == 1)
        def _():
            for i in range(STEPS):
                act_over(i).wait_recv()
                grads_on(i).wait_recv()

        @pl.when(k > 0)
        def _():
            down_grad(k - 1)

        @pl.when(k > 1)
        def _():
            down_piece(k - 2).pass_on()

        @pl.when(k == 3)
        def _():
            up_piece(0).add()
            up_piece(0).spread()

        far_copy(2, k).wait_recv()
        keep = own_rows(k)
        for r in range(CHUNK // SUB):
            third = acc[sub(k, r)] + yr[2, sub(k, r)].astype(F32)
            xhat, rstd = norm_stats(h2[sub(k, r)])
            parts[2] += fold_rows(third * xhat) * keep
            parts[3] += fold_rows(third) * keep
            resid = og[msub(k, r)].astype(F32) + norm_input_grad(xhat, rstd, mg_ref[...], third)
            g2[sub(k, r)] = resid
            nf[2, msub(k, r)] = resid.astype(BF16)
        norm_copy(2, k).start()

        @pl.when(k > 0)
        def _():
            finish(3, k - 1)

        norm_copy(2, k).wait_recv()
        mix_grad = nt(nf[2, pair(k)], wco[...]).astype(BF16)
        for slab in range(2):
            lanes = slice(slab * 128, slab * 128 + 128)
            query = cq[pair(k), lanes]
            grad = mix_grad[:, lanes]
            key, value = ck_ref[:, lanes], cv_ref[:, lanes]
            moved = []
            for part in range(2):
                one_q, one_g = pick(query, part), pick(grad, part)
                scores = nt(one_q, key) * scale + bias_ref[...]
                shifted = jnp.exp(scores - jnp.max(scores, axis=-1, keepdims=True))
                probs = shifted / jnp.sum(shifted, axis=-1, keepdims=True)
                prob_grad = nt(one_g, value)
                inner = jnp.sum(probs * prob_grad, axis=-1, keepdims=True)
                score_grad = (probs * (prob_grad - inner)).astype(BF16)
                moved.append(nn(score_grad, key) * scale)
                dkv[0, :, lanes] += tn(score_grad, one_q)
                dkv[1, :, lanes] += tn(probs.astype(BF16), one_g)
            cqg[pair(k), lanes] = merge(*moved).astype(BF16)
        rows = cqg[pair(k), :]
        produce(3, k, [(j, nt(rows, wcq[j : j + 512, :])) for j in (0, 512)])

    finish(3, STEPS - 1)
    dck_out[...] = (dkv[0] * scale).astype(BF16)
    dcv_out[...] = dkv[1].astype(BF16)
    down_grad(STEPS - 1)
    captions = [
        pltpu.make_async_remote_copy(
            src, dst, xs_sem.at[2, i], xr_sem.at[2, i], device_id={"grp": 1 - group}, device_id_type=MESH)
        for i, (src, dst) in enumerate([(dck_out, dck_over), (dcv_out, dcv_over)])
    ]
    for copy in captions:
        copy.start()

    def quarter(k):
        return pl.ds(pl.multiple_of(k * per, per), per)

    def query_over(k):
        return pltpu.make_async_remote_copy(
            dcq.at[quarter(k), 1 - group], cqx.at[quarter(k)], us_sem.at[1, k], ur_sem.at[1, k],
            device_id={"grp": 1 - group}, device_id_type=MESH)

    def output_over(k):
        return pltpu.make_async_remote_copy(
            dco.at[quarter(k), 1 - group], cox.at[quarter(k)], us_sem.at[2, k], ur_sem.at[2, k],
            device_id={"grp": 1 - group}, device_id_type=MESH)

    def down_give(k):
        return pltpu.make_async_remote_copy(
            df.at[k, group], df.at[k, group], us_sem.at[3, k], ur_sem.at[3, k],
            device_id={"grp": 1 - group}, device_id_type=MESH)

    @pl.loop(0, STEPS)
    def _(k):
        at = pl.multiple_of(k * 256, 256)
        value = tn(nf[0, :, pl.ds(at, 256)], cqg[...]).astype(BF16)
        for u in range(per):
            dcq[k * per + u, 0] = value[u * span : u * span + span // 2]
            dcq[k * per + u, 1] = value[u * span + span // 2 : (u + 1) * span]
        value = tn(cmix[...], nf[2, :, pl.ds(at, 256)]).astype(BF16)
        for u in range(per):
            dco[k * per + u, 0] = value[:128, u * span : (u + 1) * span]
            dco[k * per + u, 1] = value[128:, u * span : (u + 1) * span]

        query_over(k).start()
        output_over(k).start()

    @pl.loop(0, STEPS)
    def _(k):
        @pl.when(k < 2)
        def _():
            down_piece(jnp.minimum(k + 2, 3)).pass_on()
            up_piece(jnp.minimum(k + 1, 2)).add()
            up_piece(jnp.minimum(k + 1, 2)).spread()

        @pl.when(k > 0)
        def _():
            up_piece(jnp.maximum(k - 1, 0)).pass_on()

        df[k, group] = down_piece(k).total()
        down_give(k).start()
        far_copy(3, k).wait_recv()
        keep = own_rows(k)
        for r in range(CHUNK // SUB):
            second = acc[sub(k, r)] + yr[3, sub(k, r)].astype(F32)
            xhat, rstd = norm_stats(h1[sub(k, r)])
            parts[0] += fold_rows(second * xhat) * keep
            parts[1] += fold_rows(second) * keep
            resid = g2[sub(k, r)] + norm_input_grad(xhat, rstd, cg_ref[...], second)
            g2[sub(k, r)] = resid
            nf[3, msub(k, r)] = resid.astype(BF16)
        norm_copy(3, k).start()
        norm_copy(3, k).wait_recv()
        smg[pair(k)] = nt(nf[3, pair(k)], wo[...]).astype(BF16)
        for c in range(2):
            settle(smg, smg_out, k, c, 10).start()
            settle(nf.at[3], sb_out, k, c, 18).start()

    mine_rows = pl.ds(pl.multiple_of(chip * 256, 256), 256)
    final = [
        pltpu.make_async_copy(g2.at[mine_rows], resid_out, out_sem.at[26]),
        pltpu.make_async_copy(h2.at[mine_rows], ac_out, out_sem.at[27]),
    ]
    for copy in final:
        copy.start()
    up_piece(3).add()
    for k in range(STEPS):
        query_over(k).wait_recv()
        output_over(k).wait_recv()

    @pl.loop(0, dp)
    def _(d):
        cqx[d] = (cqx[d].astype(F32) + dcq[d, group].astype(F32)).astype(BF16)
        cox[d] = (cox[d].astype(F32) + dco[d, group].astype(F32)).astype(BF16)

    for c in range(3):
        uf[c] = up_piece(c).total()
    for k in range(STEPS):
        down_give(k).wait_recv()
    late = [
        pltpu.make_async_copy(cqx, dcq_out, out_sem.at[28]),
        pltpu.make_async_copy(cox, dco_out, out_sem.at[29]),
        pltpu.make_async_copy(uf, uf_out, out_sem.at[30]),
        pltpu.make_async_copy(df, df_out, out_sem.at[31]),
        pltpu.make_async_copy(ux.at[3], ul_out, out_sem.at[0]),
    ]
    for copy in late:
        copy.start()
    for copy in captions:
        copy.wait()
    parts_out[...] = parts[...]
    for k in range(STEPS):
        red_copy(3, k).wait_send()
        far_copy(3, k).wait_send()
        for s in range(4):
            norm_copy(s, k).wait_send()
        act_copy(k).wait()
        grads_over(k).wait_send()
        grads_on(k).wait_send()
        act_over(k).wait_send()
        query_over(k).wait_send()
        output_over(k).wait_send()
        down_give(k).wait_send()
        for c in range(2):
            settle(smg, smg_out, k, c, 10).wait()
            settle(nf.at[3], sb_out, k, c, 18).wait()
    for c in range(4):
        up_piece(c).x_end()
        down_piece(c).z_end()
    for c in range(3):
        up_piece(c).z_end()
    for copy in final + late:
        copy.wait()


def middle(dp, x_full, self_mix, out_grad, wo, wcq, wco, wup, wdn, ck, cv, bias, gains):
    full = jax.ShapeDtypeStruct((1024, 1024), BF16)
    narrow = jax.ShapeDtypeStruct((1024, 256), BF16)
    short = jax.ShapeDtypeStruct((128, 256), BF16)
    block = jax.ShapeDtypeStruct((256, 1024), F32)
    part = 1024 // dp
    rows, columns = (part // 2, 256), (128, part)
    outs = [
        narrow, full, full] + [
        jax.ShapeDtypeStruct(item, BF16)
        for item in ((3,) + rows, (4, 2) + columns, (dp,) + rows, (dp,) + rows, (dp,) + columns)
    ] + [short, short, short, short,
        jax.ShapeDtypeStruct((4, 8, 1024), F32), block, block,
    ]
    out_specs = [ANY] * 8 + [VM] * 5 + [ANY] * 2
    vm = pltpu.VMEM
    dma = pltpu.SemaphoreType.DMA
    scratch = [
        vm((256, 1024), BF16), vm((1024, 256), BF16), vm((256, 1024), BF16), vm((1024, 1024), BF16),
        vm((1024, 1024), BF16), vm((1024, 256), BF16), vm((1024, 1024), BF16), vm((512, 1024), BF16),
        vm((512, 1024), F32), vm((512, 1024), F32), vm((512, 1024), F32), vm((512, 1024), F32),
        vm((4, 1024, 1024), BF16), vm((1024, 1024), BF16), vm((1024, 1024), BF16),
        vm((1024, 256), BF16), vm((1024, 256), BF16), vm((1024, 256), BF16),
        vm((4, 512, 1024), BF16), vm((4, 512, 1024), BF16), vm((512, 1024), BF16), vm((512, 1024), BF16),
        vm((256, 1024), F32), vm((2, 128, 256), F32), vm((1024, 256), BF16),
        vm((1024, 1024), BF16), vm((1024, 512), BF16),
        vm((4, dp, 2) + rows, BF16), vm((4, dp) + rows, BF16), vm((4, dp) + columns, BF16),
        vm((3, slots(dp)) + rows, BF16), vm((4, slots(dp)) + columns, BF16), vm((3,) + rows, BF16), vm((4, 2) + columns, BF16),
        vm((dp, 2) + columns, BF16), vm((dp, 2) + rows, BF16), vm((dp,) + columns, BF16), vm((dp,) + rows, BF16),
        vm((4, 8, 1024), F32),
        dma((32,)), dma((4, 4)), dma((4, 4)), dma((4, 4)), dma((4, 4)), dma((4, 4)), dma((4, 4)),
        dma((3, 4)), dma((3, 4)), dma((4, 4)), dma((4, 4)), dma((2, 4, dp - 1)), dma((2, 4, dp - 1)),
        dma((4,)), dma((4,)), dma((32,)),
    ]
    return pl.pallas_call(
        functools.partial(middle_kernel, dp),
        out_shape=outs,
        in_specs=[ANY] * 8 + [VM] * 7,
        out_specs=out_specs,
        scratch_shapes=scratch,
        name="middle",
        compiler_params=pltpu.CompilerParams(
            collective_id=1, has_side_effects=True, vmem_limit_bytes=GRANT),
    )(x_full, self_mix, out_grad, wo, wcq, wco, wup, wdn, ck, cv, bias, *gains)


def front_kernel(
    x_own, wq_h, wk_h, wv_h, text_h, wck_h, wcv_h, ag_ref, as_ref,
    x_out, n1_out, q_out, k_out, v_out, mix_out, p0_out, p1_out, p2_out, p3_out, text_out, ck_out, cv_out,
    xf, n1, q, k, v, mix, p0, p1, p2, p3, wq, wk, wv, text, wck, wcv, theirs,
    load_sem, text_s, text_r, y_s, y_r, c_s, c_r, f_s, f_r, out_sem,
):
    rank = lax.axis_index("tp")
    core = lax.rem(rank, 2)
    pal = rank + 1 - 2 * core
    far = lax.rem(rank + 2, 4)
    beyond = lax.rem(pal + 2, 4)
    barrier = pltpu.get_barrier_semaphore()
    for peer in (pal, far):
        pl.semaphore_signal(barrier, inc=1, device_id={"tp": peer}, device_id_type=MESH)
    group = lax.axis_index("grp")
    pl.semaphore_signal(barrier, inc=1, device_id={"grp": 1 - group}, device_id_type=MESH)
    captions = pltpu.make_async_remote_copy(
        text_h, theirs, text_s.at[0], text_r.at[0], device_id={"grp": 1 - group}, device_id_type=MESH)
    loads = [
        pltpu.make_async_copy(src, dst, load_sem.at[i])
        for i, (src, dst) in enumerate([
            (x_own, xf.at[pl.ds(pl.multiple_of(rank * 256, 256), 256)]),
            (text_h, text), (wck_h, wck), (wcv_h, wcv), (wq_h, wq), (wk_h, wk), (wv_h, wv)])
    ]
    for copy in loads:
        copy.start()

    def part(block, i, size):
        return pl.ds(pl.multiple_of(block * 256 + i * size, size), size)

    across = [
        pltpu.make_async_remote_copy(
            x_own.at[pl.ds(i * 64, 64)], xf.at[part(rank, i, 64)], y_s.at[i], y_r.at[i],
            device_id={"tp": far}, device_id_type=MESH)
        for i in range(4)
    ]
    beside = pltpu.make_async_remote_copy(
        x_own, xf.at[part(rank, 0, 256)], c_s.at[0], c_r.at[0], device_id={"tp": pal}, device_id_type=MESH)
    onward = [
        pltpu.make_async_remote_copy(
            xf.at[part(far, i, 64)], xf.at[part(far, i, 64)], f_s.at[i], f_r.at[i],
            device_id={"tp": pal}, device_id_type=MESH)
        for i in range(4)
    ]
    pl.semaphore_wait(barrier, 3)
    for copy in across:
        copy.start()
    beside.start()
    captions.start()

    for copy in loads[1:4]:
        copy.wait()
    ck_out[...] = nn(text[...], wck[...]).astype(BF16)
    cv_out[...] = nn(text[...], wcv[...]).astype(BF16)
    for copy in loads[4:] + loads[:1]:
        copy.wait()

    def project(block, i):
        for r in range(4):
            rows = pl.ds(pl.multiple_of(block * 256 + i * 128 + r * 32, 32), 32)
            xhat, _ = norm_stats(xf[rows].astype(F32))
            n1[rows] = (xhat * ag_ref[...] + as_ref[...]).astype(BF16)
        rows = part(block, i, 128)
        value = n1[rows]
        q[rows] = (nn(value, wq[...]).astype(BF16) * 0.125).astype(BF16)
        k[rows] = nn(value, wk[...]).astype(BF16)
        v[rows] = nn(value, wv[...]).astype(BF16)

    def both(block):
        @pl.loop(0, 2)
        def _(i):
            project(block, i)

    both(rank)
    beside.wait_recv()
    both(pal)
    for half in range(2):
        for i in (2 * half, 2 * half + 1):
            across[i].wait_recv()
            onward[i].start()
        project(far, half)
        for i in (2 * half, 2 * half + 1):
            onward[i].wait_recv()
        project(beyond, half)
    outs = [
        pltpu.make_async_copy(src, dst, out_sem.at[i])
        for i, (src, dst) in enumerate([(xf, x_out), (n1, n1_out), (q, q_out), (k, k_out), (v, v_out)])
    ]
    for copy in outs:
        copy.start()

    captions.wait_recv()
    caption_out = pltpu.make_async_copy(theirs, text_out, out_sem.at[10])
    caption_out.start()

    kept = (p0, p1, p2, p3)
    below = lax.broadcasted_iota(jnp.int32, (256, 256), 0) >= lax.broadcasted_iota(jnp.int32, (256, 256), 1)

    @pl.loop(0, 2)
    def _(slab):
        lanes = pl.ds(pl.multiple_of(slab * 128, 128), 128)
        for i in range(4):
            done, end = i * 256, i * 256 + 256
            query = q[done:end, lanes]
            mixed = []
            for half in range(2):
                one = pick(query, half)
                diag = jnp.where(below, nt(one, k[done:end, lanes]), MASKED)
                peak = jnp.max(diag, axis=-1, keepdims=True)
                if i:
                    past = nt(one, k[0:done, lanes])
                    peak = jnp.maximum(peak, jnp.max(past, axis=-1, keepdims=True))
                    past = jnp.exp(past - peak)
                diag = jnp.exp(diag - peak)
                total = jnp.sum(diag, axis=-1, keepdims=True)
                if i:
                    total = total + jnp.sum(past, axis=-1, keepdims=True)
                inverse = 1.0 / total
                probs = (diag * inverse).astype(BF16)
                kept[i][slab * 2 + half, :, done:end] = probs
                out = nn(probs, v[done:end, lanes])
                if i:
                    probs = (past * inverse).astype(BF16)
                    kept[i][slab * 2 + half, :, 0:done] = probs
                    out = out + nn(probs, v[0:done, lanes])
                mixed.append(out)
            mix[done:end, lanes] = merge(*mixed).astype(BF16)

    tail = [
        pltpu.make_async_copy(src, dst, out_sem.at[5 + i])
        for i, (src, dst) in enumerate(
            [(mix, mix_out), (p0, p0_out), (p1, p1_out), (p2, p2_out), (p3, p3_out)])
    ]
    for copy in tail:
        copy.start()
    for copy in across + [beside, captions] + onward:
        copy.wait_send()
    for copy in outs + tail + [caption_out]:
        copy.wait()


def front(x_own, wq, wk, wv, text, wck, wcv, gains):
    full = ((1024, 1024), BF16)
    narrow = ((1024, 256), BF16)
    short = ((128, 256), BF16)
    probs = [((4, 256, 256 * (i + 1)), BF16) for i in range(4)]
    vm = pltpu.VMEM
    dma = pltpu.SemaphoreType.DMA
    return pl.pallas_call(
        front_kernel,
        out_shape=[jax.ShapeDtypeStruct(*item) for item in [full, full, narrow, narrow, narrow, narrow] + probs + [((128, 1024), BF16), short, short]],
        in_specs=[ANY] * 7 + [VM] * 2,
        out_specs=[ANY] * 11 + [VM] * 2,
        scratch_shapes=[vm(*item) for item in [full, full, narrow, narrow, narrow, narrow] + probs
                        + [narrow] * 3 + [((128, 1024), BF16), narrow, narrow, ((128, 1024), BF16)]]
        + [dma((8,)), dma((1,)), dma((1,)), dma((4,)), dma((4,)), dma((1,)), dma((1,)), dma((4,)), dma((4,)), dma((12,))],
        name="front",
        compiler_params=pltpu.CompilerParams(
            collective_id=2, has_side_effects=True, vmem_limit_bytes=GRANT),
    )(x_own, wq, wk, wv, text, wck, wcv, *gains)


def back_kernel(dp, *refs):
    refs = list(refs)

    def take(n):
        taken, refs[:n] = refs[:n], []
        return taken

    (smix_h, sb_h, act_h, wdn_h, smg_h, q_h, k_h, v_h, p0_h, p1_h, p2_h, p3_h, n1_h, wq_h, wk_h, wv_h,
     x_own, resid_h, ac_h, dcq_h, dco_h, ul_h, uf_h, df_h) = take(24)
    text, text_over, wck, wcv, dck, dcv, dck_over, dcv_over, parts_in, ag_ref = take(10)
    layer_out, image_grad, text_out, norm_out, up_o, dn_o, cq_o, co_o, so_o, ck_o, cv_o, sq_o, sk_o, sv_o = take(14)
    (smix, sb, act, wdn, smg, q, k, v, p0, p1, p2, p3, n1, wqkv, xo, resid, ac) = take(17)
    so_g, ck_g, cv_g, self_g = take(4)
    x_bufs, self_x, z_bufs, self_z = take(6), take(1)[0], take(6), take(1)[0]
    (dqkv, dkv, acc, sst, rr, yst, yr, tpart, t_st, t_rr, t_yst, t_yr, t_fin, npart, n_tp, nsum, n_all) = take(17)
    (load_sem, xs, xr, zs, zr, gs, gr, cs_sem, cr_sem, ys_sem, yr_sem, t_s, t_r, n_s, n_r, m_s, m_r) = take(17)

    rank = lax.axis_index("tp")
    group = lax.axis_index("grp")
    depth = lax.axis_index("dp")
    core = lax.rem(rank, 2)
    chip = rank // 2
    pal = rank + 1 - 2 * core
    far = lax.rem(rank + 2, 4)
    others = [(g, r) for g in range(2) for r in range(dp) if g or r]
    barrier = pltpu.get_barrier_semaphore()
    for r in range(1, 4):
        pl.semaphore_signal(barrier, inc=1, device_id={"tp": lax.rem(rank + r, 4)}, device_id_type=MESH)

    def at_other(g, r):
        return {"grp": lax.rem(group + g, 2), "dp": lax.rem(depth + r, dp)}

    for g, r in others:
        pl.semaphore_signal(barrier, inc=1, device_id=at_other(g, r), device_id_type=MESH)

    pairs = [
        (ul_h, x_bufs[3]), (dcq_h, x_bufs[0]), (dco_h, x_bufs[1]),
        (smix_h, smix), (sb_h, sb), (act_h, act), (wdn_h, wdn),
        (smg_h, smg), (q_h, q), (k_h, k), (v_h, v), (p0_h, p0), (p1_h, p1), (p2_h, p2), (p3_h, p3), (n1_h, n1)]
    pairs += [
        (weight.at[:, h * 128 : h * 128 + 128], wqkv.at[:, h * 384 + i * 128 : h * 384 + i * 128 + 128])
        for h in range(2) for i, weight in enumerate((wq_h, wk_h, wv_h))]
    pairs += [(x_own, xo), (resid_h, resid), (ac_h, ac)]
    pairs += [(uf_h.at[c], up_o.at[c, group]) for c in range(3)] + [(df_h, dn_o)]
    loads = [pltpu.make_async_copy(src, dst, load_sem.at[i]) for i, (src, dst) in enumerate(pairs)]
    for copy in loads:
        copy.start()

    place = (group, depth, dp)

    def piece(n, source=None):
        return Piece(place, source, x_bufs[n], z_bufs[n], (xs.at[n], xr.at[n]), (zs.at[n], zr.at[n]))

    def self_piece(h, i):
        n = 3 * h + i
        return Piece(place, self_g.at[n], self_x.at[n], self_z.at[n], (xs.at[6 + n], xr.at[6 + n]),
                     (zs.at[6 + n], zr.at[6 + n]))

    def give(n, src, out):
        return pltpu.make_async_remote_copy(
            src, out, gs.at[n], gr.at[n], device_id={"grp": 1 - group}, device_id_type=MESH)

    cq_p, co_p, so_p, ul_p, ck_p, cv_p = [
        piece(n, source) for n, source in enumerate((None, None, so_g, None, None, None))]
    halves = [(cq_p, cq_o), (co_p, co_o), (so_p, so_o), (ul_p, up_o.at[3]), (ck_p, ck_o), (cv_p, cv_o)]
    halves += [(self_piece(h, i), out.at[h]) for h in range(2) for i, out in enumerate((sq_o, sk_o, sv_o))]
    gives = [give(n, out.at[group], out.at[group]) for n, (_, out) in enumerate(halves)]
    early = [give(12 + c, uf_h.at[c], up_o.at[c, group]) for c in range(3)]

    def finish(n):
        one, out = halves[n]
        out[group] = one.total()
        gives[n].start()

    pl.semaphore_wait(barrier, 3 + len(others))
    for copy in loads[:3]:
        copy.wait()
    ul_p.spread()
    cq_p.spread()
    co_p.spread()

    scale = HEAD ** (-0.5)
    depth_rows = 1024 // dp
    per = 256 // depth_rows

    def caption_grad(one, ref, ours, theirs):
        for m in range(4):
            lanes = slice(m * 256, m * 256 + 256)
            value = (tn(text[:, lanes], ours[...]) + tn(text_over[:, lanes], theirs[...])).astype(BF16)
            for u in range(per):
                part = value[u * depth_rows : (u + 1) * depth_rows]
                ref[m * per + u, 0] = part[: depth_rows // 2]
                ref[m * per + u, 1] = part[depth_rows // 2 :]

        @pl.loop(0, dp)
        def _(d):
            one.x_buf[d] = ref[d, group]

        one.spread()

    def own(i):
        return pl.ds(pl.multiple_of(i * CHUNK, CHUNK), CHUNK)

    class Scatter:
        def __init__(self, n):
            self.n = n

        def red(self, i):
            n = self.n
            return pltpu.make_async_remote_copy(
                sst.at[n, own(i)], rr.at[n, own(i)], cs_sem.at[n, i], cr_sem.at[n, i],
                device_id={"tp": pal}, device_id_type=MESH)

        def far(self, j):
            n = self.n
            return pltpu.make_async_remote_copy(
                yst.at[n, own(j)], yr.at[n, own(j)], ys_sem.at[n, j], yr_sem.at[n, j],
                device_id={"tp": far}, device_id_type=MESH)

        def put(self, i, theirs, ours):
            sst[self.n, own(i)] = theirs.astype(BF16)
            self.red(i).start()
            acc[self.n, own(i)] = ours

        def send(self, j):
            i = 2 * (1 - chip) + j
            self.red(i).wait_recv()
            yst[self.n, own(j)] = (acc[self.n, own(i)] + rr[self.n, own(i)].astype(F32)).astype(BF16)
            self.far(j).start()

        def keep(self, j):
            self.red(2 * chip + j).wait_recv()
            self.far(j).wait_recv()

        def value(self, j, r):
            i = 2 * chip + j
            rows = pl.ds(pl.multiple_of(i * CHUNK + r * SUB, SUB), SUB)
            near = pl.ds(j * CHUNK + r * SUB, SUB)
            return acc[self.n, rows] + rr[self.n, rows].astype(F32) + yr[self.n, near].astype(F32)

        def end(self):
            for i in range(4):
                self.red(i).wait_send()
            for j in range(2):
                self.far(j).wait_send()

    layer, first = Scatter(0), Scatter(1)
    def sequence(step):
        return lax.rem(2 * (1 - chip) + step, 4)

    for copy in loads[3:5]:
        copy.wait()
    for d in range(dp):
        value = tn(smix[...], sb[:, d * depth_rows : (d + 1) * depth_rows]).astype(BF16)
        so_g[d, 0] = value[:128]
        so_g[d, 1] = value[128:]
    so_p.start()
    for copy in early:
        copy.start()
    for copy in loads[5:7]:
        copy.wait()

    @pl.loop(0, 4)
    def _(step):
        i = sequence(step)
        theirs = act[pl.ds(pl.multiple_of(i * 256 + (1 - core) * CHUNK, CHUNK), CHUNK), :]
        ours = act[pl.ds(pl.multiple_of(i * 256 + core * CHUNK, CHUNK), CHUNK), :]
        layer.put(i, nn(theirs, wdn[...]), nn(ours, wdn[...]))

        @pl.when((step > 0) & (step < 3))
        def _():
            layer.send(step - 1)

    caption_grad(ck_p, ck_g, dck, dck_over)
    caption_grad(cv_p, cv_g, dcv, dcv_over)
    tpart[...] = nt(dck[...], wck[...]) + nt(dcv[...], wcv[...])

    def t_rows(c):
        return pl.ds(pl.multiple_of(c * 64, 64), 64)

    t_st[...] = tpart[t_rows(1 - core)].astype(BF16)
    t_red = pltpu.make_async_remote_copy(
        t_st, t_rr, t_s.at[0], t_r.at[0], device_id={"tp": pal}, device_id_type=MESH)
    t_red.start()

    for copy in loads[7:16]:
        copy.wait()
    dkv[...] = jnp.zeros_like(dkv)
    kept = (p0, p1, p2, p3)

    @pl.loop(0, 2)
    def _(slab):
        lanes = pl.ds(pl.multiple_of(slab * 128, 128), 128)
        for i in range(4):
            begin, end = i * 256, i * 256 + 256
            query, grad = q[begin:end, lanes], smg[begin:end, lanes]
            product = grad.astype(F32) * smix[begin:end, lanes].astype(F32)
            moved = []
            for half in range(2):
                one_q, one_g = pick(query, half), pick(grad, half)
                inner = jnp.sum(pick(product, half), axis=-1, keepdims=True)
                probs = kept[i][slab * 2 + half]
                prob_grad = nt(one_g, v[0:end, lanes])
                score_grad = (probs.astype(F32) * (prob_grad - inner)).astype(BF16)
                moved.append(nn(score_grad, k[0:end, lanes]))
                dkv[0, 0:end, lanes] += tn(score_grad, one_q)
                dkv[1, 0:end, lanes] += tn(probs, one_g)
            moved = (merge(*moved) * scale).astype(BF16)
            dqkv[begin:end, pl.ds(pl.multiple_of(slab * 384, 128), 128)] = moved
            if i == 1:
                @pl.when(slab == 0)
                def _():
                    ul_p.pass_on()

                @pl.when(slab == 1)
                def _():
                    ck_p.pass_on()
                    finish(3)
            if i == 2:
                @pl.when(slab == 0)
                def _():
                    so_p.add()
                    so_p.spread()
                    cq_p.pass_on()

                @pl.when(slab == 1)
                def _():
                    cv_p.pass_on()
                    finish(0)
            if i == 3:
                @pl.when(slab == 0)
                def _():
                    co_p.pass_on()

                @pl.when(slab == 1)
                def _():
                    so_p.pass_on()
                    finish(1)

        dqkv[:, pl.ds(pl.multiple_of(slab * 384 + 128, 128), 128)] = dkv[0, :, lanes].astype(BF16)
        dqkv[:, pl.ds(pl.multiple_of(slab * 384 + 256, 128), 128)] = dkv[1, :, lanes].astype(BF16)
        right = dqkv[:, pl.ds(pl.multiple_of(slab * 384, 128), 384)]
        for m in range(4):
            value = tn(n1[:, m * 256 : m * 256 + 256], right).astype(BF16)
            for u in range(per):
                part = value[u * depth_rows : (u + 1) * depth_rows]
                for n in range(3):
                    self_g[slab * 3 + n, m * per + u, 0] = part[: depth_rows // 2, n * 128 : n * 128 + 128]
                    self_g[slab * 3 + n, m * per + u, 1] = part[depth_rows // 2 :, n * 128 : n * 128 + 128]
        for n in range(3):
            self_piece(slab, n).start()

    t_red.wait_recv()
    t_yst[...] = (tpart[t_rows(core)] + t_rr[...].astype(F32)).astype(BF16)
    t_far = pltpu.make_async_remote_copy(
        t_yst, t_yr, t_s.at[1], t_r.at[1], device_id={"tp": far}, device_id_type=MESH)
    t_far.start()
    for copy in loads[16:]:
        copy.wait()

    @pl.loop(0, 4)
    def _(step):
        i = sequence(step)

        def partial(c):
            start = pl.multiple_of(256 * (c + 2 * (i // 2)) + 128 * lax.rem(i, 2), 128)
            rows = pl.ds(start, CHUNK)
            return nt(dqkv[rows], wqkv[...])

        first.put(i, partial(1 - core), partial(core))

        @pl.when((step > 0) & (step < 3))
        def _():
            first.send(step - 1)

        @pl.when(step < 3)
        def _():
            self_piece(0, step).add()
            self_piece(0, step).spread()

    for n in range(3):
        self_piece(0, n).pass_on()
    for n in (4, 5, 2):
        finish(n)
    for j in range(2):
        layer.keep(j)
        for r in range(CHUNK // SUB):
            rows = slice(j * CHUNK + r * SUB, j * CHUNK + r * SUB + SUB)
            layer_out[rows] = (ac[rows] + layer.value(j, r)).astype(BF16)

    for n in range(3):
        self_piece(1, n).add()
        self_piece(1, n).spread()
    t_far.wait_recv()
    t_fin[t_rows(core)] = (t_yst[...].astype(F32) + t_yr[...].astype(F32)).astype(BF16)
    t_share = pltpu.make_async_remote_copy(
        t_fin.at[t_rows(core)], t_fin.at[t_rows(core)], t_s.at[2], t_r.at[2],
        device_id={"tp": pal}, device_id_type=MESH)
    t_share.start()
    for n in range(6, 9):
        finish(n)
    for n in range(3):
        self_piece(1, n).pass_on()

    npart[...] = jnp.zeros_like(npart)
    for j in range(2):
        first.keep(j)
        for r in range(CHUNK // SUB):
            rows = slice(j * CHUNK + r * SUB, j * CHUNK + r * SUB + SUB)
            given = first.value(j, r)
            xhat, rstd = norm_stats(xo[rows].astype(F32))
            npart[0] += fold_rows(given * xhat)
            npart[1] += fold_rows(given)
            image_grad[rows] = resid[rows] + norm_input_grad(xhat, rstd, ag_ref[...], given)

    def line(ref, i):
        return jnp.sum(ref[i], axis=0, keepdims=True)

    n_tp[rank] = jnp.concatenate(
        [line(npart, 0), line(npart, 1)] + [line(parts_in, i) for i in range(4)]
        + [jnp.zeros((2, 1024), F32)], axis=0)
    n_copies = [
        pltpu.make_async_remote_copy(
            n_tp.at[rank], n_tp.at[rank], n_s.at[r - 1], n_r.at[r - 1],
            device_id={"tp": lax.rem(rank + r, 4)}, device_id_type=MESH)
        for r in range(1, 4)
    ]
    for copy in n_copies:
        copy.start()
    for n in range(9, 12):
        finish(n)
    for copy in n_copies:
        copy.wait_recv()
    summed = n_tp[0] + n_tp[1] + n_tp[2] + n_tp[3]
    for d in range(dp):
        nsum[d] = summed[:, d * depth_rows : (d + 1) * depth_rows]
    slot = group * dp + depth
    m_copies = [
        pltpu.make_async_remote_copy(
            nsum.at[lax.rem(depth + r, dp)], n_all.at[slot], m_s.at[i], m_r.at[i],
            device_id=at_other(g, r), device_id_type=MESH)
        for i, (g, r) in enumerate(others)
    ]
    for copy in m_copies:
        copy.start()
    n_all[slot] = nsum[depth]

    for copy in m_copies:
        copy.wait_recv()
    total = n_all[0]
    for i in range(1, 2 * dp):
        total = total + n_all[i]
    norm_out[...] = total
    t_share.wait_recv()
    text_out[...] = t_fin[...]
    for copy in m_copies + n_copies + [t_red, t_far, t_share]:
        copy.wait_send()
    layer.end()
    first.end()
    for n, (one, _) in enumerate(halves):
        if n not in (0, 1, 3, 4, 5):
            one.x_end()
        one.z_end()
        gives[n].wait()
    for copy in early:
        copy.wait()


def back(dp, *operands):
    part = 1024 // dp
    full = ((1024, 1024), BF16)
    narrow = ((1024, 256), BF16)
    probs = [((4, 256, 256 * (i + 1)), BF16) for i in range(4)]
    rows, columns = (part // 2, 256), (128, part)
    block = ((256, 1024), F32)
    kinds = [rows, columns, columns, rows, rows, rows]
    slabs = (part // 2, 128)
    outs = [((256, 1024), BF16), block, ((128, 1024), BF16), ((8, part), F32), ((4, 2) + rows, BF16), ((4, 2) + columns, BF16)]
    outs += [((2,) + s, BF16) for s in (rows, columns, columns, rows, rows)] + [((2, 2) + slabs, BF16)] * 3
    scratch = (
        [narrow, full, full, full] + [narrow] * 4 + probs + [full] + [((1024, 768), BF16)]
        + [((256, 1024), BF16), block, block]
        + [((dp, 2) + s, BF16) for s in (columns, rows, rows)] + [((6, dp, 2) + slabs, BF16)]
        + [((dp,) + s, BF16) for s in kinds] + [((6, dp) + slabs, BF16)]
        + [((slots(dp),) + s, BF16) for s in kinds] + [((6, slots(dp)) + slabs, BF16)]
        + [((1024, 768), BF16)]
        + [((2, 1024, 256), F32), ((2, 512, 1024), F32), ((2, 512, 1024), BF16), ((2, 512, 1024), BF16),
           ((2, 256, 1024), BF16), ((2, 256, 1024), BF16), ((128, 1024), F32),
           ((64, 1024), BF16), ((64, 1024), BF16), ((64, 1024), BF16), ((64, 1024), BF16), ((128, 1024), BF16),
           ((2, 8, 1024), F32), ((4, 8, 1024), F32), ((dp, 8, part), F32), ((2 * dp, 8, part), F32)]
    )
    dma = pltpu.SemaphoreType.DMA
    many = 2 * dp - 1
    sems = [dma((32,)), dma((12,)), dma((12,)), dma((12, dp - 1)), dma((12, dp - 1)), dma((15,)), dma((15,)),
            dma((2, 4)), dma((2, 4)), dma((2, 2)), dma((2, 2)), dma((3,)), dma((3,)), dma((3,)), dma((3,)),
            dma((many,)), dma((many,))]
    return pl.pallas_call(
        functools.partial(back_kernel, dp),
        out_shape=[jax.ShapeDtypeStruct(*item) for item in outs],
        in_specs=[ANY] * 24 + [VM] * 10,
        out_specs=[VM] * len(outs),
        scratch_shapes=[pltpu.VMEM(*item) for item in scratch] + sems,
        name="back",
        compiler_params=pltpu.CompilerParams(
            collective_id=3, has_side_effects=True, vmem_limit_bytes=GRANT),
    )(*operands)


def emit_kernel(n, *refs):
    layer, image, text, norms, up, down = refs[:6]
    outs = refs[n:]
    outs[0][...] = layer[...]
    outs[1][...] = image[...]
    outs[2][...] = text[...].astype(F32)
    for i in range(6):
        outs[3 + i][...] = norms[i]
    rows, columns = up.shape[2], down.shape[2]
    for c in range(4):
        for h in range(2):
            outs[9][h * rows : (h + 1) * rows, c * 256 : c * 256 + 256] = up[c, h].astype(F32)
            at = h * 512 + c * columns
            outs[10][at : at + columns, :] = down[c, h].astype(F32)
    for given, out in zip(refs[6 : n - 3], outs[11:]):
        rows = given.shape[1]
        for h in range(2):
            out[h * rows : (h + 1) * rows] = given[h].astype(F32)
    for given, out in zip(refs[n - 3 : n], outs[-3:]):
        rows = given.shape[2]
        for s in range(2):
            for h in range(2):
                out[h * rows : (h + 1) * rows, s * 128 : s * 128 + 128] = given[s, h].astype(F32)


def emit(arrays):
    part = arrays[3].shape[1]
    shapes = [(part,)] * 6 + [(part, 1024), (1024, part)]
    outs = [jax.ShapeDtypeStruct((256, 1024), BF16), jax.ShapeDtypeStruct((256, 1024), F32), jax.ShapeDtypeStruct((128, 1024), F32)]
    outs += [jax.ShapeDtypeStruct(item, F32) for item in shapes]
    outs += [jax.ShapeDtypeStruct((2 * item.shape[1], item.shape[2]), F32) for item in arrays[6:-3]]
    outs += [jax.ShapeDtypeStruct((part, 256), F32)] * 3
    return pl.pallas_call(
        functools.partial(emit_kernel, len(arrays)),
        out_shape=outs,
        in_specs=[VM] * len(arrays),
        out_specs=[VM] * len(outs),
        name="emit",
        compiler_params=pltpu.CompilerParams(vmem_limit_bytes=GRANT),
    )(*arrays)


def local(
    dp,
    image_rows,
    text_states,
    caption_lengths,
    out_grad,
    self_query,
    self_key,
    self_value,
    self_output,
    cross_query,
    cross_key,
    cross_value,
    cross_output,
    mlp_up,
    mlp_down,
    attn_gain,
    attn_shift,
    cross_gain,
    cross_shift,
    mlp_gain,
    mlp_shift,
):
    text = text_states[0]
    bias = jnp.where(jnp.arange(TEXT)[None, :] < caption_lengths[0], 0.0, MASKED)
    x_full, norm_one, q, k, v, self_mix, p0, p1, p2, p3, other_text, cross_k, cross_v = front(
        image_rows, self_query, self_key, self_value, text, cross_key, cross_value,
        [attn_gain[None, :], attn_shift[None, :]])
    gains = [item[None, :] for item in (cross_gain, cross_shift, mlp_gain, mlp_shift)]
    (mix_grad, self_back, activated, up_sum, down_sum, up_late, c_query, c_output, k_grad, v_grad, k_over, v_over, parts, resid,
     after_cross) = middle(
        dp, x_full, self_mix, out_grad, self_output, cross_query, cross_output, mlp_up, mlp_down,
        cross_k, cross_v, bias, gains)
    arrays = back(
        dp, self_mix, self_back, activated, mlp_down, mix_grad, q, k, v, p0, p1, p2, p3, norm_one,
        self_query, self_key, self_value, image_rows, resid, after_cross, c_query, c_output, up_late,
        up_sum, down_sum, text, other_text, cross_key, cross_value, k_grad, v_grad, k_over, v_over, parts, attn_gain[None, :])
    layer_out, image_grad, text_grad, *rest = emit(arrays)
    norms, (up, down, cq, co, so, ck, cv, sq, sk, sv) = rest[:6], rest[6:]
    return (layer_out, image_grad, text_grad[None], sq, sk, sv, so, cq, ck, cv, co, up, down, *norms)


def solution(mesh):
    placed = (
        P(("grp", "dp", "tp"), None),
        P(("grp", "dp"), None, None),
        P(("grp", "dp")),
        P(("grp", "dp"), None),
        P(None, "tp"),
        P(None, "tp"),
        P(None, "tp"),
        P("tp", None),
        P(None, "tp"),
        P(None, "tp"),
        P(None, "tp"),
        P("tp", None),
        P(None, "tp"),
        P("tp", None),
        P(),
        P(),
        P(),
        P(),
        P(),
        P(),
    )
    return jax.shard_map(
        functools.partial(local, mesh.shape["dp"]),
        mesh=mesh,
        in_specs=placed,
        out_specs=(
            P(("grp", "dp", "tp"), None),
            P(("grp", "dp", "tp"), None),
            P(("grp", "dp"), None, None),
            P("dp", "tp"),
            P("dp", "tp"),
            P("dp", "tp"),
            P("tp", "dp"),
            P("dp", "tp"),
            P("dp", "tp"),
            P("dp", "tp"),
            P("tp", "dp"),
            P("dp", "tp"),
            P("tp", "dp"),
            P("dp"),
            P("dp"),
            P("dp"),
            P("dp"),
            P("dp"),
            P("dp"),
        ),
        check_vma=False,
    )
```

```python
import functools

import jax
import jax.numpy as jnp
from jax import lax
from jax.experimental import pallas as pl
from jax.experimental.pallas import tpu as pltpu
from jax.sharding import PartitionSpec as P

HEAD = 64
TEXT = 128
EPSILON = 1e-05
MASKED = -1e30
MESH = pl.DeviceIdType.MESH
F32 = jnp.float32
BF16 = jnp.bfloat16
ANY = pl.BlockSpec(memory_space=pl.ANY)
VM = pl.BlockSpec(memory_space=pltpu.VMEM)
GRANT = 60 * 1024 * 1024


def nn(left, right):
    return lax.dot_general(left, right, (((1,), (0,)), ((), ())), preferred_element_type=F32)


def nt(left, right):
    return lax.dot_general(left, right, (((1,), (1,)), ((), ())), preferred_element_type=F32)


def tn(left, right):
    return lax.dot_general(left, right, (((0,), (0,)), ((), ())), preferred_element_type=F32)


def norm_stats(hidden):
    middle = jnp.mean(hidden, axis=-1, keepdims=True)
    centred = hidden - middle
    spread = jnp.mean(centred * centred, axis=-1, keepdims=True)
    rstd = lax.rsqrt(spread + EPSILON)
    return centred * rstd, rstd


def norm_input_grad(xhat, rstd, gain, cotangent):
    scaled = cotangent * gain
    first = jnp.mean(scaled, axis=-1, keepdims=True)
    second = jnp.mean(scaled * xhat, axis=-1, keepdims=True)
    return (scaled - first - xhat * second) * rstd


def fold_rows(value):
    rows = value.shape[0]
    total = value[0:8]
    for start in range(8, rows, 8):
        total = total + value[start : start + 8]
    return total


def lane_keep(shape, part):
    lanes = lax.broadcasted_iota(jnp.int32, shape, 1)
    return (lanes // HEAD) == part


def pick(value, part):
    return jnp.where(lane_keep(value.shape, part), value, jnp.zeros_like(value))


def merge(first, second):
    return jnp.where(lane_keep(first.shape, 0), first, second)


class Piece:
    def __init__(self, place, source, x_buf, z_buf, x_sems, z_sems):
        self.place, self.source, self.x_buf, self.z_buf = place, source, x_buf, z_buf
        self.x_sems, self.z_sems = x_sems, z_sems
        depth = place[1]
        self.line = place[2] == 4
        self.mate = depth + 1 - 2 * lax.rem(depth, 2)
        self.end = (depth == 0) | (depth == 3)
        self.inner = (depth == 1) | (depth == 2)

    def x_copy(self):
        other = 1 - self.place[0]
        return pltpu.make_async_remote_copy(
            self.source.at[:, other], self.x_buf, *self.x_sems,
            device_id={"grp": other}, device_id_type=MESH)

    def z_copies(self):
        _, depth, size = self.place
        return [
            pltpu.make_async_remote_copy(
                self.x_buf.at[lax.rem(depth + r, size)], self.z_buf.at[r - 1],
                self.z_sems[0].at[r - 1], self.z_sems[1].at[r - 1],
                device_id={"dp": lax.rem(depth + r, size)}, device_id_type=MESH)
            for r in range(1, size)
        ]

    def hop(self, parts, slots, sent, got, to):
        return pltpu.make_async_remote_copy(
            self.x_buf.at[parts], self.z_buf.at[slots], self.z_sems[0].at[sent], self.z_sems[1].at[got],
            device_id={"dp": to}, device_id_type=MESH)

    def three(self):
        return self.hop(pl.ds(jnp.where(self.place[1] == 0, 1, 0), 3), pl.ds(0, 3), 0, 0, self.mate)

    def single(self):
        return self.hop(self.mate, 0, 0, 0, self.mate)

    def late(self, i):
        to = 3 - (self.mate if i else self.place[1])
        return self.hop(to, 3, 1 + i, 1, to)

    def start(self):
        self.x_copy().start()

    def add(self):
        self.x_copy().wait_recv()

        @pl.loop(0, self.place[2])
        def _(d):
            mine = self.source[d, self.place[0]]
            self.x_buf[d] = (self.x_buf[d].astype(F32) + mine.astype(F32)).astype(BF16)

    def spread(self):
        if not self.line:
            for copy in self.z_copies():
                copy.start()
            return

        @pl.when(self.end)
        def _():
            self.three().start()

        @pl.when(self.inner)
        def _():
            self.single().start()

    def pass_on(self):
        if not self.line:
            return

        @pl.when(self.inner)
        def _():
            self.three().wait_recv()
            for i in range(2):
                to = 3 - (self.mate if i else self.place[1])
                slot = to - jnp.where(self.place[1] == 1, 1, 0)
                self.x_buf[to] = (self.x_buf[to].astype(F32) + self.z_buf[slot].astype(F32)).astype(BF16)
                self.late(i).start()

    def total(self):
        depth = self.place[1]
        total = self.x_buf[depth].astype(F32)
        if not self.line:
            for copy in self.z_copies():
                copy.wait_recv()
            for r in range(self.place[2] - 1):
                total = total + self.z_buf[r].astype(F32)
            return total.astype(BF16)

        @pl.when(self.end)
        def _():
            self.single().wait_recv()

        self.late(0).wait_recv()
        near = self.z_buf[jnp.where(depth == 2, 2, 0)].astype(F32)
        return (total + near + self.z_buf[3].astype(F32)).astype(BF16)

    def x_end(self):
        self.x_copy().wait_send()

    def z_end(self):
        if not self.line:
            for copy in self.z_copies():
                copy.wait_send()
            return

        @pl.when(self.end)
        def _():
            self.three().wait_send()

        @pl.when(self.inner)
        def _():
            self.single().wait_send()
            self.late(0).wait_send()
            self.late(1).wait_send()


def slots(dp):
    return 4 if dp == 4 else dp - 1


CHUNK = 128
STEPS = 4
SUB = 32


def natural(core, step):
    return 256 * (core + 2 * (step // 2)) + 128 * (step % 2)


def middle_kernel(
    dp, x_full, self_mix, out_grad, wo_h, wcq_h, wco_h, wup_h, wdn_h,
    ck_ref, cv_ref, bias_ref, cg_ref, cs_ref, mg_ref, ms_ref,
    smg_out, sb_out, lay_out, uf_out, df_out, dcq_out, dco_out, dck_out, dcv_out, dck_over, dcv_over, parts_out, resid_out, ac_out,
    wo, wcq, wco, wup, wdn, smix, og, xr, h1, h2, acc, g2, nf, act, pg, cq, cmix, cqg,
    rr, yr, sst, yst, pbuf, dkv, smg, og2, act2, ug, ux, dx, uz, dz, uf, df, dco, dcq, cox, cqx, parts,
    load_sem, cs_sem, cr_sem, ns_sem, nr_sem, ys_sem, yr_sem, xs_sem, xr_sem, us_sem, ur_sem, ds_sem, dr_sem, os_sem, or_sem, ls_sem, lr_sem, out_sem,
):
    span = 1024 // dp
    per = 256 // span
    rank = lax.axis_index("tp")
    core = lax.rem(rank, 2)
    chip = rank // 2
    pal = rank + 1 - 2 * core
    far = lax.rem(rank + 2, 4)
    group = lax.axis_index("grp")
    depth = lax.axis_index("dp")
    place = (group, depth, dp)
    barrier = pltpu.get_barrier_semaphore()
    for peer in (pal, far):
        pl.semaphore_signal(barrier, inc=1, device_id={"tp": peer}, device_id_type=MESH)
    pl.semaphore_signal(barrier, inc=1, device_id={"grp": 1 - group}, device_id_type=MESH)
    for r in range(1, dp):
        pl.semaphore_signal(barrier, inc=1, device_id={"dp": lax.rem(depth + r, dp)}, device_id_type=MESH)

    loads = []

    def load(src, dst):
        loads.append(pltpu.make_async_copy(src, dst, load_sem.at[len(loads)]))

    for k in range(STEPS):
        for c in range(2):
            load(self_mix.at[pl.ds(natural(c, k), CHUNK)], smix.at[pl.ds(k * 256 + c * 128, CHUNK)])
    load(wo_h, wo)
    n_first = len(loads)
    for copy in loads:
        copy.start()
    for k in range(STEPS):
        start = pl.multiple_of(256 * (core + 2 * (k // 2)) + 128 * (k % 2), 128)
        load(x_full.at[pl.ds(start, CHUNK)], xr.at[pl.ds(k * CHUNK, CHUNK)])
    load(wcq_h, wcq)
    load(wco_h, wco)
    n_second = len(loads)
    for k in range(STEPS):
        for c in range(2):
            load(out_grad.at[pl.ds(natural(c, k), CHUNK)], og.at[pl.ds(k * 256 + c * 128, CHUNK)])
    load(wup_h, wup)
    load(wdn_h, wdn)
    n_third = len(loads)

    dkv[...] = jnp.zeros_like(dkv)
    parts[...] = jnp.zeros_like(parts)

    def own(k):
        return pl.ds(pl.multiple_of(k * CHUNK, CHUNK), CHUNK)

    def pair(k):
        return pl.ds(pl.multiple_of(k * 256, 256), 256)

    def mine(k):
        return pl.ds(pl.multiple_of(k * 256 + core * CHUNK, CHUNK), CHUNK)

    def red_copy(s, k):
        return pltpu.make_async_remote_copy(
            sst.at[own(k)], rr.at[s, own(k)], cs_sem.at[s, k], cr_sem.at[s, k],
            device_id={"tp": pal}, device_id_type=MESH)

    def far_copy(s, k):
        return pltpu.make_async_remote_copy(
            yst.at[own(k)], yr.at[s, own(k)], ys_sem.at[s, k], yr_sem.at[s, k],
            device_id={"tp": far}, device_id_type=MESH)

    def norm_copy(s, k):
        return pltpu.make_async_remote_copy(
            nf.at[s, mine(k)], nf.at[s, mine(k)], ns_sem.at[s, k], nr_sem.at[s, k],
            device_id={"tp": pal}, device_id_type=MESH)

    def produce(s, k, columns):
        for j, value in columns:
            pbuf[:, j : j + value.shape[1]] = value
        if s > 0:
            red_copy(s - 1, k).wait_send()
        sst[own(k)] = pbuf[pl.ds(pl.multiple_of((1 - core) * CHUNK, CHUNK), CHUNK), :].astype(BF16)
        red_copy(s, k).start()
        acc[own(k)] = pbuf[pl.ds(pl.multiple_of(core * CHUNK, CHUNK), CHUNK), :]

    def finish(s, k):
        if s > 0:
            far_copy(s - 1, k).wait_send()
        red_copy(s, k).wait_recv()
        total = acc[own(k)] + rr[s, own(k)].astype(F32)
        acc[own(k)] = total
        yst[own(k)] = total.astype(BF16)
        far_copy(s, k).start()

    def grads_over(k):
        start = pl.multiple_of(256 * (core + 2 * (k // 2)) + 128 * (k % 2), 128)
        return pltpu.make_async_remote_copy(
            out_grad.at[pl.ds(start, CHUNK)], og2.at[mine(k)], xs_sem.at[0, k], xr_sem.at[0, k],
            device_id={"grp": 1 - group}, device_id_type=MESH)

    def grads_on(k):
        return pltpu.make_async_remote_copy(
            og2.at[mine(k)], og2.at[mine(k)], os_sem.at[k], or_sem.at[k],
            device_id={"tp": pal}, device_id_type=MESH)

    def act_over(k):
        columns = pl.ds(pl.multiple_of((1 - group) * 512, 512), 512)
        return pltpu.make_async_remote_copy(
            act.at[pair(k), columns], act2.at[pair(k)], xs_sem.at[1, k], xr_sem.at[1, k],
            device_id={"grp": 1 - group}, device_id_type=MESH)

    def sub(k, r):
        return pl.ds(pl.multiple_of(k * CHUNK + r * SUB, SUB), SUB)

    def msub(k, r):
        return pl.ds(pl.multiple_of(k * 256 + core * CHUNK + r * SUB, SUB), SUB)

    pl.semaphore_wait(barrier, 2 + dp)
    for copy in loads[:n_first]:
        copy.wait()
    for copy in loads[n_first:]:
        copy.start()
    for k in range(STEPS):
        grads_over(k).start()

    @pl.loop(0, STEPS)
    def _(k):
        rows = smix[pair(k), :]
        produce(0, k, [(j, nn(rows, wo[:, j : j + 512])) for j in (0, 512)])

        @pl.when(k > 0)
        def _():
            finish(0, k - 1)

    finish(0, STEPS - 1)
    for copy in loads[n_first:n_second]:
        copy.wait()

    scale = HEAD ** (-0.5)

    def settle(src, dst, k, c, slot):
        start = pl.multiple_of(256 * (c + 2 * (k // 2)) + 128 * (k % 2), 128)
        return pltpu.make_async_copy(
            src.at[pl.ds(pl.multiple_of(k * 256 + c * CHUNK, CHUNK), CHUNK)],
            dst.at[pl.ds(start, CHUNK)], out_sem.at[slot + 2 * k + c])

    @pl.loop(0, STEPS)
    def _(k):
        far_copy(0, k).wait_recv()
        for r in range(CHUNK // SUB):
            hidden = xr[sub(k, r)].astype(F32) + acc[sub(k, r)] + yr[0, sub(k, r)].astype(F32)
            h1[sub(k, r)] = hidden
            xhat, _ = norm_stats(hidden)
            nf[0, msub(k, r)] = (xhat * cg_ref[...] + cs_ref[...]).astype(BF16)
        norm_copy(0, k).start()
        grads_over(k).wait_recv()
        grads_on(k).start()

        @pl.when(k > 0)
        def _():
            finish(1, k - 1)

        norm_copy(0, k).wait_recv()
        cq[pair(k)] = nn(nf[0, pair(k)], wcq[...]).astype(BF16)
        for slab in range(2):
            lanes = slice(slab * 128, slab * 128 + 128)
            query = cq[pair(k), lanes]
            key, value = ck_ref[:, lanes], cv_ref[:, lanes]
            mixed = []
            for part in range(2):
                scores = nt(pick(query, part), key) * scale + bias_ref[...]
                shifted = jnp.exp(scores - jnp.max(scores, axis=-1, keepdims=True))
                probs = shifted / jnp.sum(shifted, axis=-1, keepdims=True)
                mixed.append(nn(probs.astype(BF16), value))
            cmix[pair(k), lanes] = merge(*mixed).astype(BF16)
        rows = cmix[pair(k), :]
        produce(1, k, [(j, nn(rows, wco[:, j : j + 512])) for j in (0, 512)])

    finish(1, STEPS - 1)
    for copy in loads[n_second:n_third]:
        copy.wait()

    @pl.loop(0, STEPS)
    def _(k):
        far_copy(1, k).wait_recv()
        for r in range(CHUNK // SUB):
            hidden = h1[sub(k, r)] + acc[sub(k, r)] + yr[1, sub(k, r)].astype(F32)
            h2[sub(k, r)] = hidden
            xhat, _ = norm_stats(hidden)
            nf[1, msub(k, r)] = (xhat * mg_ref[...] + ms_ref[...]).astype(BF16)
        norm_copy(1, k).start()

        @pl.when(k > 0)
        def _():
            finish(2, k - 1)

        norm_copy(1, k).wait_recv()
        rows = nf[1, pair(k)]
        grads = og[pair(k), :]
        for j in range(0, 1024, 256):
            cols = slice(j, j + 256)
            pre = nn(rows, wup[:, cols])
            back = nt(grads, wdn[cols, :])
            square = pre * pre
            bend = jnp.tanh(0.7978845608028654 * pre * (1.0 + 0.044715 * square))
            half = 0.5 * (1.0 + bend)
            act[pair(k), cols] = (pre * half).astype(BF16)
            slope = half + 0.5 * pre * (1.0 - bend * bend) * (
                0.7978845608028654 * (1.0 + 3 * 0.044715 * square))
            pg[pair(k), cols] = (back * slope).astype(BF16)
        act_over(k).start()
        rows = pg[pair(k), :]
        produce(2, k, [(j, nt(rows, wup[j : j + 256, :])) for j in range(0, 1024, 256)])

    finish(2, STEPS - 1)

    def up_piece(c):
        return Piece(place, ug.at[c], ux.at[c], uz.at[c], (us_sem.at[0, c], ur_sem.at[0, c]),
                     (ds_sem.at[0, c], dr_sem.at[0, c]))

    def down_piece(c):
        return Piece(place, None, dx.at[c], dz.at[c], None, (ds_sem.at[1, c], dr_sem.at[1, c]))

    def down_grad(c):
        mine_left = act[:, pl.ds(pl.multiple_of(group * 512 + c * 128, 128), 128)]
        other_left = act2[:, pl.ds(pl.multiple_of(c * 128, 128), 128)]
        for m in range(4):
            lanes = slice(m * 256, m * 256 + 256)
            value = (tn(mine_left, og[:, lanes]) + tn(other_left, og2[:, lanes])).astype(BF16)
            for u in range(per):
                dx[c, m * per + u] = value[:, u * span : (u + 1) * span]
        down_piece(c).spread()

    def own_rows(k):
        return jnp.where(k // 2 == chip, 1.0, 0.0)

    @pl.loop(0, STEPS)
    def _(k):
        at = pl.multiple_of(k * 256, 256)
        right = pg[:, pl.ds(at, 256)]
        for m in range(4):
            value = tn(nf[1, :, m * 256 : m * 256 + 256], right).astype(BF16)
            for u in range(per):
                ug[k, m * per + u, 0] = value[u * span : u * span + span // 2]
                ug[k, m * per + u, 1] = value[u * span + span // 2 : (u + 1) * span]
        up_piece(k).start()

        @pl.when(k == 1)
        def _():
            for i in range(STEPS):
                act_over(i).wait_recv()
                grads_on(i).wait_recv()

        @pl.when((k == 1) | (k == 2))
        def _():
            down_grad(2 * k - 2)
            down_grad(2 * k - 1)

        @pl.when(k == 2)
        def _():
            down_piece(0).pass_on()

        @pl.when(k == 3)
        def _():
            up_piece(0).add()
            up_piece(0).spread()
            down_piece(1).pass_on()

        far_copy(2, k).wait_recv()
        keep = own_rows(k)
        for r in range(CHUNK // SUB):
            third = acc[sub(k, r)] + yr[2, sub(k, r)].astype(F32)
            xhat, rstd = norm_stats(h2[sub(k, r)])
            parts[2] += fold_rows(third * xhat) * keep
            parts[3] += fold_rows(third) * keep
            resid = og[msub(k, r)].astype(F32) + norm_input_grad(xhat, rstd, mg_ref[...], third)
            g2[sub(k, r)] = resid
            nf[2, msub(k, r)] = resid.astype(BF16)
        norm_copy(2, k).start()

        @pl.when(k > 0)
        def _():
            finish(3, k - 1)

        norm_copy(2, k).wait_recv()
        mix_grad = nt(nf[2, pair(k)], wco[...]).astype(BF16)
        for slab in range(2):
            lanes = slice(slab * 128, slab * 128 + 128)
            query = cq[pair(k), lanes]
            grad = mix_grad[:, lanes]
            key, value = ck_ref[:, lanes], cv_ref[:, lanes]
            moved = []
            for part in range(2):
                one_q, one_g = pick(query, part), pick(grad, part)
                scores = nt(one_q, key) * scale + bias_ref[...]
                shifted = jnp.exp(scores - jnp.max(scores, axis=-1, keepdims=True))
                probs = shifted / jnp.sum(shifted, axis=-1, keepdims=True)
                prob_grad = nt(one_g, value)
                inner = jnp.sum(probs * prob_grad, axis=-1, keepdims=True)
                score_grad = (probs * (prob_grad - inner)).astype(BF16)
                moved.append(nn(score_grad, key) * scale)
                dkv[0, :, lanes] += tn(score_grad, one_q)
                dkv[1, :, lanes] += tn(probs.astype(BF16), one_g)
            cqg[pair(k), lanes] = merge(*moved).astype(BF16)
        rows = cqg[pair(k), :]
        produce(3, k, [(j, nt(rows, wcq[j : j + 512, :])) for j in (0, 512)])

    finish(3, STEPS - 1)
    dck_out[...] = (dkv[0] * scale).astype(BF16)
    dcv_out[...] = dkv[1].astype(BF16)
    captions = [
        pltpu.make_async_remote_copy(
            src, dst, xs_sem.at[2, i], xr_sem.at[2, i], device_id={"grp": 1 - group}, device_id_type=MESH)
        for i, (src, dst) in enumerate([(dck_out, dck_over), (dcv_out, dcv_over)])
    ]
    for copy in captions:
        copy.start()

    def quarter(k):
        return pl.ds(pl.multiple_of(k * per, per), per)

    def query_over(k):
        return pltpu.make_async_remote_copy(
            dcq.at[quarter(k), 1 - group], cqx.at[quarter(k)], us_sem.at[1, k], ur_sem.at[1, k],
            device_id={"grp": 1 - group}, device_id_type=MESH)

    def output_over(k):
        return pltpu.make_async_remote_copy(
            dco.at[quarter(k), 1 - group], cox.at[quarter(k)], us_sem.at[2, k], ur_sem.at[2, k],
            device_id={"grp": 1 - group}, device_id_type=MESH)

    def down_give(k):
        return pltpu.make_async_remote_copy(
            df.at[k, group], df.at[k, group], us_sem.at[3, k], ur_sem.at[3, k],
            device_id={"grp": 1 - group}, device_id_type=MESH)

    @pl.loop(0, STEPS)
    def _(k):
        at = pl.multiple_of(k * 256, 256)
        value = tn(nf[0, :, pl.ds(at, 256)], cqg[...]).astype(BF16)
        for u in range(per):
            dcq[k * per + u, 0] = value[u * span : u * span + span // 2]
            dcq[k * per + u, 1] = value[u * span + span // 2 : (u + 1) * span]
        value = tn(cmix[...], nf[2, :, pl.ds(at, 256)]).astype(BF16)
        for u in range(per):
            dco[k * per + u, 0] = value[:128, u * span : (u + 1) * span]
            dco[k * per + u, 1] = value[128:, u * span : (u + 1) * span]

        query_over(k).start()
        output_over(k).start()

    def layer_red(k):
        return pltpu.make_async_remote_copy(
            yr.at[0, own(k)], rr.at[0, own(k)], ls_sem.at[k], lr_sem.at[k],
            device_id={"tp": pal}, device_id_type=MESH)

    @pl.loop(0, STEPS)
    def _(k):
        rows = act[pair(k), :]
        for j in (0, 512):
            pbuf[:, j : j + 512] = nn(rows, wdn[:, j : j + 512])
        yr[0, own(k)] = pbuf[pl.ds(pl.multiple_of((1 - core) * CHUNK, CHUNK), CHUNK), :].astype(BF16)
        layer_red(k).start()
        h2[own(k)] = h2[own(k)] * own_rows(k) + pbuf[pl.ds(pl.multiple_of(core * CHUNK, CHUNK), CHUNK), :]

    mine_rows = pl.ds(pl.multiple_of(chip * 256, 256), 256)
    their_rows = pl.ds(pl.multiple_of((1 - chip) * 256, 256), 256)
    cross_copy = pltpu.make_async_copy(h2.at[mine_rows], ac_out, out_sem.at[27])
    layer_copy = pltpu.make_async_copy(xr.at[their_rows], lay_out, out_sem.at[2])
    summed = [
        pltpu.make_async_copy(cqx, dcq_out, out_sem.at[28]),
        pltpu.make_async_copy(cox, dco_out, out_sem.at[29]),
    ]

    @pl.loop(0, STEPS)
    def _(k):
        @pl.when(k == 0)
        def _():
            down_piece(2).pass_on()
            for c in (1, 2):
                up_piece(c).add()
                up_piece(c).spread()
            down_piece(3).pass_on()

        @pl.when(k == 1)
        def _():
            up_piece(3).add()
            up_piece(3).spread()
            up_piece(0).pass_on()

        @pl.when(k == 2)
        def _():
            up_piece(1).pass_on()

        df[k, group] = down_piece(k).total()
        down_give(k).start()
        layer_red(k).wait_recv()
        total = h2[own(k)] + rr[0, own(k)].astype(F32)
        h2[own(k)] = total
        xr[own(k)] = total.astype(BF16)

        @pl.when(k == 3)
        def _():
            for i in range(STEPS):
                query_over(i).wait_recv()
                output_over(i).wait_recv()

            @pl.loop(0, dp)
            def _(d):
                cqx[d] = (cqx[d].astype(F32) + dcq[d, group].astype(F32)).astype(BF16)
                cox[d] = (cox[d].astype(F32) + dco[d, group].astype(F32)).astype(BF16)

            for copy in summed + [cross_copy, layer_copy]:
                copy.start()
            up_piece(2).pass_on()
            up_piece(3).pass_on()

        far_copy(3, k).wait_recv()
        keep = own_rows(k)
        for r in range(CHUNK // SUB):
            second = acc[sub(k, r)] + yr[3, sub(k, r)].astype(F32)
            xhat, rstd = norm_stats(h1[sub(k, r)])
            parts[0] += fold_rows(second * xhat) * keep
            parts[1] += fold_rows(second) * keep
            resid = g2[sub(k, r)] + norm_input_grad(xhat, rstd, cg_ref[...], second)
            g2[sub(k, r)] = resid
            nf[3, msub(k, r)] = resid.astype(BF16)
        norm_copy(3, k).start()
        norm_copy(3, k).wait_recv()
        smg[pair(k)] = nt(nf[3, pair(k)], wo[...]).astype(BF16)
        for c in range(2):
            settle(smg, smg_out, k, c, 10).start()
            settle(nf.at[3], sb_out, k, c, 18).start()

    resid_copy = pltpu.make_async_copy(g2.at[mine_rows], resid_out, out_sem.at[26])
    resid_copy.start()
    for c in range(4):
        uf[c] = up_piece(c).total()
    sums_copy = pltpu.make_async_copy(uf, uf_out, out_sem.at[30])
    sums_copy.start()
    for k in range(STEPS):
        down_give(k).wait_recv()
    down_copy = pltpu.make_async_copy(df, df_out, out_sem.at[31])
    down_copy.start()
    late = [resid_copy, sums_copy, down_copy, cross_copy, layer_copy] + summed
    for copy in captions:
        copy.wait()
    parts_out[...] = parts[...]
    for k in range(STEPS):
        red_copy(3, k).wait_send()
        far_copy(3, k).wait_send()
        for s in range(4):
            norm_copy(s, k).wait_send()
        layer_red(k).wait_send()
        grads_over(k).wait_send()
        grads_on(k).wait_send()
        act_over(k).wait_send()
        query_over(k).wait_send()
        output_over(k).wait_send()
        down_give(k).wait_send()
        for c in range(2):
            settle(smg, smg_out, k, c, 10).wait()
            settle(nf.at[3], sb_out, k, c, 18).wait()
    for c in range(4):
        up_piece(c).x_end()
        down_piece(c).z_end()
        up_piece(c).z_end()
    for copy in late:
        copy.wait()


def middle(dp, x_full, self_mix, out_grad, wo, wcq, wco, wup, wdn, ck, cv, bias, gains):
    full = jax.ShapeDtypeStruct((1024, 1024), BF16)
    narrow = jax.ShapeDtypeStruct((1024, 256), BF16)
    short = jax.ShapeDtypeStruct((128, 256), BF16)
    block = jax.ShapeDtypeStruct((256, 1024), F32)
    part = 1024 // dp
    rows, columns = (part // 2, 256), (128, part)
    outs = [
        narrow, full, jax.ShapeDtypeStruct((256, 1024), BF16)] + [
        jax.ShapeDtypeStruct(item, BF16)
        for item in ((4,) + rows, (4, 2) + columns, (dp,) + rows, (dp,) + columns)
    ] + [short, short, short, short,
        jax.ShapeDtypeStruct((4, 8, 1024), F32), block, block,
    ]
    out_specs = [ANY] * 7 + [VM] * 5 + [ANY] * 2
    vm = pltpu.VMEM
    dma = pltpu.SemaphoreType.DMA
    scratch = [
        vm((256, 1024), BF16), vm((1024, 256), BF16), vm((256, 1024), BF16), vm((1024, 1024), BF16),
        vm((1024, 1024), BF16), vm((1024, 256), BF16), vm((1024, 1024), BF16), vm((512, 1024), BF16),
        vm((512, 1024), F32), vm((512, 1024), F32), vm((512, 1024), F32), vm((512, 1024), F32),
        vm((4, 1024, 1024), BF16), vm((1024, 1024), BF16), vm((1024, 1024), BF16),
        vm((1024, 256), BF16), vm((1024, 256), BF16), vm((1024, 256), BF16),
        vm((4, 512, 1024), BF16), vm((4, 512, 1024), BF16), vm((512, 1024), BF16), vm((512, 1024), BF16),
        vm((256, 1024), F32), vm((2, 128, 256), F32), vm((1024, 256), BF16),
        vm((1024, 1024), BF16), vm((1024, 512), BF16),
        vm((4, dp, 2) + rows, BF16), vm((4, dp) + rows, BF16), vm((4, dp) + columns, BF16),
        vm((4, slots(dp)) + rows, BF16), vm((4, slots(dp)) + columns, BF16), vm((4,) + rows, BF16), vm((4, 2) + columns, BF16),
        vm((dp, 2) + columns, BF16), vm((dp, 2) + rows, BF16), vm((dp,) + columns, BF16), vm((dp,) + rows, BF16),
        vm((4, 8, 1024), F32),
        dma((32,)), dma((4, 4)), dma((4, 4)), dma((4, 4)), dma((4, 4)), dma((4, 4)), dma((4, 4)),
        dma((3, 4)), dma((3, 4)), dma((4, 4)), dma((4, 4)), dma((2, 4, dp - 1)), dma((2, 4, dp - 1)),
        dma((4,)), dma((4,)), dma((4,)), dma((4,)), dma((32,)),
    ]
    return pl.pallas_call(
        functools.partial(middle_kernel, dp),
        out_shape=outs,
        in_specs=[ANY] * 8 + [VM] * 7,
        out_specs=out_specs,
        scratch_shapes=scratch,
        name="middle",
        compiler_params=pltpu.CompilerParams(
            collective_id=1, has_side_effects=True, vmem_limit_bytes=GRANT),
    )(x_full, self_mix, out_grad, wo, wcq, wco, wup, wdn, ck, cv, bias, *gains)


def front_kernel(
    x_own, wq_h, wk_h, wv_h, text_h, wck_h, wcv_h, ag_ref, as_ref,
    x_out, n1_out, q_out, k_out, v_out, mix_out, p0_out, p1_out, p2_out, p3_out, text_out, ck_out, cv_out,
    xf, n1, q, k, v, mix, p0, p1, p2, p3, wq, wk, wv, text, wck, wcv, theirs,
    load_sem, text_s, text_r, y_s, y_r, c_s, c_r, f_s, f_r, out_sem,
):
    rank = lax.axis_index("tp")
    core = lax.rem(rank, 2)
    pal = rank + 1 - 2 * core
    far = lax.rem(rank + 2, 4)
    beyond = lax.rem(pal + 2, 4)
    barrier = pltpu.get_barrier_semaphore()
    for peer in (pal, far):
        pl.semaphore_signal(barrier, inc=1, device_id={"tp": peer}, device_id_type=MESH)
    group = lax.axis_index("grp")
    pl.semaphore_signal(barrier, inc=1, device_id={"grp": 1 - group}, device_id_type=MESH)
    captions = pltpu.make_async_remote_copy(
        text_h, theirs, text_s.at[0], text_r.at[0], device_id={"grp": 1 - group}, device_id_type=MESH)
    loads = [
        pltpu.make_async_copy(src, dst, load_sem.at[i])
        for i, (src, dst) in enumerate([
            (x_own, xf.at[pl.ds(pl.multiple_of(rank * 256, 256), 256)]),
            (text_h, text), (wck_h, wck), (wcv_h, wcv), (wq_h, wq), (wk_h, wk), (wv_h, wv)])
    ]
    for copy in loads:
        copy.start()

    def part(block, i, size):
        return pl.ds(pl.multiple_of(block * 256 + i * size, size), size)

    across = [
        pltpu.make_async_remote_copy(
            x_own.at[pl.ds(i * 64, 64)], xf.at[part(rank, i, 64)], y_s.at[i], y_r.at[i],
            device_id={"tp": far}, device_id_type=MESH)
        for i in range(4)
    ]
    beside = pltpu.make_async_remote_copy(
        x_own, xf.at[part(rank, 0, 256)], c_s.at[0], c_r.at[0], device_id={"tp": pal}, device_id_type=MESH)
    onward = [
        pltpu.make_async_remote_copy(
            xf.at[part(far, i, 64)], xf.at[part(far, i, 64)], f_s.at[i], f_r.at[i],
            device_id={"tp": pal}, device_id_type=MESH)
        for i in range(4)
    ]
    pl.semaphore_wait(barrier, 3)
    for copy in across:
        copy.start()
    beside.start()
    captions.start()

    for copy in loads[1:4]:
        copy.wait()
    ck_out[...] = nn(text[...], wck[...]).astype(BF16)
    cv_out[...] = nn(text[...], wcv[...]).astype(BF16)
    for copy in loads[4:] + loads[:1]:
        copy.wait()

    def project(block, i):
        for r in range(4):
            rows = pl.ds(pl.multiple_of(block * 256 + i * 128 + r * 32, 32), 32)
            xhat, _ = norm_stats(xf[rows].astype(F32))
            n1[rows] = (xhat * ag_ref[...] + as_ref[...]).astype(BF16)
        rows = part(block, i, 128)
        value = n1[rows]
        q[rows] = (nn(value, wq[...]).astype(BF16) * 0.125).astype(BF16)
        k[rows] = nn(value, wk[...]).astype(BF16)
        v[rows] = nn(value, wv[...]).astype(BF16)

    def both(block):
        @pl.loop(0, 2)
        def _(i):
            project(block, i)

    both(rank)
    beside.wait_recv()
    both(pal)
    for half in range(2):
        for i in (2 * half, 2 * half + 1):
            across[i].wait_recv()
            onward[i].start()
        project(far, half)
        for i in (2 * half, 2 * half + 1):
            onward[i].wait_recv()
        project(beyond, half)
    outs = [
        pltpu.make_async_copy(src, dst, out_sem.at[i])
        for i, (src, dst) in enumerate([(xf, x_out), (n1, n1_out), (q, q_out), (k, k_out), (v, v_out)])
    ]
    for copy in outs:
        copy.start()

    captions.wait_recv()
    caption_out = pltpu.make_async_copy(theirs, text_out, out_sem.at[10])
    caption_out.start()

    kept = (p0, p1, p2, p3)
    below = lax.broadcasted_iota(jnp.int32, (256, 256), 0) >= lax.broadcasted_iota(jnp.int32, (256, 256), 1)

    @pl.loop(0, 2)
    def _(slab):
        lanes = pl.ds(pl.multiple_of(slab * 128, 128), 128)
        for i in range(4):
            done, end = i * 256, i * 256 + 256
            query = q[done:end, lanes]
            mixed = []
            for half in range(2):
                one = pick(query, half)
                diag = jnp.where(below, nt(one, k[done:end, lanes]), MASKED)
                peak = jnp.max(diag, axis=-1, keepdims=True)
                if i:
                    past = nt(one, k[0:done, lanes])
                    peak = jnp.maximum(peak, jnp.max(past, axis=-1, keepdims=True))
                    past = jnp.exp(past - peak)
                diag = jnp.exp(diag - peak)
                total = jnp.sum(diag, axis=-1, keepdims=True)
                if i:
                    total = total + jnp.sum(past, axis=-1, keepdims=True)
                inverse = 1.0 / total
                probs = (diag * inverse).astype(BF16)
                kept[i][slab * 2 + half, :, done:end] = probs
                out = nn(probs, v[done:end, lanes])
                if i:
                    probs = (past * inverse).astype(BF16)
                    kept[i][slab * 2 + half, :, 0:done] = probs
                    out = out + nn(probs, v[0:done, lanes])
                mixed.append(out)
            mix[done:end, lanes] = merge(*mixed).astype(BF16)

    tail = [
        pltpu.make_async_copy(src, dst, out_sem.at[5 + i])
        for i, (src, dst) in enumerate(
            [(mix, mix_out), (p0, p0_out), (p1, p1_out), (p2, p2_out), (p3, p3_out)])
    ]
    for copy in tail:
        copy.start()
    for copy in across + [beside, captions] + onward:
        copy.wait_send()
    for copy in outs + tail + [caption_out]:
        copy.wait()


def front(x_own, wq, wk, wv, text, wck, wcv, gains):
    full = ((1024, 1024), BF16)
    narrow = ((1024, 256), BF16)
    short = ((128, 256), BF16)
    probs = [((4, 256, 256 * (i + 1)), BF16) for i in range(4)]
    vm = pltpu.VMEM
    dma = pltpu.SemaphoreType.DMA
    return pl.pallas_call(
        front_kernel,
        out_shape=[jax.ShapeDtypeStruct(*item) for item in [full, full, narrow, narrow, narrow, narrow] + probs + [((128, 1024), BF16), short, short]],
        in_specs=[ANY] * 7 + [VM] * 2,
        out_specs=[ANY] * 11 + [VM] * 2,
        scratch_shapes=[vm(*item) for item in [full, full, narrow, narrow, narrow, narrow] + probs
                        + [narrow] * 3 + [((128, 1024), BF16), narrow, narrow, ((128, 1024), BF16)]]
        + [dma((8,)), dma((1,)), dma((1,)), dma((4,)), dma((4,)), dma((1,)), dma((1,)), dma((4,)), dma((4,)), dma((12,))],
        name="front",
        compiler_params=pltpu.CompilerParams(
            collective_id=2, has_side_effects=True, vmem_limit_bytes=GRANT),
    )(x_own, wq, wk, wv, text, wck, wcv, *gains)


def back_kernel(dp, *refs):
    refs = list(refs)

    def take(n):
        taken, refs[:n] = refs[:n], []
        return taken

    (smix_h, sb_h, lay_h, smg_h, q_h, k_h, v_h, p0_h, p1_h, p2_h, p3_h, n1_h, wq_h, wk_h, wv_h,
     x_own, resid_h, ac_h, dcq_h, dco_h, uf_h) = take(21)
    text, text_over, wck, wcv, dck, dcv, dck_over, dcv_over, parts_in, ag_ref = take(10)
    layer_out, image_grad, text_out, norm_out, up_o, cq_o, co_o, so_o, ck_o, cv_o, sq_o, sk_o, sv_o = take(13)
    (smix, sb, smg, q, k, v, p0, p1, p2, p3, n1, wqkv, xo, resid, ac) = take(15)
    so_g, ck_g, cv_g, self_g = take(4)
    x_bufs, self_x, z_bufs, self_z = take(5), take(1)[0], take(5), take(1)[0]
    (dqkv, dkv, acc, sst, rr, yst, yr, lay, tpart, t_st, t_rr, t_yst, t_yr, t_fin, npart, n_tp, nsum, n_all) = take(18)
    (load_sem, xs, xr, zs, zr, gs, gr, cs_sem, cr_sem, ys_sem, yr_sem, ls, lr, t_s, t_r, n_s, n_r, m_s, m_r) = take(19)

    rank = lax.axis_index("tp")
    group = lax.axis_index("grp")
    depth = lax.axis_index("dp")
    core = lax.rem(rank, 2)
    chip = rank // 2
    pal = rank + 1 - 2 * core
    far = lax.rem(rank + 2, 4)
    others = [(g, r) for g in range(2) for r in range(dp) if g or r]
    barrier = pltpu.get_barrier_semaphore()
    for r in range(1, 4):
        pl.semaphore_signal(barrier, inc=1, device_id={"tp": lax.rem(rank + r, 4)}, device_id_type=MESH)

    def at_other(g, r):
        return {"grp": lax.rem(group + g, 2), "dp": lax.rem(depth + r, dp)}

    for g, r in others:
        pl.semaphore_signal(barrier, inc=1, device_id=at_other(g, r), device_id_type=MESH)

    pairs = [
        (dcq_h, x_bufs[0]), (dco_h, x_bufs[1]),
        (smix_h, smix), (sb_h, sb),
        (smg_h, smg), (q_h, q), (k_h, k), (v_h, v), (p0_h, p0), (p1_h, p1), (p2_h, p2), (p3_h, p3), (n1_h, n1)]
    pairs += [
        (weight.at[:, h * 128 : h * 128 + 128], wqkv.at[:, h * 384 + i * 128 : h * 384 + i * 128 + 128])
        for h in range(2) for i, weight in enumerate((wq_h, wk_h, wv_h))]
    pairs += [(x_own, xo), (resid_h, resid), (ac_h, ac)]
    pairs += [(uf_h.at[c], up_o.at[c, group]) for c in range(4)]
    loads = [pltpu.make_async_copy(src, dst, load_sem.at[i]) for i, (src, dst) in enumerate(pairs)]
    for copy in loads[:13]:
        copy.start()

    place = (group, depth, dp)

    def piece(n, source=None):
        return Piece(place, source, x_bufs[n], z_bufs[n], (xs.at[n], xr.at[n]), (zs.at[n], zr.at[n]))

    def self_piece(h, i):
        n = 3 * h + i
        return Piece(place, self_g.at[n], self_x.at[n], self_z.at[n], (xs.at[5 + n], xr.at[5 + n]),
                     (zs.at[5 + n], zr.at[5 + n]))

    def give(n, src, out):
        return pltpu.make_async_remote_copy(
            src, out, gs.at[n], gr.at[n], device_id={"grp": 1 - group}, device_id_type=MESH)

    cq_p, co_p, so_p, ck_p, cv_p = [
        piece(n, source) for n, source in enumerate((None, None, so_g, None, None))]
    halves = [(cq_p, cq_o), (co_p, co_o), (so_p, so_o), (ck_p, ck_o), (cv_p, cv_o)]
    halves += [(self_piece(h, i), out.at[h]) for h in range(2) for i, out in enumerate((sq_o, sk_o, sv_o))]
    gives = [give(n, out.at[group], out.at[group]) for n, (_, out) in enumerate(halves)]
    early = [give(12 + c, uf_h.at[c], up_o.at[c, group]) for c in range(4)]

    def finish(n):
        one, out = halves[n]
        out[group] = one.total()
        gives[n].start()

    layer = [
        pltpu.make_async_remote_copy(
            lay_h.at[pl.ds(j * CHUNK, CHUNK)], lay.at[pl.ds(j * CHUNK, CHUNK)], ls.at[j], lr.at[j],
            device_id={"tp": far}, device_id_type=MESH)
        for j in range(2)
    ]
    pl.semaphore_wait(barrier, 3 + len(others))
    for copy in layer:
        copy.start()
    for copy in loads[:2]:
        copy.wait()
    cq_p.spread()
    co_p.spread()

    scale = HEAD ** (-0.5)
    depth_rows = 1024 // dp
    per = 256 // depth_rows

    def caption_grad(one, ref, ours, theirs):
        for m in range(4):
            lanes = slice(m * 256, m * 256 + 256)
            value = (tn(text[:, lanes], ours[...]) + tn(text_over[:, lanes], theirs[...])).astype(BF16)
            for u in range(per):
                part = value[u * depth_rows : (u + 1) * depth_rows]
                ref[m * per + u, 0] = part[: depth_rows // 2]
                ref[m * per + u, 1] = part[depth_rows // 2 :]

        @pl.loop(0, dp)
        def _(d):
            one.x_buf[d] = ref[d, group]

        one.spread()

    def own(i):
        return pl.ds(pl.multiple_of(i * CHUNK, CHUNK), CHUNK)

    class Scatter:
        def __init__(self, n):
            self.n = n

        def red(self, i):
            n = self.n
            return pltpu.make_async_remote_copy(
                sst.at[n, own(i)], rr.at[n, own(i)], cs_sem.at[n, i], cr_sem.at[n, i],
                device_id={"tp": pal}, device_id_type=MESH)

        def far(self, j):
            n = self.n
            return pltpu.make_async_remote_copy(
                yst.at[n, own(j)], yr.at[n, own(j)], ys_sem.at[n, j], yr_sem.at[n, j],
                device_id={"tp": far}, device_id_type=MESH)

        def put(self, i, theirs, ours):
            sst[self.n, own(i)] = theirs.astype(BF16)
            self.red(i).start()
            acc[self.n, own(i)] = ours

        def send(self, j):
            i = 2 * (1 - chip) + j
            self.red(i).wait_recv()
            yst[self.n, own(j)] = (acc[self.n, own(i)] + rr[self.n, own(i)].astype(F32)).astype(BF16)
            self.far(j).start()

        def keep(self, j):
            self.red(2 * chip + j).wait_recv()
            self.far(j).wait_recv()

        def value(self, j, r):
            i = 2 * chip + j
            rows = pl.ds(pl.multiple_of(i * CHUNK + r * SUB, SUB), SUB)
            near = pl.ds(j * CHUNK + r * SUB, SUB)
            return acc[self.n, rows] + rr[self.n, rows].astype(F32) + yr[self.n, near].astype(F32)

        def end(self):
            for i in range(4):
                self.red(i).wait_send()
            for j in range(2):
                self.far(j).wait_send()

    first = Scatter(0)

    def sequence(step):
        return lax.rem(2 * (1 - chip) + step, 4)

    for copy in loads[2:4]:
        copy.wait()
    for copy in loads[13:]:
        copy.start()
    for d in range(dp):
        value = tn(smix[...], sb[:, d * depth_rows : (d + 1) * depth_rows]).astype(BF16)
        so_g[d, 0] = value[:128]
        so_g[d, 1] = value[128:]
    so_p.start()
    for copy in early:
        copy.start()

    caption_grad(ck_p, ck_g, dck, dck_over)
    caption_grad(cv_p, cv_g, dcv, dcv_over)
    tpart[...] = nt(dck[...], wck[...]) + nt(dcv[...], wcv[...])

    def t_rows(c):
        return pl.ds(pl.multiple_of(c * 64, 64), 64)

    t_st[...] = tpart[t_rows(1 - core)].astype(BF16)
    t_red = pltpu.make_async_remote_copy(
        t_st, t_rr, t_s.at[0], t_r.at[0], device_id={"tp": pal}, device_id_type=MESH)
    t_red.start()

    for copy in loads[4:13]:
        copy.wait()
    dkv[...] = jnp.zeros_like(dkv)
    kept = (p0, p1, p2, p3)

    @pl.loop(0, 2)
    def _(slab):
        lanes = pl.ds(pl.multiple_of(slab * 128, 128), 128)
        for i in range(4):
            begin, end = i * 256, i * 256 + 256
            query, grad = q[begin:end, lanes], smg[begin:end, lanes]
            product = grad.astype(F32) * smix[begin:end, lanes].astype(F32)
            moved = []
            for half in range(2):
                one_q, one_g = pick(query, half), pick(grad, half)
                inner = jnp.sum(pick(product, half), axis=-1, keepdims=True)
                probs = kept[i][slab * 2 + half]
                prob_grad = nt(one_g, v[0:end, lanes])
                score_grad = (probs.astype(F32) * (prob_grad - inner)).astype(BF16)
                moved.append(nn(score_grad, k[0:end, lanes]))
                dkv[0, 0:end, lanes] += tn(score_grad, one_q)
                dkv[1, 0:end, lanes] += tn(probs, one_g)
            moved = (merge(*moved) * scale).astype(BF16)
            dqkv[begin:end, pl.ds(pl.multiple_of(slab * 384, 128), 128)] = moved
            if i == 1:
                @pl.when(slab == 0)
                def _():
                    cq_p.pass_on()

                @pl.when(slab == 1)
                def _():
                    ck_p.pass_on()
                    finish(0)
            if i == 2:
                @pl.when(slab == 0)
                def _():
                    so_p.add()
                    so_p.spread()

                @pl.when(slab == 1)
                def _():
                    cv_p.pass_on()
                    finish(1)
            if i == 3:
                @pl.when(slab == 0)
                def _():
                    co_p.pass_on()

                @pl.when(slab == 1)
                def _():
                    so_p.pass_on()
                    finish(3)

        dqkv[:, pl.ds(pl.multiple_of(slab * 384 + 128, 128), 128)] = dkv[0, :, lanes].astype(BF16)
        dqkv[:, pl.ds(pl.multiple_of(slab * 384 + 256, 128), 128)] = dkv[1, :, lanes].astype(BF16)
        right = dqkv[:, pl.ds(pl.multiple_of(slab * 384, 128), 384)]
        for m in range(4):
            value = tn(n1[:, m * 256 : m * 256 + 256], right).astype(BF16)
            for u in range(per):
                part = value[u * depth_rows : (u + 1) * depth_rows]
                for n in range(3):
                    self_g[slab * 3 + n, m * per + u, 0] = part[: depth_rows // 2, n * 128 : n * 128 + 128]
                    self_g[slab * 3 + n, m * per + u, 1] = part[depth_rows // 2 :, n * 128 : n * 128 + 128]
        for n in range(3):
            self_piece(slab, n).start()

    t_red.wait_recv()
    t_yst[...] = (tpart[t_rows(core)] + t_rr[...].astype(F32)).astype(BF16)
    t_far = pltpu.make_async_remote_copy(
        t_yst, t_yr, t_s.at[1], t_r.at[1], device_id={"tp": far}, device_id_type=MESH)
    t_far.start()
    for copy in loads[13:]:
        copy.wait()

    @pl.loop(0, 4)
    def _(step):
        i = sequence(step)

        def partial(c):
            start = pl.multiple_of(256 * (c + 2 * (i // 2)) + 128 * lax.rem(i, 2), 128)
            rows = pl.ds(start, CHUNK)
            return nt(dqkv[rows], wqkv[...])

        first.put(i, partial(1 - core), partial(core))

        @pl.when((step > 0) & (step < 3))
        def _():
            first.send(step - 1)

        @pl.when(step < 3)
        def _():
            self_piece(0, step).add()
            self_piece(0, step).spread()

    for n in range(3):
        self_piece(0, n).pass_on()
    for n in (4, 2):
        finish(n)
    for j in range(2):
        layer[j].wait_recv()
        for r in range(CHUNK // SUB):
            rows = slice(j * CHUNK + r * SUB, j * CHUNK + r * SUB + SUB)
            layer_out[rows] = (ac[rows] + lay[rows].astype(F32)).astype(BF16)

    for n in range(3):
        self_piece(1, n).add()
        self_piece(1, n).spread()
    t_far.wait_recv()
    t_fin[t_rows(core)] = (t_yst[...].astype(F32) + t_yr[...].astype(F32)).astype(BF16)
    t_share = pltpu.make_async_remote_copy(
        t_fin.at[t_rows(core)], t_fin.at[t_rows(core)], t_s.at[2], t_r.at[2],
        device_id={"tp": pal}, device_id_type=MESH)
    t_share.start()
    for n in range(5, 8):
        finish(n)
    for n in range(3):
        self_piece(1, n).pass_on()

    npart[...] = jnp.zeros_like(npart)
    for j in range(2):
        first.keep(j)
        for r in range(CHUNK // SUB):
            rows = slice(j * CHUNK + r * SUB, j * CHUNK + r * SUB + SUB)
            given = first.value(j, r)
            xhat, rstd = norm_stats(xo[rows].astype(F32))
            npart[0] += fold_rows(given * xhat)
            npart[1] += fold_rows(given)
            image_grad[rows] = resid[rows] + norm_input_grad(xhat, rstd, ag_ref[...], given)

    def line(ref, i):
        return jnp.sum(ref[i], axis=0, keepdims=True)

    n_tp[rank] = jnp.concatenate(
        [line(npart, 0), line(npart, 1)] + [line(parts_in, i) for i in range(4)]
        + [jnp.zeros((2, 1024), F32)], axis=0)
    n_copies = [
        pltpu.make_async_remote_copy(
            n_tp.at[rank], n_tp.at[rank], n_s.at[r - 1], n_r.at[r - 1],
            device_id={"tp": lax.rem(rank + r, 4)}, device_id_type=MESH)
        for r in range(1, 4)
    ]
    for copy in n_copies:
        copy.start()
    for n in range(8, 11):
        finish(n)
    for copy in n_copies:
        copy.wait_recv()
    summed = n_tp[0] + n_tp[1] + n_tp[2] + n_tp[3]
    for d in range(dp):
        nsum[d] = summed[:, d * depth_rows : (d + 1) * depth_rows]
    slot = group * dp + depth
    m_copies = [
        pltpu.make_async_remote_copy(
            nsum.at[lax.rem(depth + r, dp)], n_all.at[slot], m_s.at[i], m_r.at[i],
            device_id=at_other(g, r), device_id_type=MESH)
        for i, (g, r) in enumerate(others)
    ]
    for copy in m_copies:
        copy.start()
    n_all[slot] = nsum[depth]

    for copy in m_copies:
        copy.wait_recv()
    total = n_all[0]
    for i in range(1, 2 * dp):
        total = total + n_all[i]
    norm_out[...] = total
    t_share.wait_recv()
    text_out[...] = t_fin[...]
    for copy in m_copies + n_copies + [t_red, t_far, t_share]:
        copy.wait_send()
    for copy in layer:
        copy.wait_send()
    first.end()
    for n, (one, _) in enumerate(halves):
        if n not in (0, 1, 3, 4):
            one.x_end()
        one.z_end()
        gives[n].wait()
    for copy in early:
        copy.wait()


def back(dp, *operands):
    part = 1024 // dp
    full = ((1024, 1024), BF16)
    narrow = ((1024, 256), BF16)
    probs = [((4, 256, 256 * (i + 1)), BF16) for i in range(4)]
    rows, columns = (part // 2, 256), (128, part)
    block = ((256, 1024), F32)
    kinds = [rows, columns, columns, rows, rows]
    slabs = (part // 2, 128)
    outs = [((256, 1024), BF16), block, ((128, 1024), BF16), ((8, part), F32), ((4, 2) + rows, BF16)]
    outs += [((2,) + s, BF16) for s in (rows, columns, columns, rows, rows)] + [((2, 2) + slabs, BF16)] * 3
    scratch = (
        [narrow, full] + [narrow] * 4 + probs + [full] + [((1024, 768), BF16)]
        + [((256, 1024), BF16), block, block]
        + [((dp, 2) + s, BF16) for s in (columns, rows, rows)] + [((6, dp, 2) + slabs, BF16)]
        + [((dp,) + s, BF16) for s in kinds] + [((6, dp) + slabs, BF16)]
        + [((slots(dp),) + s, BF16) for s in kinds] + [((6, slots(dp)) + slabs, BF16)]
        + [((1024, 768), BF16)]
        + [((2, 1024, 256), F32), ((1, 512, 1024), F32), ((1, 512, 1024), BF16), ((1, 512, 1024), BF16),
           ((1, 256, 1024), BF16), ((1, 256, 1024), BF16), ((256, 1024), BF16), ((128, 1024), F32),
           ((64, 1024), BF16), ((64, 1024), BF16), ((64, 1024), BF16), ((64, 1024), BF16), ((128, 1024), BF16),
           ((2, 8, 1024), F32), ((4, 8, 1024), F32), ((dp, 8, part), F32), ((2 * dp, 8, part), F32)]
    )
    dma = pltpu.SemaphoreType.DMA
    many = 2 * dp - 1
    sems = [dma((32,)), dma((12,)), dma((12,)), dma((12, dp - 1)), dma((12, dp - 1)), dma((16,)), dma((16,)),
            dma((1, 4)), dma((1, 4)), dma((1, 2)), dma((1, 2)), dma((2,)), dma((2,)), dma((3,)), dma((3,)), dma((3,)), dma((3,)),
            dma((many,)), dma((many,))]
    return pl.pallas_call(
        functools.partial(back_kernel, dp),
        out_shape=[jax.ShapeDtypeStruct(*item) for item in outs],
        in_specs=[ANY] * 21 + [VM] * 10,
        out_specs=[VM] * len(outs),
        scratch_shapes=[pltpu.VMEM(*item) for item in scratch] + sems,
        name="back",
        compiler_params=pltpu.CompilerParams(
            collective_id=3, has_side_effects=True, vmem_limit_bytes=GRANT),
    )(*operands)


def emit_kernel(n, *refs):
    layer, image, text, norms, up, down = refs[:6]
    outs = refs[n:]
    outs[0][...] = layer[...]
    outs[1][...] = image[...]
    outs[2][...] = text[...].astype(F32)
    for i in range(6):
        outs[3 + i][...] = norms[i]
    rows, columns = up.shape[2], down.shape[2]
    for c in range(4):
        for h in range(2):
            outs[9][h * rows : (h + 1) * rows, c * 256 : c * 256 + 256] = up[c, h].astype(F32)
            at = h * 512 + c * columns
            outs[10][at : at + columns, :] = down[c, h].astype(F32)
    for given, out in zip(refs[6 : n - 3], outs[11:]):
        rows = given.shape[1]
        for h in range(2):
            out[h * rows : (h + 1) * rows] = given[h].astype(F32)
    for given, out in zip(refs[n - 3 : n], outs[-3:]):
        rows = given.shape[2]
        for s in range(2):
            for h in range(2):
                out[h * rows : (h + 1) * rows, s * 128 : s * 128 + 128] = given[s, h].astype(F32)


def emit(arrays):
    part = arrays[3].shape[1]
    shapes = [(part,)] * 6 + [(part, 1024), (1024, part)]
    outs = [jax.ShapeDtypeStruct((256, 1024), BF16), jax.ShapeDtypeStruct((256, 1024), F32), jax.ShapeDtypeStruct((128, 1024), F32)]
    outs += [jax.ShapeDtypeStruct(item, F32) for item in shapes]
    outs += [jax.ShapeDtypeStruct((2 * item.shape[1], item.shape[2]), F32) for item in arrays[6:-3]]
    outs += [jax.ShapeDtypeStruct((part, 256), F32)] * 3
    return pl.pallas_call(
        functools.partial(emit_kernel, len(arrays)),
        out_shape=outs,
        in_specs=[VM] * len(arrays),
        out_specs=[VM] * len(outs),
        name="emit",
        compiler_params=pltpu.CompilerParams(vmem_limit_bytes=GRANT),
    )(*arrays)


def local(
    dp,
    image_rows,
    text_states,
    caption_lengths,
    out_grad,
    self_query,
    self_key,
    self_value,
    self_output,
    cross_query,
    cross_key,
    cross_value,
    cross_output,
    mlp_up,
    mlp_down,
    attn_gain,
    attn_shift,
    cross_gain,
    cross_shift,
    mlp_gain,
    mlp_shift,
):
    text = text_states[0]
    bias = jnp.where(jnp.arange(TEXT)[None, :] < caption_lengths[0], 0.0, MASKED)
    x_full, norm_one, q, k, v, self_mix, p0, p1, p2, p3, other_text, cross_k, cross_v = front(
        image_rows, self_query, self_key, self_value, text, cross_key, cross_value,
        [attn_gain[None, :], attn_shift[None, :]])
    gains = [item[None, :] for item in (cross_gain, cross_shift, mlp_gain, mlp_shift)]
    (mix_grad, self_back, layer_part, up_sum, down_sum, c_query, c_output, k_grad, v_grad, k_over, v_over, parts, resid,
     after_cross) = middle(
        dp, x_full, self_mix, out_grad, self_output, cross_query, cross_output, mlp_up, mlp_down,
        cross_k, cross_v, bias, gains)
    arrays = back(
        dp, self_mix, self_back, layer_part, mix_grad, q, k, v, p0, p1, p2, p3, norm_one,
        self_query, self_key, self_value, image_rows, resid, after_cross, c_query, c_output,
        up_sum, text, other_text, cross_key, cross_value, k_grad, v_grad, k_over, v_over, parts, attn_gain[None, :])
    layer_out, image_grad, text_grad, *rest = emit([*arrays[:5], down_sum, *arrays[5:]])
    norms, (up, down, cq, co, so, ck, cv, sq, sk, sv) = rest[:6], rest[6:]
    return (layer_out, image_grad, text_grad[None], sq, sk, sv, so, cq, ck, cv, co, up, down, *norms)


def solution(mesh):
    placed = (
        P(("grp", "dp", "tp"), None),
        P(("grp", "dp"), None, None),
        P(("grp", "dp")),
        P(("grp", "dp"), None),
        P(None, "tp"),
        P(None, "tp"),
        P(None, "tp"),
        P("tp", None),
        P(None, "tp"),
        P(None, "tp"),
        P(None, "tp"),
        P("tp", None),
        P(None, "tp"),
        P("tp", None),
        P(),
        P(),
        P(),
        P(),
        P(),
        P(),
    )
    return jax.shard_map(
        functools.partial(local, mesh.shape["dp"]),
        mesh=mesh,
        in_specs=placed,
        out_specs=(
            P(("grp", "dp", "tp"), None),
            P(("grp", "dp", "tp"), None),
            P(("grp", "dp"), None, None),
            P("dp", "tp"),
            P("dp", "tp"),
            P("dp", "tp"),
            P("tp", "dp"),
            P("dp", "tp"),
            P("dp", "tp"),
            P("dp", "tp"),
            P("tp", "dp"),
            P("dp", "tp"),
            P("tp", "dp"),
            P("dp"),
            P("dp"),
            P("dp"),
            P("dp"),
            P("dp"),
            P("dp"),
        ),
        check_vma=False,
    )
```

```python
import functools

import jax
import jax.numpy as jnp
from jax import lax
from jax.experimental import pallas as pl
from jax.experimental.pallas import tpu as pltpu
from jax.sharding import PartitionSpec as P

HEAD = 64
TEXT = 128
EPSILON = 1e-05
MASKED = -1e30
MESH = pl.DeviceIdType.MESH
F32 = jnp.float32
BF16 = jnp.bfloat16
ANY = pl.BlockSpec(memory_space=pl.ANY)
VM = pl.BlockSpec(memory_space=pltpu.VMEM)
GRANT = 60 * 1024 * 1024


def nn(left, right):
    return lax.dot_general(left, right, (((1,), (0,)), ((), ())), preferred_element_type=F32)


def nt(left, right):
    return lax.dot_general(left, right, (((1,), (1,)), ((), ())), preferred_element_type=F32)


def tn(left, right):
    return lax.dot_general(left, right, (((0,), (0,)), ((), ())), preferred_element_type=F32)


def norm_stats(hidden):
    middle = jnp.mean(hidden, axis=-1, keepdims=True)
    centred = hidden - middle
    spread = jnp.mean(centred * centred, axis=-1, keepdims=True)
    rstd = lax.rsqrt(spread + EPSILON)
    return centred * rstd, rstd


def norm_input_grad(xhat, rstd, gain, cotangent):
    scaled = cotangent * gain
    first = jnp.mean(scaled, axis=-1, keepdims=True)
    second = jnp.mean(scaled * xhat, axis=-1, keepdims=True)
    return (scaled - first - xhat * second) * rstd


def fold_rows(value):
    rows = value.shape[0]
    total = value[0:8]
    for start in range(8, rows, 8):
        total = total + value[start : start + 8]
    return total


def lane_keep(shape, part):
    lanes = lax.broadcasted_iota(jnp.int32, shape, 1)
    return (lanes // HEAD) == part


def pick(value, part):
    return jnp.where(lane_keep(value.shape, part), value, jnp.zeros_like(value))


def merge(first, second):
    return jnp.where(lane_keep(first.shape, 0), first, second)


class Piece:
    def __init__(self, place, source, x_buf, z_buf, x_sems, z_sems):
        self.place, self.source, self.x_buf, self.z_buf = place, source, x_buf, z_buf
        self.x_sems, self.z_sems = x_sems, z_sems
        depth = place[1]
        self.line = place[2] == 4
        self.mate = depth + 1 - 2 * lax.rem(depth, 2)
        self.end = (depth == 0) | (depth == 3)
        self.inner = (depth == 1) | (depth == 2)

    def x_copy(self):
        other = 1 - self.place[0]
        return pltpu.make_async_remote_copy(
            self.source.at[:, other], self.x_buf, *self.x_sems,
            device_id={"grp": other}, device_id_type=MESH)

    def z_copies(self):
        _, depth, size = self.place
        return [
            pltpu.make_async_remote_copy(
                self.x_buf.at[lax.rem(depth + r, size)], self.z_buf.at[r - 1],
                self.z_sems[0].at[r - 1], self.z_sems[1].at[r - 1],
                device_id={"dp": lax.rem(depth + r, size)}, device_id_type=MESH)
            for r in range(1, size)
        ]

    def hop(self, parts, slots, sent, got, to):
        return pltpu.make_async_remote_copy(
            self.x_buf.at[parts], self.z_buf.at[slots], self.z_sems[0].at[sent], self.z_sems[1].at[got],
            device_id={"dp": to}, device_id_type=MESH)

    def three(self):
        return self.hop(pl.ds(jnp.where(self.place[1] == 0, 1, 0), 3), pl.ds(0, 3), 0, 0, self.mate)

    def single(self):
        return self.hop(self.mate, 0, 0, 0, self.mate)

    def late(self, i):
        to = 3 - (self.mate if i else self.place[1])
        return self.hop(to, 3, 1 + i, 1, to)

    def start(self):
        self.x_copy().start()

    def add(self):
        self.x_copy().wait_recv()

        @pl.loop(0, self.place[2])
        def _(d):
            mine = self.source[d, self.place[0]]
            self.x_buf[d] = (self.x_buf[d].astype(F32) + mine.astype(F32)).astype(BF16)

    def spread(self):
        if not self.line:
            for copy in self.z_copies():
                copy.start()
            return

        @pl.when(self.end)
        def _():
            self.three().start()

        @pl.when(self.inner)
        def _():
            self.single().start()

    def pass_on(self):
        if not self.line:
            return

        @pl.when(self.inner)
        def _():
            self.three().wait_recv()
            for i in range(2):
                to = 3 - (self.mate if i else self.place[1])
                slot = to - jnp.where(self.place[1] == 1, 1, 0)
                self.x_buf[to] = (self.x_buf[to].astype(F32) + self.z_buf[slot].astype(F32)).astype(BF16)
                self.late(i).start()

    def total(self):
        depth = self.place[1]
        total = self.x_buf[depth].astype(F32)
        if not self.line:
            for copy in self.z_copies():
                copy.wait_recv()
            for r in range(self.place[2] - 1):
                total = total + self.z_buf[r].astype(F32)
            return total.astype(BF16)

        @pl.when(self.end)
        def _():
            self.single().wait_recv()

        self.late(0).wait_recv()
        near = self.z_buf[jnp.where(depth == 2, 2, 0)].astype(F32)
        return (total + near + self.z_buf[3].astype(F32)).astype(BF16)

    def x_end(self):
        self.x_copy().wait_send()

    def z_end(self):
        if not self.line:
            for copy in self.z_copies():
                copy.wait_send()
            return

        @pl.when(self.end)
        def _():
            self.three().wait_send()

        @pl.when(self.inner)
        def _():
            self.single().wait_send()
            self.late(0).wait_send()
            self.late(1).wait_send()


def slots(dp):
    return 4 if dp == 4 else dp - 1


CHUNK = 128
STEPS = 4
SUB = 32


def natural(core, step):
    return 256 * (core + 2 * (step // 2)) + 128 * (step % 2)


def middle_kernel(
    dp, x_full, self_mix, out_grad, wo_h, wcq_h, wco_h, wup_h, wdn_h,
    ck_ref, cv_ref, bias_ref, cg_ref, cs_ref, mg_ref, ms_ref,
    smg_out, sb_out, lay_out, uf_out, df_out, dcq_out, dco_out, dck_out, dcv_out, dck_over, dcv_over, parts_out, resid_out, ac_out,
    wo, wcq, wco, wup, wdn, smix, og, xr, h1, h2, acc, g2, nf, act, pg, cq, cmix, cqg,
    rr, yr, sst, yst, pbuf, dkv, smg, og2, act2, ug, ux, dx, uz, dz, uf, df, dco, dcq, cox, cqx, parts,
    load_sem, cs_sem, cr_sem, ns_sem, nr_sem, ys_sem, yr_sem, xs_sem, xr_sem, us_sem, ur_sem, ds_sem, dr_sem, os_sem, or_sem, ls_sem, lr_sem, out_sem,
):
    span = 1024 // dp
    per = 256 // span
    rank = lax.axis_index("tp")
    core = lax.rem(rank, 2)
    chip = rank // 2
    pal = rank + 1 - 2 * core
    far = lax.rem(rank + 2, 4)
    group = lax.axis_index("grp")
    depth = lax.axis_index("dp")
    place = (group, depth, dp)
    barrier = pltpu.get_barrier_semaphore()
    for peer in (pal, far):
        pl.semaphore_signal(barrier, inc=1, device_id={"tp": peer}, device_id_type=MESH)
    pl.semaphore_signal(barrier, inc=1, device_id={"grp": 1 - group}, device_id_type=MESH)
    for r in range(1, dp):
        pl.semaphore_signal(barrier, inc=1, device_id={"dp": lax.rem(depth + r, dp)}, device_id_type=MESH)

    loads = []

    def load(src, dst):
        loads.append(pltpu.make_async_copy(src, dst, load_sem.at[len(loads)]))

    for k in range(STEPS):
        for c in range(2):
            load(self_mix.at[pl.ds(natural(c, k), CHUNK)], smix.at[pl.ds(k * 256 + c * 128, CHUNK)])
    load(wo_h, wo)
    n_first = len(loads)
    for copy in loads:
        copy.start()
    for k in range(STEPS):
        start = pl.multiple_of(256 * (core + 2 * (k // 2)) + 128 * (k % 2), 128)
        load(x_full.at[pl.ds(start, CHUNK)], xr.at[pl.ds(k * CHUNK, CHUNK)])
    load(wcq_h, wcq)
    load(wco_h, wco)
    n_second = len(loads)
    for k in range(STEPS):
        for c in range(2):
            load(out_grad.at[pl.ds(natural(c, k), CHUNK)], og.at[pl.ds(k * 256 + c * 128, CHUNK)])
    load(wup_h, wup)
    load(wdn_h, wdn)
    n_third = len(loads)

    dkv[...] = jnp.zeros_like(dkv)
    parts[...] = jnp.zeros_like(parts)

    def own(k):
        return pl.ds(pl.multiple_of(k * CHUNK, CHUNK), CHUNK)

    def pair(k):
        return pl.ds(pl.multiple_of(k * 256, 256), 256)

    def mine(k):
        return pl.ds(pl.multiple_of(k * 256 + core * CHUNK, CHUNK), CHUNK)

    def red_copy(s, k):
        return pltpu.make_async_remote_copy(
            sst.at[own(k)], rr.at[s, own(k)], cs_sem.at[s, k], cr_sem.at[s, k],
            device_id={"tp": pal}, device_id_type=MESH)

    def far_copy(s, k):
        return pltpu.make_async_remote_copy(
            yst.at[own(k)], yr.at[s, own(k)], ys_sem.at[s, k], yr_sem.at[s, k],
            device_id={"tp": far}, device_id_type=MESH)

    def norm_copy(s, k):
        return pltpu.make_async_remote_copy(
            nf.at[s, mine(k)], nf.at[s, mine(k)], ns_sem.at[s, k], nr_sem.at[s, k],
            device_id={"tp": pal}, device_id_type=MESH)

    def produce(s, k, columns):
        for j, value in columns:
            pbuf[:, j : j + value.shape[1]] = value
        if s > 0:
            red_copy(s - 1, k).wait_send()
        sst[own(k)] = pbuf[pl.ds(pl.multiple_of((1 - core) * CHUNK, CHUNK), CHUNK), :].astype(BF16)
        red_copy(s, k).start()
        acc[own(k)] = pbuf[pl.ds(pl.multiple_of(core * CHUNK, CHUNK), CHUNK), :]

    def finish(s, k):
        if s > 0:
            far_copy(s - 1, k).wait_send()
        red_copy(s, k).wait_recv()
        total = acc[own(k)] + rr[s, own(k)].astype(F32)
        acc[own(k)] = total
        yst[own(k)] = total.astype(BF16)
        far_copy(s, k).start()

    def grads_over(k):
        start = pl.multiple_of(256 * (core + 2 * (k // 2)) + 128 * (k % 2), 128)
        return pltpu.make_async_remote_copy(
            out_grad.at[pl.ds(start, CHUNK)], og2.at[mine(k)], xs_sem.at[0, k], xr_sem.at[0, k],
            device_id={"grp": 1 - group}, device_id_type=MESH)

    def grads_on(k):
        return pltpu.make_async_remote_copy(
            og2.at[mine(k)], og2.at[mine(k)], os_sem.at[k], or_sem.at[k],
            device_id={"tp": pal}, device_id_type=MESH)

    def act_over(k):
        columns = pl.ds(pl.multiple_of((1 - group) * 512, 512), 512)
        return pltpu.make_async_remote_copy(
            act.at[pair(k), columns], act2.at[pair(k)], xs_sem.at[1, k], xr_sem.at[1, k],
            device_id={"grp": 1 - group}, device_id_type=MESH)

    def sub(k, r):
        return pl.ds(pl.multiple_of(k * CHUNK + r * SUB, SUB), SUB)

    def msub(k, r):
        return pl.ds(pl.multiple_of(k * 256 + core * CHUNK + r * SUB, SUB), SUB)

    pl.semaphore_wait(barrier, 2 + dp)
    for copy in loads[:n_first]:
        copy.wait()
    for copy in loads[n_first:]:
        copy.start()
    for k in range(STEPS):
        grads_over(k).start()

    @pl.loop(0, STEPS)
    def _(k):
        rows = smix[pair(k), :]
        produce(0, k, [(j, nn(rows, wo[:, j : j + 512])) for j in (0, 512)])

        @pl.when(k > 0)
        def _():
            finish(0, k - 1)

    finish(0, STEPS - 1)
    for copy in loads[n_first:n_second]:
        copy.wait()

    scale = HEAD ** (-0.5)

    def settle(src, dst, k, c, slot):
        start = pl.multiple_of(256 * (c + 2 * (k // 2)) + 128 * (k % 2), 128)
        return pltpu.make_async_copy(
            src.at[pl.ds(pl.multiple_of(k * 256 + c * CHUNK, CHUNK), CHUNK)],
            dst.at[pl.ds(start, CHUNK)], out_sem.at[slot + 2 * k + c])

    @pl.loop(0, STEPS)
    def _(k):
        far_copy(0, k).wait_recv()
        for r in range(CHUNK // SUB):
            hidden = xr[sub(k, r)].astype(F32) + acc[sub(k, r)] + yr[0, sub(k, r)].astype(F32)
            h1[sub(k, r)] = hidden
            xhat, _ = norm_stats(hidden)
            nf[0, msub(k, r)] = (xhat * cg_ref[...] + cs_ref[...]).astype(BF16)
        norm_copy(0, k).start()
        grads_over(k).wait_recv()
        grads_on(k).start()

        @pl.when(k > 0)
        def _():
            finish(1, k - 1)

        norm_copy(0, k).wait_recv()
        cq[pair(k)] = nn(nf[0, pair(k)], wcq[...]).astype(BF16)
        for slab in range(2):
            lanes = slice(slab * 128, slab * 128 + 128)
            query = cq[pair(k), lanes]
            key, value = ck_ref[:, lanes], cv_ref[:, lanes]
            mixed = []
            for part in range(2):
                scores = nt(pick(query, part), key) * scale + bias_ref[...]
                shifted = jnp.exp(scores - jnp.max(scores, axis=-1, keepdims=True))
                probs = shifted / jnp.sum(shifted, axis=-1, keepdims=True)
                mixed.append(nn(probs.astype(BF16), value))
            cmix[pair(k), lanes] = merge(*mixed).astype(BF16)
        rows = cmix[pair(k), :]
        produce(1, k, [(j, nn(rows, wco[:, j : j + 512])) for j in (0, 512)])

    finish(1, STEPS - 1)
    for copy in loads[n_second:n_third]:
        copy.wait()

    @pl.loop(0, STEPS)
    def _(k):
        far_copy(1, k).wait_recv()
        for r in range(CHUNK // SUB):
            hidden = h1[sub(k, r)] + acc[sub(k, r)] + yr[1, sub(k, r)].astype(F32)
            h2[sub(k, r)] = hidden
            xhat, _ = norm_stats(hidden)
            nf[1, msub(k, r)] = (xhat * mg_ref[...] + ms_ref[...]).astype(BF16)
        norm_copy(1, k).start()

        @pl.when(k > 0)
        def _():
            finish(2, k - 1)

        norm_copy(1, k).wait_recv()
        rows = nf[1, pair(k)]
        grads = og[pair(k), :]
        for j in range(0, 1024, 256):
            cols = slice(j, j + 256)
            pre = nn(rows, wup[:, cols])
            back = nt(grads, wdn[cols, :])
            square = pre * pre
            bend = jnp.tanh(0.7978845608028654 * pre * (1.0 + 0.044715 * square))
            half = 0.5 * (1.0 + bend)
            act[pair(k), cols] = (pre * half).astype(BF16)
            slope = half + 0.5 * pre * (1.0 - bend * bend) * (
                0.7978845608028654 * (1.0 + 3 * 0.044715 * square))
            pg[pair(k), cols] = (back * slope).astype(BF16)
        act_over(k).start()
        rows = pg[pair(k), :]
        produce(2, k, [(j, nt(rows, wup[j : j + 256, :])) for j in range(0, 1024, 256)])

    finish(2, STEPS - 1)

    def up_piece(c):
        return Piece(place, ug.at[c], ux.at[c], uz.at[c], (us_sem.at[0, c], ur_sem.at[0, c]),
                     (ds_sem.at[0, c], dr_sem.at[0, c]))

    def down_piece(c):
        return Piece(place, None, dx.at[c], dz.at[c], None, (ds_sem.at[1, c], dr_sem.at[1, c]))

    def down_grad(c):
        mine_left = act[:, pl.ds(pl.multiple_of(group * 512 + c * 128, 128), 128)]
        other_left = act2[:, pl.ds(pl.multiple_of(c * 128, 128), 128)]
        for m in range(4):
            lanes = slice(m * 256, m * 256 + 256)
            value = (tn(mine_left, og[:, lanes]) + tn(other_left, og2[:, lanes])).astype(BF16)
            for u in range(per):
                dx[c, m * per + u] = value[:, u * span : (u + 1) * span]
        down_piece(c).spread()

    def own_rows(k):
        return jnp.where(k // 2 == chip, 1.0, 0.0)

    @pl.loop(0, STEPS)
    def _(k):
        @pl.when(k == 1)
        def _():
            for i in range(STEPS):
                act_over(i).wait_recv()
                grads_on(i).wait_recv()

        @pl.when((k == 1) | (k == 2))
        def _():
            down_grad(2 * k - 2)
            down_grad(2 * k - 1)

        at = pl.multiple_of(k * 256, 256)
        right = pg[:, pl.ds(at, 256)]
        for m in range(4):
            value = tn(nf[1, :, m * 256 : m * 256 + 256], right).astype(BF16)
            for u in range(per):
                ug[k, m * per + u, 0] = value[u * span : u * span + span // 2]
                ug[k, m * per + u, 1] = value[u * span + span // 2 : (u + 1) * span]
        up_piece(k).start()

        @pl.when(k == 2)
        def _():
            down_piece(0).pass_on()

        @pl.when(k == 3)
        def _():
            up_piece(0).add()
            up_piece(0).spread()
            down_piece(1).pass_on()

        far_copy(2, k).wait_recv()
        keep = own_rows(k)
        for r in range(CHUNK // SUB):
            third = acc[sub(k, r)] + yr[2, sub(k, r)].astype(F32)
            xhat, rstd = norm_stats(h2[sub(k, r)])
            parts[2] += fold_rows(third * xhat) * keep
            parts[3] += fold_rows(third) * keep
            resid = og[msub(k, r)].astype(F32) + norm_input_grad(xhat, rstd, mg_ref[...], third)
            g2[sub(k, r)] = resid
            nf[2, msub(k, r)] = resid.astype(BF16)
        norm_copy(2, k).start()

        @pl.when(k > 0)
        def _():
            finish(3, k - 1)

        norm_copy(2, k).wait_recv()
        mix_grad = nt(nf[2, pair(k)], wco[...]).astype(BF16)
        for slab in range(2):
            lanes = slice(slab * 128, slab * 128 + 128)
            query = cq[pair(k), lanes]
            grad = mix_grad[:, lanes]
            key, value = ck_ref[:, lanes], cv_ref[:, lanes]
            moved = []
            for part in range(2):
                one_q, one_g = pick(query, part), pick(grad, part)
                scores = nt(one_q, key) * scale + bias_ref[...]
                shifted = jnp.exp(scores - jnp.max(scores, axis=-1, keepdims=True))
                probs = shifted / jnp.sum(shifted, axis=-1, keepdims=True)
                prob_grad = nt(one_g, value)
                inner = jnp.sum(probs * prob_grad, axis=-1, keepdims=True)
                score_grad = (probs * (prob_grad - inner)).astype(BF16)
                moved.append(nn(score_grad, key) * scale)
                dkv[0, :, lanes] += tn(score_grad, one_q)
                dkv[1, :, lanes] += tn(probs.astype(BF16), one_g)
            cqg[pair(k), lanes] = merge(*moved).astype(BF16)
        rows = cqg[pair(k), :]
        produce(3, k, [(j, nt(rows, wcq[j : j + 512, :])) for j in (0, 512)])

    finish(3, STEPS - 1)
    dck_out[...] = (dkv[0] * scale).astype(BF16)
    dcv_out[...] = dkv[1].astype(BF16)
    captions = [
        pltpu.make_async_remote_copy(
            src, dst, xs_sem.at[2, i], xr_sem.at[2, i], device_id={"grp": 1 - group}, device_id_type=MESH)
        for i, (src, dst) in enumerate([(dck_out, dck_over), (dcv_out, dcv_over)])
    ]
    for copy in captions:
        copy.start()

    def quarter(k):
        return pl.ds(pl.multiple_of(k * per, per), per)

    def query_over(k):
        return pltpu.make_async_remote_copy(
            dcq.at[quarter(k), 1 - group], cqx.at[quarter(k)], us_sem.at[1, k], ur_sem.at[1, k],
            device_id={"grp": 1 - group}, device_id_type=MESH)

    def output_over(k):
        return pltpu.make_async_remote_copy(
            dco.at[quarter(k), 1 - group], cox.at[quarter(k)], us_sem.at[2, k], ur_sem.at[2, k],
            device_id={"grp": 1 - group}, device_id_type=MESH)

    def down_give(k):
        return pltpu.make_async_remote_copy(
            df.at[k, group], df.at[k, group], us_sem.at[3, k], ur_sem.at[3, k],
            device_id={"grp": 1 - group}, device_id_type=MESH)

    @pl.loop(0, STEPS)
    def _(k):
        at = pl.multiple_of(k * 256, 256)
        value = tn(nf[0, :, pl.ds(at, 256)], cqg[...]).astype(BF16)
        for u in range(per):
            dcq[k * per + u, 0] = value[u * span : u * span + span // 2]
            dcq[k * per + u, 1] = value[u * span + span // 2 : (u + 1) * span]
        value = tn(cmix[...], nf[2, :, pl.ds(at, 256)]).astype(BF16)
        for u in range(per):
            dco[k * per + u, 0] = value[:128, u * span : (u + 1) * span]
            dco[k * per + u, 1] = value[128:, u * span : (u + 1) * span]

        query_over(k).start()
        output_over(k).start()

    def layer_red(k):
        return pltpu.make_async_remote_copy(
            yr.at[0, own(k)], rr.at[0, own(k)], ls_sem.at[k], lr_sem.at[k],
            device_id={"tp": pal}, device_id_type=MESH)

    @pl.loop(0, STEPS)
    def _(k):
        rows = act[pair(k), :]
        for j in (0, 512):
            pbuf[:, j : j + 512] = nn(rows, wdn[:, j : j + 512])
        yr[0, own(k)] = pbuf[pl.ds(pl.multiple_of((1 - core) * CHUNK, CHUNK), CHUNK), :].astype(BF16)
        layer_red(k).start()
        h2[own(k)] = h2[own(k)] * own_rows(k) + pbuf[pl.ds(pl.multiple_of(core * CHUNK, CHUNK), CHUNK), :]

    mine_rows = pl.ds(pl.multiple_of(chip * 256, 256), 256)
    their_rows = pl.ds(pl.multiple_of((1 - chip) * 256, 256), 256)
    cross_copy = pltpu.make_async_copy(h2.at[mine_rows], ac_out, out_sem.at[27])
    layer_copy = pltpu.make_async_copy(xr.at[their_rows], lay_out, out_sem.at[2])
    summed = [
        pltpu.make_async_copy(cqx, dcq_out, out_sem.at[28]),
        pltpu.make_async_copy(cox, dco_out, out_sem.at[29]),
    ]

    @pl.loop(0, STEPS)
    def _(k):
        @pl.when(k == 0)
        def _():
            down_piece(2).pass_on()
            for c in (1, 2):
                up_piece(c).add()
                up_piece(c).spread()
            down_piece(3).pass_on()

        @pl.when(k == 1)
        def _():
            up_piece(3).add()
            up_piece(3).spread()
            up_piece(0).pass_on()

        @pl.when(k == 2)
        def _():
            up_piece(1).pass_on()

        df[k, group] = down_piece(k).total()
        down_give(k).start()
        layer_red(k).wait_recv()
        total = h2[own(k)] + rr[0, own(k)].astype(F32)
        h2[own(k)] = total
        xr[own(k)] = total.astype(BF16)

        @pl.when(k == 3)
        def _():
            for i in range(STEPS):
                query_over(i).wait_recv()
                output_over(i).wait_recv()

            @pl.loop(0, dp)
            def _(d):
                cqx[d] = (cqx[d].astype(F32) + dcq[d, group].astype(F32)).astype(BF16)
                cox[d] = (cox[d].astype(F32) + dco[d, group].astype(F32)).astype(BF16)

            for copy in summed + [cross_copy, layer_copy]:
                copy.start()
            up_piece(2).pass_on()
            up_piece(3).pass_on()

        far_copy(3, k).wait_recv()
        keep = own_rows(k)
        for r in range(CHUNK // SUB):
            second = acc[sub(k, r)] + yr[3, sub(k, r)].astype(F32)
            xhat, rstd = norm_stats(h1[sub(k, r)])
            parts[0] += fold_rows(second * xhat) * keep
            parts[1] += fold_rows(second) * keep
            resid = g2[sub(k, r)] + norm_input_grad(xhat, rstd, cg_ref[...], second)
            g2[sub(k, r)] = resid
            nf[3, msub(k, r)] = resid.astype(BF16)
        norm_copy(3, k).start()
        norm_copy(3, k).wait_recv()
        smg[pair(k)] = nt(nf[3, pair(k)], wo[...]).astype(BF16)
        for c in range(2):
            settle(smg, smg_out, k, c, 10).start()
            settle(nf.at[3], sb_out, k, c, 18).start()

    resid_copy = pltpu.make_async_copy(g2.at[mine_rows], resid_out, out_sem.at[26])
    resid_copy.start()
    for c in range(4):
        uf[c] = up_piece(c).total()
    sums_copy = pltpu.make_async_copy(uf, uf_out, out_sem.at[30])
    sums_copy.start()
    for k in range(STEPS):
        down_give(k).wait_recv()
    down_copy = pltpu.make_async_copy(df, df_out, out_sem.at[31])
    down_copy.start()
    late = [resid_copy, sums_copy, down_copy, cross_copy, layer_copy] + summed
    for copy in captions:
        copy.wait()
    parts_out[...] = parts[...]
    for k in range(STEPS):
        red_copy(3, k).wait_send()
        far_copy(3, k).wait_send()
        for s in range(4):
            norm_copy(s, k).wait_send()
        layer_red(k).wait_send()
        grads_over(k).wait_send()
        grads_on(k).wait_send()
        act_over(k).wait_send()
        query_over(k).wait_send()
        output_over(k).wait_send()
        down_give(k).wait_send()
        for c in range(2):
            settle(smg, smg_out, k, c, 10).wait()
            settle(nf.at[3], sb_out, k, c, 18).wait()
    for c in range(4):
        up_piece(c).x_end()
        down_piece(c).z_end()
        up_piece(c).z_end()
    for copy in late:
        copy.wait()


def middle(dp, x_full, self_mix, out_grad, wo, wcq, wco, wup, wdn, ck, cv, bias, gains):
    full = jax.ShapeDtypeStruct((1024, 1024), BF16)
    narrow = jax.ShapeDtypeStruct((1024, 256), BF16)
    short = jax.ShapeDtypeStruct((128, 256), BF16)
    block = jax.ShapeDtypeStruct((256, 1024), F32)
    part = 1024 // dp
    rows, columns = (part // 2, 256), (128, part)
    outs = [
        narrow, full, jax.ShapeDtypeStruct((256, 1024), BF16)] + [
        jax.ShapeDtypeStruct(item, BF16)
        for item in ((4,) + rows, (4, 2) + columns, (dp,) + rows, (dp,) + columns)
    ] + [short, short, short, short,
        jax.ShapeDtypeStruct((4, 8, 1024), F32), block, block,
    ]
    out_specs = [ANY] * 7 + [VM] * 5 + [ANY] * 2
    vm = pltpu.VMEM
    dma = pltpu.SemaphoreType.DMA
    scratch = [
        vm((256, 1024), BF16), vm((1024, 256), BF16), vm((256, 1024), BF16), vm((1024, 1024), BF16),
        vm((1024, 1024), BF16), vm((1024, 256), BF16), vm((1024, 1024), BF16), vm((512, 1024), BF16),
        vm((512, 1024), F32), vm((512, 1024), F32), vm((512, 1024), F32), vm((512, 1024), F32),
        vm((4, 1024, 1024), BF16), vm((1024, 1024), BF16), vm((1024, 1024), BF16),
        vm((1024, 256), BF16), vm((1024, 256), BF16), vm((1024, 256), BF16),
        vm((4, 512, 1024), BF16), vm((4, 512, 1024), BF16), vm((512, 1024), BF16), vm((512, 1024), BF16),
        vm((256, 1024), F32), vm((2, 128, 256), F32), vm((1024, 256), BF16),
        vm((1024, 1024), BF16), vm((1024, 512), BF16),
        vm((4, dp, 2) + rows, BF16), vm((4, dp) + rows, BF16), vm((4, dp) + columns, BF16),
        vm((4, slots(dp)) + rows, BF16), vm((4, slots(dp)) + columns, BF16), vm((4,) + rows, BF16), vm((4, 2) + columns, BF16),
        vm((dp, 2) + columns, BF16), vm((dp, 2) + rows, BF16), vm((dp,) + columns, BF16), vm((dp,) + rows, BF16),
        vm((4, 8, 1024), F32),
        dma((32,)), dma((4, 4)), dma((4, 4)), dma((4, 4)), dma((4, 4)), dma((4, 4)), dma((4, 4)),
        dma((3, 4)), dma((3, 4)), dma((4, 4)), dma((4, 4)), dma((2, 4, dp - 1)), dma((2, 4, dp - 1)),
        dma((4,)), dma((4,)), dma((4,)), dma((4,)), dma((32,)),
    ]
    return pl.pallas_call(
        functools.partial(middle_kernel, dp),
        out_shape=outs,
        in_specs=[ANY] * 8 + [VM] * 7,
        out_specs=out_specs,
        scratch_shapes=scratch,
        name="middle",
        compiler_params=pltpu.CompilerParams(
            collective_id=1, has_side_effects=True, vmem_limit_bytes=GRANT),
    )(x_full, self_mix, out_grad, wo, wcq, wco, wup, wdn, ck, cv, bias, *gains)


def front_kernel(
    x_own, wq_h, wk_h, wv_h, text_h, wck_h, wcv_h, ag_ref, as_ref,
    x_out, n1_out, q_out, k_out, v_out, mix_out, p0_out, p1_out, p2_out, p3_out, text_out, ck_out, cv_out,
    xf, n1, q, k, v, mix, p0, p1, p2, p3, wq, wk, wv, text, wck, wcv, theirs,
    load_sem, text_s, text_r, y_s, y_r, c_s, c_r, f_s, f_r, out_sem,
):
    rank = lax.axis_index("tp")
    core = lax.rem(rank, 2)
    pal = rank + 1 - 2 * core
    far = lax.rem(rank + 2, 4)
    beyond = lax.rem(pal + 2, 4)
    barrier = pltpu.get_barrier_semaphore()
    for peer in (pal, far):
        pl.semaphore_signal(barrier, inc=1, device_id={"tp": peer}, device_id_type=MESH)
    group = lax.axis_index("grp")
    pl.semaphore_signal(barrier, inc=1, device_id={"grp": 1 - group}, device_id_type=MESH)
    captions = pltpu.make_async_remote_copy(
        text_h, theirs, text_s.at[0], text_r.at[0], device_id={"grp": 1 - group}, device_id_type=MESH)
    loads = [
        pltpu.make_async_copy(src, dst, load_sem.at[i])
        for i, (src, dst) in enumerate([
            (x_own, xf.at[pl.ds(pl.multiple_of(rank * 256, 256), 256)]),
            (text_h, text), (wck_h, wck), (wcv_h, wcv), (wq_h, wq), (wk_h, wk), (wv_h, wv)])
    ]
    for copy in loads:
        copy.start()

    def part(block, i, size):
        return pl.ds(pl.multiple_of(block * 256 + i * size, size), size)

    across = [
        pltpu.make_async_remote_copy(
            x_own.at[pl.ds(i * 64, 64)], xf.at[part(rank, i, 64)], y_s.at[i], y_r.at[i],
            device_id={"tp": far}, device_id_type=MESH)
        for i in range(4)
    ]
    beside = pltpu.make_async_remote_copy(
        x_own, xf.at[part(rank, 0, 256)], c_s.at[0], c_r.at[0], device_id={"tp": pal}, device_id_type=MESH)
    onward = [
        pltpu.make_async_remote_copy(
            xf.at[part(far, i, 64)], xf.at[part(far, i, 64)], f_s.at[i], f_r.at[i],
            device_id={"tp": pal}, device_id_type=MESH)
        for i in range(4)
    ]
    pl.semaphore_wait(barrier, 3)
    for copy in across:
        copy.start()
    beside.start()
    captions.start()

    for copy in loads[1:4]:
        copy.wait()
    ck_out[...] = nn(text[...], wck[...]).astype(BF16)
    cv_out[...] = nn(text[...], wcv[...]).astype(BF16)
    for copy in loads[4:] + loads[:1]:
        copy.wait()

    def project(block, i):
        for r in range(4):
            rows = pl.ds(pl.multiple_of(block * 256 + i * 128 + r * 32, 32), 32)
            xhat, _ = norm_stats(xf[rows].astype(F32))
            n1[rows] = (xhat * ag_ref[...] + as_ref[...]).astype(BF16)
        rows = part(block, i, 128)
        value = n1[rows]
        q[rows] = (nn(value, wq[...]).astype(BF16) * 0.125).astype(BF16)
        k[rows] = nn(value, wk[...]).astype(BF16)
        v[rows] = nn(value, wv[...]).astype(BF16)

    def both(block):
        @pl.loop(0, 2)
        def _(i):
            project(block, i)

    both(rank)
    beside.wait_recv()
    both(pal)
    for half in range(2):
        for i in (2 * half, 2 * half + 1):
            across[i].wait_recv()
            onward[i].start()
        project(far, half)
        for i in (2 * half, 2 * half + 1):
            onward[i].wait_recv()
        project(beyond, half)
    outs = [
        pltpu.make_async_copy(src, dst, out_sem.at[i])
        for i, (src, dst) in enumerate([(xf, x_out), (n1, n1_out), (q, q_out), (k, k_out), (v, v_out)])
    ]
    for copy in outs:
        copy.start()

    captions.wait_recv()
    caption_out = pltpu.make_async_copy(theirs, text_out, out_sem.at[10])
    caption_out.start()

    kept = (p0, p1, p2, p3)
    below = lax.broadcasted_iota(jnp.int32, (256, 256), 0) >= lax.broadcasted_iota(jnp.int32, (256, 256), 1)

    @pl.loop(0, 2)
    def _(slab):
        lanes = pl.ds(pl.multiple_of(slab * 128, 128), 128)
        for i in range(4):
            done, end = i * 256, i * 256 + 256
            query = q[done:end, lanes]
            mixed = []
            for half in range(2):
                one = pick(query, half)
                diag = jnp.where(below, nt(one, k[done:end, lanes]), MASKED)
                peak = jnp.max(diag, axis=-1, keepdims=True)
                if i:
                    past = nt(one, k[0:done, lanes])
                    peak = jnp.maximum(peak, jnp.max(past, axis=-1, keepdims=True))
                    past = jnp.exp(past - peak)
                diag = jnp.exp(diag - peak)
                total = jnp.sum(diag, axis=-1, keepdims=True)
                if i:
                    total = total + jnp.sum(past, axis=-1, keepdims=True)
                inverse = 1.0 / total
                probs = (diag * inverse).astype(BF16)
                kept[i][slab * 2 + half, :, done:end] = probs
                out = nn(probs, v[done:end, lanes])
                if i:
                    probs = (past * inverse).astype(BF16)
                    kept[i][slab * 2 + half, :, 0:done] = probs
                    out = out + nn(probs, v[0:done, lanes])
                mixed.append(out)
            mix[done:end, lanes] = merge(*mixed).astype(BF16)

    tail = [
        pltpu.make_async_copy(src, dst, out_sem.at[5 + i])
        for i, (src, dst) in enumerate(
            [(mix, mix_out), (p0, p0_out), (p1, p1_out), (p2, p2_out), (p3, p3_out)])
    ]
    for copy in tail:
        copy.start()
    for copy in across + [beside, captions] + onward:
        copy.wait_send()
    for copy in outs + tail + [caption_out]:
        copy.wait()


def front(x_own, wq, wk, wv, text, wck, wcv, gains):
    full = ((1024, 1024), BF16)
    narrow = ((1024, 256), BF16)
    short = ((128, 256), BF16)
    probs = [((4, 256, 256 * (i + 1)), BF16) for i in range(4)]
    vm = pltpu.VMEM
    dma = pltpu.SemaphoreType.DMA
    return pl.pallas_call(
        front_kernel,
        out_shape=[jax.ShapeDtypeStruct(*item) for item in [full, full, narrow, narrow, narrow, narrow] + probs + [((128, 1024), BF16), short, short]],
        in_specs=[ANY] * 7 + [VM] * 2,
        out_specs=[ANY] * 11 + [VM] * 2,
        scratch_shapes=[vm(*item) for item in [full, full, narrow, narrow, narrow, narrow] + probs
                        + [narrow] * 3 + [((128, 1024), BF16), narrow, narrow, ((128, 1024), BF16)]]
        + [dma((8,)), dma((1,)), dma((1,)), dma((4,)), dma((4,)), dma((1,)), dma((1,)), dma((4,)), dma((4,)), dma((12,))],
        name="front",
        compiler_params=pltpu.CompilerParams(
            collective_id=2, has_side_effects=True, vmem_limit_bytes=GRANT),
    )(x_own, wq, wk, wv, text, wck, wcv, *gains)


def back_kernel(dp, *refs):
    refs = list(refs)

    def take(n):
        taken, refs[:n] = refs[:n], []
        return taken

    (smix_h, sb_h, lay_h, smg_h, q_h, k_h, v_h, p0_h, p1_h, p2_h, p3_h, n1_h, wq_h, wk_h, wv_h,
     x_own, resid_h, ac_h, dcq_h, dco_h, uf_h) = take(21)
    text, text_over, wck, wcv, dck, dcv, dck_over, dcv_over, parts_in, ag_ref = take(10)
    layer_out, image_grad, text_out, norm_out, up_o, cq_o, co_o, so_o, ck_o, cv_o, sq_o, sk_o, sv_o = take(13)
    (smix, sb, smg, q, k, v, p0, p1, p2, p3, n1, wqkv, xo, resid, ac) = take(15)
    so_g, ck_g, cv_g, self_g = take(4)
    x_bufs, self_x, z_bufs, self_z = take(5), take(1)[0], take(5), take(1)[0]
    (dqkv, dkv, acc, sst, rr, yst, yr, lay, tpart, t_st, t_rr, t_yst, t_yr, t_fin, npart, n_tp, nsum, n_all) = take(18)
    (load_sem, xs, xr, zs, zr, gs, gr, cs_sem, cr_sem, ys_sem, yr_sem, ls, lr, t_s, t_r, n_s, n_r, m_s, m_r) = take(19)

    rank = lax.axis_index("tp")
    group = lax.axis_index("grp")
    depth = lax.axis_index("dp")
    core = lax.rem(rank, 2)
    chip = rank // 2
    pal = rank + 1 - 2 * core
    far = lax.rem(rank + 2, 4)
    others = [(g, r) for g in range(2) for r in range(dp) if g or r]
    barrier = pltpu.get_barrier_semaphore()
    for r in range(1, 4):
        pl.semaphore_signal(barrier, inc=1, device_id={"tp": lax.rem(rank + r, 4)}, device_id_type=MESH)

    def at_other(g, r):
        return {"grp": lax.rem(group + g, 2), "dp": lax.rem(depth + r, dp)}

    for g, r in others:
        pl.semaphore_signal(barrier, inc=1, device_id=at_other(g, r), device_id_type=MESH)

    pairs = [
        (dcq_h, x_bufs[0]), (dco_h, x_bufs[1]),
        (smix_h, smix), (sb_h, sb),
        (smg_h, smg), (q_h, q), (k_h, k), (v_h, v), (p0_h, p0), (p1_h, p1), (p2_h, p2), (p3_h, p3), (n1_h, n1)]
    pairs += [
        (weight.at[:, h * 128 : h * 128 + 128], wqkv.at[:, h * 384 + i * 128 : h * 384 + i * 128 + 128])
        for h in range(2) for i, weight in enumerate((wq_h, wk_h, wv_h))]
    pairs += [(x_own, xo), (resid_h, resid), (ac_h, ac)]
    pairs += [(uf_h.at[c], up_o.at[c, group]) for c in range(4)]
    loads = [pltpu.make_async_copy(src, dst, load_sem.at[i]) for i, (src, dst) in enumerate(pairs)]
    for copy in loads[:13]:
        copy.start()

    place = (group, depth, dp)

    def piece(n, source=None):
        return Piece(place, source, x_bufs[n], z_bufs[n], (xs.at[n], xr.at[n]), (zs.at[n], zr.at[n]))

    def self_piece(h, i):
        n = 3 * h + i
        return Piece(place, self_g.at[n], self_x.at[n], self_z.at[n], (xs.at[5 + n], xr.at[5 + n]),
                     (zs.at[5 + n], zr.at[5 + n]))

    def give(n, src, out):
        return pltpu.make_async_remote_copy(
            src, out, gs.at[n], gr.at[n], device_id={"grp": 1 - group}, device_id_type=MESH)

    cq_p, co_p, so_p, ck_p, cv_p = [
        piece(n, source) for n, source in enumerate((None, None, so_g, None, None))]
    halves = [(cq_p, cq_o), (co_p, co_o), (so_p, so_o), (ck_p, ck_o), (cv_p, cv_o)]
    halves += [(self_piece(h, i), out.at[h]) for h in range(2) for i, out in enumerate((sq_o, sk_o, sv_o))]
    gives = [give(n, out.at[group], out.at[group]) for n, (_, out) in enumerate(halves)]
    early = [give(12 + c, uf_h.at[c], up_o.at[c, group]) for c in range(4)]

    def finish(n):
        one, out = halves[n]
        out[group] = one.total()
        gives[n].start()

    layer = [
        pltpu.make_async_remote_copy(
            lay_h.at[pl.ds(j * CHUNK, CHUNK)], lay.at[pl.ds(j * CHUNK, CHUNK)], ls.at[j], lr.at[j],
            device_id={"tp": far}, device_id_type=MESH)
        for j in range(2)
    ]
    pl.semaphore_wait(barrier, 3 + len(others))
    for copy in layer:
        copy.start()
    for copy in loads[:2]:
        copy.wait()
    cq_p.spread()
    co_p.spread()

    scale = HEAD ** (-0.5)
    depth_rows = 1024 // dp
    per = 256 // depth_rows

    def caption_grad(one, ref, ours, theirs):
        for m in range(4):
            lanes = slice(m * 256, m * 256 + 256)
            value = (tn(text[:, lanes], ours[...]) + tn(text_over[:, lanes], theirs[...])).astype(BF16)
            for u in range(per):
                part = value[u * depth_rows : (u + 1) * depth_rows]
                ref[m * per + u, 0] = part[: depth_rows // 2]
                ref[m * per + u, 1] = part[depth_rows // 2 :]

        @pl.loop(0, dp)
        def _(d):
            one.x_buf[d] = ref[d, group]

        one.spread()

    def own(i):
        return pl.ds(pl.multiple_of(i * CHUNK, CHUNK), CHUNK)

    class Scatter:
        def __init__(self, n):
            self.n = n

        def red(self, i):
            n = self.n
            return pltpu.make_async_remote_copy(
                sst.at[n, own(i)], rr.at[n, own(i)], cs_sem.at[n, i], cr_sem.at[n, i],
                device_id={"tp": pal}, device_id_type=MESH)

        def far(self, j):
            n = self.n
            return pltpu.make_async_remote_copy(
                yst.at[n, own(j)], yr.at[n, own(j)], ys_sem.at[n, j], yr_sem.at[n, j],
                device_id={"tp": far}, device_id_type=MESH)

        def put(self, i, theirs, ours):
            sst[self.n, own(i)] = theirs.astype(BF16)
            self.red(i).start()
            acc[self.n, own(i)] = ours

        def send(self, j):
            i = 2 * (1 - chip) + j
            self.red(i).wait_recv()
            yst[self.n, own(j)] = (acc[self.n, own(i)] + rr[self.n, own(i)].astype(F32)).astype(BF16)
            self.far(j).start()

        def keep(self, j):
            self.red(2 * chip + j).wait_recv()
            self.far(j).wait_recv()

        def value(self, j, r):
            i = 2 * chip + j
            rows = pl.ds(pl.multiple_of(i * CHUNK + r * SUB, SUB), SUB)
            near = pl.ds(j * CHUNK + r * SUB, SUB)
            return acc[self.n, rows] + rr[self.n, rows].astype(F32) + yr[self.n, near].astype(F32)

        def end(self):
            for i in range(4):
                self.red(i).wait_send()
            for j in range(2):
                self.far(j).wait_send()

    first = Scatter(0)

    def sequence(step):
        return lax.rem(2 * (1 - chip) + step, 4)

    for copy in loads[2:4]:
        copy.wait()
    for copy in loads[13:]:
        copy.start()
    for d in range(dp):
        value = tn(smix[...], sb[:, d * depth_rows : (d + 1) * depth_rows]).astype(BF16)
        so_g[d, 0] = value[:128]
        so_g[d, 1] = value[128:]
    so_p.start()
    for copy in early:
        copy.start()

    caption_grad(ck_p, ck_g, dck, dck_over)
    caption_grad(cv_p, cv_g, dcv, dcv_over)
    tpart[...] = nt(dck[...], wck[...]) + nt(dcv[...], wcv[...])

    def t_rows(c):
        return pl.ds(pl.multiple_of(c * 64, 64), 64)

    t_st[...] = tpart[t_rows(1 - core)].astype(BF16)
    t_red = pltpu.make_async_remote_copy(
        t_st, t_rr, t_s.at[0], t_r.at[0], device_id={"tp": pal}, device_id_type=MESH)
    t_red.start()

    for copy in loads[4:13]:
        copy.wait()
    dkv[...] = jnp.zeros_like(dkv)
    kept = (p0, p1, p2, p3)

    @pl.loop(0, 2)
    def _(slab):
        lanes = pl.ds(pl.multiple_of(slab * 128, 128), 128)
        for i in range(4):
            begin, end = i * 256, i * 256 + 256
            query, grad = q[begin:end, lanes], smg[begin:end, lanes]
            product = grad.astype(F32) * smix[begin:end, lanes].astype(F32)
            moved = []
            for half in range(2):
                one_q, one_g = pick(query, half), pick(grad, half)
                inner = jnp.sum(pick(product, half), axis=-1, keepdims=True)
                probs = kept[i][slab * 2 + half]
                prob_grad = nt(one_g, v[0:end, lanes])
                score_grad = (probs.astype(F32) * (prob_grad - inner)).astype(BF16)
                moved.append(nn(score_grad, k[0:end, lanes]))
                dkv[0, 0:end, lanes] += tn(score_grad, one_q)
                dkv[1, 0:end, lanes] += tn(probs, one_g)
            moved = (merge(*moved) * scale).astype(BF16)
            dqkv[begin:end, pl.ds(pl.multiple_of(slab * 384, 128), 128)] = moved
            if i == 1:
                @pl.when(slab == 0)
                def _():
                    cq_p.pass_on()

                @pl.when(slab == 1)
                def _():
                    ck_p.pass_on()
                    finish(0)
            if i == 2:
                @pl.when(slab == 0)
                def _():
                    so_p.add()
                    so_p.spread()

                @pl.when(slab == 1)
                def _():
                    cv_p.pass_on()
                    finish(1)
            if i == 3:
                @pl.when(slab == 0)
                def _():
                    co_p.pass_on()

                @pl.when(slab == 1)
                def _():
                    so_p.pass_on()
                    finish(3)

        dqkv[:, pl.ds(pl.multiple_of(slab * 384 + 128, 128), 128)] = dkv[0, :, lanes].astype(BF16)
        dqkv[:, pl.ds(pl.multiple_of(slab * 384 + 256, 128), 128)] = dkv[1, :, lanes].astype(BF16)
        right = dqkv[:, pl.ds(pl.multiple_of(slab * 384, 128), 384)]
        for m in range(4):
            value = tn(n1[:, m * 256 : m * 256 + 256], right).astype(BF16)
            for u in range(per):
                part = value[u * depth_rows : (u + 1) * depth_rows]
                for n in range(3):
                    self_g[slab * 3 + n, m * per + u, 0] = part[: depth_rows // 2, n * 128 : n * 128 + 128]
                    self_g[slab * 3 + n, m * per + u, 1] = part[depth_rows // 2 :, n * 128 : n * 128 + 128]
        for n in range(3):
            self_piece(slab, n).start()

    t_red.wait_recv()
    t_yst[...] = (tpart[t_rows(core)] + t_rr[...].astype(F32)).astype(BF16)
    t_far = pltpu.make_async_remote_copy(
        t_yst, t_yr, t_s.at[1], t_r.at[1], device_id={"tp": far}, device_id_type=MESH)
    t_far.start()
    for copy in loads[13:]:
        copy.wait()

    @pl.loop(0, 4)
    def _(step):
        i = sequence(step)

        def partial(c):
            start = pl.multiple_of(256 * (c + 2 * (i // 2)) + 128 * lax.rem(i, 2), 128)
            rows = pl.ds(start, CHUNK)
            return nt(dqkv[rows], wqkv[...])

        first.put(i, partial(1 - core), partial(core))

        @pl.when((step > 0) & (step < 3))
        def _():
            first.send(step - 1)

        @pl.when(step < 3)
        def _():
            self_piece(0, step).add()
            self_piece(0, step).spread()

    for n in range(3):
        self_piece(0, n).pass_on()
    for n in (4, 2):
        finish(n)
    for j in range(2):
        layer[j].wait_recv()
        for r in range(CHUNK // SUB):
            rows = slice(j * CHUNK + r * SUB, j * CHUNK + r * SUB + SUB)
            layer_out[rows] = (ac[rows] + lay[rows].astype(F32)).astype(BF16)

    for n in range(3):
        self_piece(1, n).add()
        self_piece(1, n).spread()
    t_far.wait_recv()
    t_fin[t_rows(core)] = (t_yst[...].astype(F32) + t_yr[...].astype(F32)).astype(BF16)
    t_share = pltpu.make_async_remote_copy(
        t_fin.at[t_rows(core)], t_fin.at[t_rows(core)], t_s.at[2], t_r.at[2],
        device_id={"tp": pal}, device_id_type=MESH)
    t_share.start()
    for n in range(5, 8):
        finish(n)
    for n in range(3):
        self_piece(1, n).pass_on()

    npart[...] = jnp.zeros_like(npart)
    for j in range(2):
        first.keep(j)
        for r in range(CHUNK // SUB):
            rows = slice(j * CHUNK + r * SUB, j * CHUNK + r * SUB + SUB)
            given = first.value(j, r)
            xhat, rstd = norm_stats(xo[rows].astype(F32))
            npart[0] += fold_rows(given * xhat)
            npart[1] += fold_rows(given)
            image_grad[rows] = resid[rows] + norm_input_grad(xhat, rstd, ag_ref[...], given)

    def line(ref, i):
        return jnp.sum(ref[i], axis=0, keepdims=True)

    n_tp[rank] = jnp.concatenate(
        [line(npart, 0), line(npart, 1)] + [line(parts_in, i) for i in range(4)]
        + [jnp.zeros((2, 1024), F32)], axis=0)
    n_copies = [
        pltpu.make_async_remote_copy(
            n_tp.at[rank], n_tp.at[rank], n_s.at[r - 1], n_r.at[r - 1],
            device_id={"tp": lax.rem(rank + r, 4)}, device_id_type=MESH)
        for r in range(1, 4)
    ]
    for copy in n_copies:
        copy.start()
    for n in range(8, 11):
        finish(n)
    for copy in n_copies:
        copy.wait_recv()
    summed = n_tp[0] + n_tp[1] + n_tp[2] + n_tp[3]
    for d in range(dp):
        nsum[d] = summed[:, d * depth_rows : (d + 1) * depth_rows]
    slot = group * dp + depth
    m_copies = [
        pltpu.make_async_remote_copy(
            nsum.at[lax.rem(depth + r, dp)], n_all.at[slot], m_s.at[i], m_r.at[i],
            device_id=at_other(g, r), device_id_type=MESH)
        for i, (g, r) in enumerate(others)
    ]
    for copy in m_copies:
        copy.start()
    n_all[slot] = nsum[depth]

    for copy in m_copies:
        copy.wait_recv()
    total = n_all[0]
    for i in range(1, 2 * dp):
        total = total + n_all[i]
    norm_out[...] = total
    t_share.wait_recv()
    text_out[...] = t_fin[...]
    for copy in m_copies + n_copies + [t_red, t_far, t_share]:
        copy.wait_send()
    for copy in layer:
        copy.wait_send()
    first.end()
    for n, (one, _) in enumerate(halves):
        if n not in (0, 1, 3, 4):
            one.x_end()
        one.z_end()
        gives[n].wait()
    for copy in early:
        copy.wait()


def back(dp, *operands):
    part = 1024 // dp
    full = ((1024, 1024), BF16)
    narrow = ((1024, 256), BF16)
    probs = [((4, 256, 256 * (i + 1)), BF16) for i in range(4)]
    rows, columns = (part // 2, 256), (128, part)
    block = ((256, 1024), F32)
    kinds = [rows, columns, columns, rows, rows]
    slabs = (part // 2, 128)
    outs = [((256, 1024), BF16), block, ((128, 1024), BF16), ((8, part), F32), ((4, 2) + rows, BF16)]
    outs += [((2,) + s, BF16) for s in (rows, columns, columns, rows, rows)] + [((2, 2) + slabs, BF16)] * 3
    scratch = (
        [narrow, full] + [narrow] * 4 + probs + [full] + [((1024, 768), BF16)]
        + [((256, 1024), BF16), block, block]
        + [((dp, 2) + s, BF16) for s in (columns, rows, rows)] + [((6, dp, 2) + slabs, BF16)]
        + [((dp,) + s, BF16) for s in kinds] + [((6, dp) + slabs, BF16)]
        + [((slots(dp),) + s, BF16) for s in kinds] + [((6, slots(dp)) + slabs, BF16)]
        + [((1024, 768), BF16)]
        + [((2, 1024, 256), F32), ((1, 512, 1024), F32), ((1, 512, 1024), BF16), ((1, 512, 1024), BF16),
           ((1, 256, 1024), BF16), ((1, 256, 1024), BF16), ((256, 1024), BF16), ((128, 1024), F32),
           ((64, 1024), BF16), ((64, 1024), BF16), ((64, 1024), BF16), ((64, 1024), BF16), ((128, 1024), BF16),
           ((2, 8, 1024), F32), ((4, 8, 1024), F32), ((dp, 8, part), F32), ((2 * dp, 8, part), F32)]
    )
    dma = pltpu.SemaphoreType.DMA
    many = 2 * dp - 1
    sems = [dma((32,)), dma((12,)), dma((12,)), dma((12, dp - 1)), dma((12, dp - 1)), dma((16,)), dma((16,)),
            dma((1, 4)), dma((1, 4)), dma((1, 2)), dma((1, 2)), dma((2,)), dma((2,)), dma((3,)), dma((3,)), dma((3,)), dma((3,)),
            dma((many,)), dma((many,))]
    return pl.pallas_call(
        functools.partial(back_kernel, dp),
        out_shape=[jax.ShapeDtypeStruct(*item) for item in outs],
        in_specs=[ANY] * 21 + [VM] * 10,
        out_specs=[VM] * len(outs),
        scratch_shapes=[pltpu.VMEM(*item) for item in scratch] + sems,
        name="back",
        compiler_params=pltpu.CompilerParams(
            collective_id=3, has_side_effects=True, vmem_limit_bytes=GRANT),
    )(*operands)


def emit_kernel(n, *refs):
    layer, image, text, norms, up, down = refs[:6]
    outs = refs[n:]
    outs[0][...] = layer[...]
    outs[1][...] = image[...]
    outs[2][...] = text[...].astype(F32)
    for i in range(6):
        outs[3 + i][...] = norms[i]
    rows, columns = up.shape[2], down.shape[2]
    for c in range(4):
        for h in range(2):
            outs[9][h * rows : (h + 1) * rows, c * 256 : c * 256 + 256] = up[c, h].astype(F32)
            at = h * 512 + c * columns
            outs[10][at : at + columns, :] = down[c, h].astype(F32)
    for given, out in zip(refs[6 : n - 3], outs[11:]):
        rows = given.shape[1]
        for h in range(2):
            out[h * rows : (h + 1) * rows] = given[h].astype(F32)
    for given, out in zip(refs[n - 3 : n], outs[-3:]):
        rows = given.shape[2]
        for s in range(2):
            for h in range(2):
                out[h * rows : (h + 1) * rows, s * 128 : s * 128 + 128] = given[s, h].astype(F32)


def emit(arrays):
    part = arrays[3].shape[1]
    shapes = [(part,)] * 6 + [(part, 1024), (1024, part)]
    outs = [jax.ShapeDtypeStruct((256, 1024), BF16), jax.ShapeDtypeStruct((256, 1024), F32), jax.ShapeDtypeStruct((128, 1024), F32)]
    outs += [jax.ShapeDtypeStruct(item, F32) for item in shapes]
    outs += [jax.ShapeDtypeStruct((2 * item.shape[1], item.shape[2]), F32) for item in arrays[6:-3]]
    outs += [jax.ShapeDtypeStruct((part, 256), F32)] * 3
    return pl.pallas_call(
        functools.partial(emit_kernel, len(arrays)),
        out_shape=outs,
        in_specs=[VM] * len(arrays),
        out_specs=[VM] * len(outs),
        name="emit",
        compiler_params=pltpu.CompilerParams(vmem_limit_bytes=GRANT),
    )(*arrays)


def local(
    dp,
    image_rows,
    text_states,
    caption_lengths,
    out_grad,
    self_query,
    self_key,
    self_value,
    self_output,
    cross_query,
    cross_key,
    cross_value,
    cross_output,
    mlp_up,
    mlp_down,
    attn_gain,
    attn_shift,
    cross_gain,
    cross_shift,
    mlp_gain,
    mlp_shift,
):
    text = text_states[0]
    bias = jnp.where(jnp.arange(TEXT)[None, :] < caption_lengths[0], 0.0, MASKED)
    x_full, norm_one, q, k, v, self_mix, p0, p1, p2, p3, other_text, cross_k, cross_v = front(
        image_rows, self_query, self_key, self_value, text, cross_key, cross_value,
        [attn_gain[None, :], attn_shift[None, :]])
    gains = [item[None, :] for item in (cross_gain, cross_shift, mlp_gain, mlp_shift)]
    (mix_grad, self_back, layer_part, up_sum, down_sum, c_query, c_output, k_grad, v_grad, k_over, v_over, parts, resid,
     after_cross) = middle(
        dp, x_full, self_mix, out_grad, self_output, cross_query, cross_output, mlp_up, mlp_down,
        cross_k, cross_v, bias, gains)
    arrays = back(
        dp, self_mix, self_back, layer_part, mix_grad, q, k, v, p0, p1, p2, p3, norm_one,
        self_query, self_key, self_value, image_rows, resid, after_cross, c_query, c_output,
        up_sum, text, other_text, cross_key, cross_value, k_grad, v_grad, k_over, v_over, parts, attn_gain[None, :])
    layer_out, image_grad, text_grad, *rest = emit([*arrays[:5], down_sum, *arrays[5:]])
    norms, (up, down, cq, co, so, ck, cv, sq, sk, sv) = rest[:6], rest[6:]
    return (layer_out, image_grad, text_grad[None], sq, sk, sv, so, cq, ck, cv, co, up, down, *norms)


def solution(mesh):
    placed = (
        P(("grp", "dp", "tp"), None),
        P(("grp", "dp"), None, None),
        P(("grp", "dp")),
        P(("grp", "dp"), None),
        P(None, "tp"),
        P(None, "tp"),
        P(None, "tp"),
        P("tp", None),
        P(None, "tp"),
        P(None, "tp"),
        P(None, "tp"),
        P("tp", None),
        P(None, "tp"),
        P("tp", None),
        P(),
        P(),
        P(),
        P(),
        P(),
        P(),
    )
    return jax.shard_map(
        functools.partial(local, mesh.shape["dp"]),
        mesh=mesh,
        in_specs=placed,
        out_specs=(
            P(("grp", "dp", "tp"), None),
            P(("grp", "dp", "tp"), None),
            P(("grp", "dp"), None, None),
            P("dp", "tp"),
            P("dp", "tp"),
            P("dp", "tp"),
            P("tp", "dp"),
            P("dp", "tp"),
            P("dp", "tp"),
            P("dp", "tp"),
            P("tp", "dp"),
            P("dp", "tp"),
            P("tp", "dp"),
            P("dp"),
            P("dp"),
            P("dp"),
            P("dp"),
            P("dp"),
            P("dp"),
        ),
        check_vma=False,
    )
```
